32 devices in a mesh: shard: 4 (over z), replica: 8 (over y, x, core).
Axes of the slice: x: 2, y: 2, z: 4, core: 2. Of those that a mesh axis runs over, the one named last changes fastest.
Arguments:
- tokens: bfloat16 [32, 1024, 768], P(('shard', 'replica')), may hold values from -6 to 6
- cotangent: bfloat16 [32, 1024, 768], P(('shard', 'replica')), may hold values from -6 to 6
- piece_starts: int32 [32, 3], P(('shard', 'replica')), may hold values from 0 to 1024, as said below
- labels: int32 [32], P(('shard', 'replica')), may hold values from 0 to 13
- qkv_weight: bfloat16 [768, 2304], P('shard'), may hold values from -0.21875 to 0.21875
- query_bias: bfloat16 [768], P('shard'), may hold values from -3 to 3
- value_bias: bfloat16 [768], P('shard'), may hold values from -3 to 3
- out_weight: bfloat16 [768, 768], P('shard'), may hold values from -3.5 to 3.5
- out_bias: bfloat16 [768], P('shard'), may hold values from -3 to 3
- attention_gain: bfloat16 [768], P('shard'), may hold values from 0.5 to 1.5
- attention_shift: bfloat16 [768], P('shard'), may hold values from -2 to 2
- up_weight: bfloat16 [768, 3072], P('shard'), may hold values from -0.21875 to 0.21875
- up_bias: bfloat16 [3072], P('shard'), may hold values from -3 to 3
- down_weight: bfloat16 [3072, 768], P('shard'), may hold values from -0.109375 to 0.109375
- down_bias: bfloat16 [768], P('shard'), may hold values from -3 to 3
- feed_gain: bfloat16 [768], P('shard'), may hold values from 0.5 to 1.5
- feed_shift: bfloat16 [768], P('shard'), may hold values from -2 to 2
- student_weight: bfloat16 [768, 128], P('shard'), may hold values from -0.21875 to 0.21875
- student_bias: bfloat16 [128], P('shard'), may hold values from -3 to 3
- pool_weight: bfloat16 [128, 384], P('shard'), may hold values from -0.5 to 0.5
- dense_weight: bfloat16 [128, 128], P('shard'), may hold values from -6 to 6
- dense_bias: bfloat16 [128], P('shard'), may hold values from -2 to 2
- class_weight: bfloat16 [128, 14], P('shard'), may hold values from -0.5 to 0.5
- class_bias: bfloat16 [14], replicated, may hold values from -3 to 3
Outputs:
- hidden: bfloat16 [32, 1024, 768], P(('shard', 'replica'))
- logits: float32 [32, 14], P(('shard', 'replica'))
- input_grad: float32 [32, 1024, 768], P(('shard', 'replica'))
- grad_qkv_weight: float32 [768, 2304], P('shard')
- grad_query_bias: float32 [768], P('shard')
- grad_value_bias: float32 [768], P('shard')
- grad_out_weight: float32 [768, 768], P('shard')
- grad_out_bias: float32 [768], P('shard')
- grad_attention_gain: float32 [768], P('shard')
- grad_attention_shift: float32 [768], P('shard')
- grad_up_weight: float32 [768, 3072], P('shard')
- grad_up_bias: float32 [3072], P('shard')
- grad_down_weight: float32 [3072, 768], P('shard')
- grad_down_bias: float32 [768], P('shard')
- grad_feed_gain: float32 [768], P('shard')
- grad_feed_shift: float32 [768], P('shard')
- grad_student_weight: float32 [768, 128], P('shard')
- grad_student_bias: float32 [128], P('shard')
- grad_pool_weight: float32 [128, 384], P('shard')
- grad_dense_weight: float32 [128, 128], P('shard')
- grad_dense_bias: float32 [128], P('shard')
- grad_class_weight: float32 [128, 14], P('shard')
- grad_class_bias: float32 [14], replicated
The draws below stay inside these ranges and needn't reach their ends.
Inputs may be any that keep to these rules, and one draw needn't show every extreme that they name: `piece_starts`: each entry is the first position of a picture piece of 256 tokens inside its sequence, or 1024 for an unused slot; pieces may intersect.
All inputs are finite; a program needn't handle non-finite values.
Results may differ from the reference program's by a relative error of at most 0.019.
Values may be sent and summed in bfloat16 or wider, within the bound.
No kernel may reach another device: no remote copies, remote signals or barrier semaphores. Data moves between devices by JAX's collectives and lax.ppermute only.
A program may use at most 256 MiB of HBM per device.

```python
import jax
import jax.numpy as jnp
from jax import lax

D = 768
HEADS = 12
FF = 3072
STUDENT = 128
POOL_HEADS = 2
CLASSES = 14
SEQ_LEN = 1024
PIECE = 256
PIECES = 3
SEQS = 32


def draw_piece_starts(key, part):
    count_key = jax.random.fold_in(key, 11)
    place_key = jax.random.fold_in(key, 12)
    counts = jax.random.randint(count_key, (SEQS, 1), 0, PIECES + 1)
    places = jax.random.randint(place_key, (SEQS, PIECES), 0, SEQ_LEN - PIECE + 1)
    slots = jnp.arange(PIECES)[None, :]
    starts = jnp.where(slots < counts, places, SEQ_LEN)
    starts = starts.at[0, 0].set(0).at[0, PIECES - 1].set(SEQ_LEN)
    return starts.astype(jnp.int32)


def touch_ends(array, key, least, top_value):
    shape = array.shape
    spot = [jax.random.randint(jax.random.fold_in(key, axis), (), 0, shape[axis]) for axis in range(len(shape))]
    array = array.at[tuple(spot)].set(least)
    longest = shape.index(max(shape))
    spot[longest] = (spot[longest] + 1) % shape[longest]
    return array.at[tuple(spot)].set(top_value)


def steps_of(rng, shape, split, least, top_value):
    level, own = 1.0, jax.random.fold_in(rng, 6)
    for axis_at, parts in split:
        steps = jnp.exp(jax.random.uniform(jax.random.fold_in(own, axis_at), (parts,), jnp.float32, least / len(split), top_value / len(split)))
        level = level * jnp.repeat(steps, shape[axis_at] // parts).reshape([-1 if axis == axis_at else 1 for axis in range(len(shape))])
    return level


def noise(stream_key, dims, scale, most, split=(), held_as=jnp.bfloat16):
    array = jax.random.normal(stream_key, dims, jnp.float32) * scale
    if len(split) > 0:
        array = steps_of(stream_key, dims, split, -0.22, 0.18) * array
    return jnp.clip(array, min=-most, max=most).astype(held_as)


def setup_inputs(seed: int = 0) -> dict:
    streams_of = jax.random.split(jax.random.key(seed), 25)
    return {
        "tokens": noise(streams_of[0], (SEQS, SEQ_LEN, D), 1.0, 6.0, ((0, 32),)),
        "cotangent": noise(streams_of[1], (SEQS, SEQ_LEN, D), 1.0, 6.0, ((0, 32),)),
        "piece_starts": draw_piece_starts(jax.random.fold_in(streams_of[24], 71), 0),
        "labels": touch_ends(jax.random.randint(streams_of[3], (SEQS,), 0, CLASSES), jax.random.fold_in(streams_of[3], 1), 0, CLASSES - 1).astype(jnp.int32),
        "qkv_weight": noise(streams_of[4], (D, 3 * D), D ** -0.5, 0.21875, ((0, 4),)),
        "query_bias": noise(streams_of[5], (D,), 0.5, 3.0, ((0, 4),)),
        "value_bias": noise(streams_of[6], (D,), 0.5, 3.0, ((0, 4),)),
        "out_weight": noise(streams_of[7], (D, D), (max(1, D // 256)) ** -0.5, 3.5, ((0, 4),)),
        "out_bias": noise(streams_of[8], (D,), 0.5, 3.0, ((0, 4),)),
        "attention_gain": jnp.clip(1.0 + 0.1 * jax.random.normal(streams_of[9], (D,), jnp.float32), 0.5, 1.5).astype(jnp.bfloat16),
        "attention_shift": noise(streams_of[10], (D,), 0.3, 2.0, ((0, 4),)),
        "up_weight": noise(streams_of[11], (D, FF), D ** -0.5, 0.21875, ((0, 4),)),
        "up_bias": noise(streams_of[12], (FF,), 0.5, 3.0, ((0, 4),)),
        "down_weight": noise(streams_of[13], (FF, D), FF ** -0.5, 0.109375, ((0, 4),)),
        "down_bias": noise(streams_of[14], (D,), 0.5, 3.0, ((0, 4),)),
        "feed_gain": jnp.clip(1.0 + 0.1 * jax.random.normal(streams_of[15], (D,), jnp.float32), 0.5, 1.5).astype(jnp.bfloat16),
        "feed_shift": noise(streams_of[16], (D,), 0.3, 2.0, ((0, 4),)),
        "student_weight": noise(streams_of[17], (D, STUDENT), D ** -0.5, 0.21875, ((0, 4),)),
        "student_bias": noise(streams_of[18], (STUDENT,), 0.5, 3.0, ((0, 4),)),
        "pool_weight": noise(streams_of[19], (STUDENT, 3 * STUDENT), STUDENT ** -0.5, 0.5, ((0, 4),)),
        "dense_weight": noise(streams_of[20], (STUDENT, STUDENT), (max(1, 4 * STUDENT // SEQ_LEN)) ** -0.5, 6.0, ((0, 4),)),
        "dense_bias": noise(streams_of[21], (STUDENT,), 0.3, 2.0, ((0, 4),)),
        "class_weight": noise(streams_of[22], (STUDENT, CLASSES), STUDENT ** -0.5, 0.5, ((0, 4),)),
        "class_bias": noise(streams_of[23], (CLASSES,), 0.5, 3.0),
    }


PRECISE = lax.Precision.HIGHEST
NORM_EPS = 1e-06
MASKED_SCORE = -1e+30

@jax.custom_vjp
def low(v):
    return lax.optimization_barrier(v.astype(jnp.bfloat16)).astype(jnp.float32)

@jax.custom_vjp
def low_back(v):
    return v

def low_keep(v):
    return (low(v), None)

def low_pass(kept, grad):
    return (grad,)

def back_keep(v):
    return (v, None)

def back_low(kept, grad):
    return (low(grad),)
low.defvjp(low_keep, low_pass)
low_back.defvjp(back_keep, back_low)

def matmul_high(left, right):
    return jnp.dot(left, right, precision=PRECISE, preferred_element_type=jnp.float32)

def layer_norm(values, gain, shift):
    middle = lax.optimization_barrier(jnp.mean(values, axis=-1, keepdims=True))
    centered = values - middle
    spread = lax.optimization_barrier(jnp.mean(centered * centered, axis=-1, keepdims=True))
    return centered * lax.rsqrt(spread + NORM_EPS) * gain + shift

def allowed_mask(starts, row_place, col_place, piece):
    row_inside = (starts[:, None] <= row_place[None, :]) & (row_place[None, :] < starts[:, None] + piece)
    col_inside = (starts[:, None] <= col_place[None, :]) & (col_place[None, :] < starts[:, None] + piece)
    shared = jnp.any(row_inside[:, :, None] & col_inside[:, None, :], axis=0)
    return shared | (col_place[None, :] <= row_place[:, None])

def forward(sequence, params, starts, label):
    qkv_weight, query_bias, value_bias, out_weight, out_bias, attention_gain, attention_shift, up_weight, up_bias, down_weight, down_bias, feed_gain, feed_shift, student_weight, student_bias, pool_weight, dense_weight, dense_bias, class_weight, class_bias = params
    length = sequence.shape[0]
    head_dim = D // HEADS
    qkv_bias = jnp.concatenate([query_bias, jnp.zeros_like(query_bias), value_bias])
    joined = low(low_back(matmul_high(sequence, qkv_weight) + qkv_bias)).reshape(length, 3, HEADS, head_dim)
    query = joined[:, 0]
    key_rows = joined[:, 1]
    value_rows = joined[:, 2]
    scores = jnp.einsum('qhd,khd->hqk', query, key_rows, precision=PRECISE) * head_dim ** (-0.5)
    scores = low_back(scores)
    places = jnp.arange(length)
    allowed = allowed_mask(starts, places, places, PIECE)
    scores = jnp.where(allowed[None], scores, MASKED_SCORE)
    weights = jax.nn.softmax(scores, axis=-1)
    mixed = jnp.einsum('hqk,khd->qhd', low(weights), value_rows, precision=PRECISE).reshape(length, D)
    mixed = low(low_back(mixed))
    branch = low_back(matmul_high(mixed, out_weight)) + out_bias
    first = layer_norm(sequence + branch, attention_gain, attention_shift)
    inner = low_back(matmul_high(low(first), up_weight)) + up_bias
    active = low(jax.nn.gelu(inner, approximate=False))
    feed = low_back(matmul_high(active, down_weight)) + down_bias
    second = layer_norm(first + feed, feed_gain, feed_shift)
    student = low(low_back(matmul_high(low(second), student_weight)) + student_bias)
    pool_dim = STUDENT // POOL_HEADS
    pooling = low(low_back(matmul_high(student, pool_weight))).reshape(length, 3, POOL_HEADS, pool_dim)
    pool_query = pooling[0, 0]
    pool_scores = jnp.einsum('hd,jhd->hj', pool_query, pooling[:, 1], precision=PRECISE) * pool_dim ** (-0.5)
    pool_weights = jax.nn.softmax(pool_scores, axis=-1)
    pooled = jnp.einsum('hj,jhd->hd', pool_weights, pooling[:, 2], precision=PRECISE).reshape(STUDENT)
    summary = jnp.tanh(matmul_high(pooled, dense_weight) + dense_bias)
    logits = matmul_high(summary, class_weight) + class_bias
    picked = jnp.sum(jnp.where(jnp.arange(CLASSES) == label, logits, 0.0))
    loss = jax.nn.logsumexp(logits) - picked
    return (second, logits, loss)

def reference(tokens, cotangent, piece_starts, labels, qkv_weight, query_bias, value_bias, out_weight, out_bias, attention_gain, attention_shift, up_weight, up_bias, down_weight, down_bias, feed_gain, feed_shift, student_weight, student_bias, pool_weight, dense_weight, dense_bias, class_weight, class_bias):
    raw_params = (qkv_weight, query_bias, value_bias, out_weight, out_bias, attention_gain, attention_shift, up_weight, up_bias, down_weight, down_bias, feed_gain, feed_shift, student_weight, student_bias, pool_weight, dense_weight, dense_bias, class_weight, class_bias)
    params = tuple((weight_arg.astype(jnp.float32) for weight_arg in raw_params))
    zero_sums = tuple((jnp.zeros(weight_arg.shape, jnp.float32) for weight_arg in params))

    def one_sequence(totals, inputs):
        sequence, direction, starts, label = inputs

        def local_forward(seq_in, prm):
            return forward(seq_in, prm, starts, label)
        outputs, pullback = jax.vjp(local_forward, sequence, params)
        second, logits, loss = outputs
        grad_sequence, grad_params = pullback((direction, jnp.zeros_like(logits), jnp.ones_like(loss)))
        totals = tuple((total_term + grad_term for total_term, grad_term in zip(totals, grad_params)))
        return (totals, (second.astype(jnp.bfloat16), logits, grad_sequence))
    totals, outputs = lax.scan(one_sequence, zero_sums, (tokens.astype(jnp.float32), cotangent.astype(jnp.float32), piece_starts, labels))
    hidden, logits, input_grad = outputs
    return (hidden, logits, input_grad, totals[0], totals[1], totals[2], totals[3], totals[4], totals[5], totals[6], totals[7], totals[8], totals[9], totals[10], totals[11], totals[12], totals[13], totals[14], totals[15], totals[16], totals[17], totals[18], totals[19])
```

```python
from functools import partial

import jax
import jax.numpy as jnp
from jax import lax
from jax.experimental import pallas as pl
from jax.experimental.pallas import tpu as pltpu
from jax.sharding import PartitionSpec as P

HEADS = 12
POOL_HEADS = 2
PIECE = 256
NORM_EPS = 1e-06
MASKED_SCORE = -1e30
FLOAT = jnp.float32
HALF = jnp.bfloat16
PRECISE = lax.Precision.HIGHEST
LANES = 128
BLOCK = 256

ERF_SLOPE = 0.42
ERF_TERMS = (
    0.23691840576326206,
    0.2382680869907842,
    0.20182398814655725,
    0.2493386597508521,
    -0.10108083678814953,
    0.4156989047782712,
    -0.3092846516362072,
    0.06831743518928779,
)


def params_of(kinds, limit=60 << 20):
    return pltpu.CompilerParams(dimension_semantics=kinds, vmem_limit_bytes=limit)


def whole(shape, space=None):
    return pl.BlockSpec(shape, lambda *_: (0,) * len(shape))


def mult(left, right):
    return jnp.dot(left, right, preferred_element_type=FLOAT)


def mult_rt(left, right):
    return lax.dot_general(left, right, (((1,), (1,)), ((), ())), preferred_element_type=FLOAT)


def mult_lt(left, right):
    return lax.dot_general(left, right, (((0,), (0,)), ((), ())), preferred_element_type=FLOAT)


def precise(left, right, dims):
    return lax.dot_general(
        left, right, ((dims[:1], dims[1:]), ((), ())), precision=PRECISE, preferred_element_type=FLOAT
    )


def key_extent(block, length):
    return min(length, (block + 2) * BLOCK)


def allowed_block(starts_ref, first_row, first_col, shape, row_axis):
    rows = first_row + lax.broadcasted_iota(jnp.int32, shape, row_axis)
    cols = first_col + lax.broadcasted_iota(jnp.int32, shape, 1 - row_axis)
    allowed = cols <= rows
    for piece in range(starts_ref.shape[1]):
        start = starts_ref[0, piece]
        inside = (rows >= start) & (rows < start + PIECE) & (cols >= start) & (cols < start + PIECE)
        allowed = allowed | inside
    return allowed


def fill_bias(starts_ref, bias_ref, length, row_axis):
    for block in range(length // BLOCK):
        wide = key_extent(block, length) - block * BLOCK
        shape = (BLOCK, wide) if row_axis == 0 else (wide, BLOCK)
        allowed = allowed_block(starts_ref, block * BLOCK, block * BLOCK, shape, row_axis)
        bias = jnp.where(allowed, 0.0, MASKED_SCORE).astype(FLOAT)
        if row_axis == 0:
            bias_ref[block, :, 0:wide] = bias
        else:
            bias_ref[block, 0:wide, :] = bias


def half_lanes(value, half):
    lane = lax.broadcasted_iota(jnp.int32, value.shape, 1)
    keep = (lane < LANES // 2) if half == 0 else (lane >= LANES // 2)
    return jnp.where(keep, value, jnp.zeros_like(value))


def attend_forward_kernel(starts_ref, q_ref, k_ref, v_ref, mixed_ref, lse_ref, bias_ref):
    length = q_ref.shape[0]
    scale = (LANES // 2) ** (-0.5)

    @pl.when(pl.program_id(0) == 0)
    def _():
        fill_bias(starts_ref, bias_ref, length, 0)

    values = [half_lanes(v_ref[...], half) for half in range(2)]
    lane = lax.broadcasted_iota(jnp.int32, (BLOCK, LANES), 1)
    for block in range(length // BLOCK):
        begin = block * BLOCK
        extent = key_extent(block, length)
        query = q_ref[begin : begin + BLOCK, :] * jnp.asarray(scale, HALF)
        outs = []
        logs = []
        for half in range(2):
            scores = mult_rt(half_lanes(query, half), k_ref[0:extent, :])
            edge = scores[:, begin:extent] + bias_ref[block, :, 0 : extent - begin]
            parts = [edge] if begin == 0 else [scores[:, 0:begin], edge]
            ceiling = parts[0].max(axis=1, keepdims=True)
            for part in parts[1:]:
                ceiling = jnp.maximum(ceiling, part.max(axis=1, keepdims=True))
            total = 0.0
            mixed = 0.0
            place = 0
            for part in parts:
                raised = jnp.exp(part - ceiling)
                total = total + raised.sum(axis=1, keepdims=True)
                mixed = mixed + mult(
                    raised.astype(HALF), values[half][place : place + part.shape[1], :]
                )
                place += part.shape[1]
            outs.append(mixed / total)
            logs.append(ceiling + jnp.log(total))
        mixed_ref[begin : begin + BLOCK, :] = (outs[0] + outs[1]).astype(HALF)
        both = jnp.where(lane == 0, logs[0], logs[1])
        lse_ref[:, begin : begin + BLOCK] = both.T[0:8, :]


def attend_forward(joined, starts):
    length, wide = joined.shape
    pairs = wide // 3 // LANES
    return pl.pallas_call(
        attend_forward_kernel,
        grid=(pairs,),
        in_specs=[
            pl.BlockSpec(memory_space=pltpu.SMEM),
            pl.BlockSpec((length, LANES), lambda h: (0, h)),
            pl.BlockSpec((length, LANES), lambda h: (0, pairs + h)),
            pl.BlockSpec((length, LANES), lambda h: (0, 2 * pairs + h)),
        ],
        out_specs=[
            pl.BlockSpec((length, LANES), lambda h: (0, h)),
            pl.BlockSpec((8, length), lambda h: (h, 0)),
        ],
        out_shape=[
            jax.ShapeDtypeStruct((length, wide // 3), HALF),
            jax.ShapeDtypeStruct((pairs * 8, length), FLOAT),
        ],
        scratch_shapes=[pltpu.VMEM((length // BLOCK, BLOCK, 2 * BLOCK), FLOAT)],
        compiler_params=params_of(("arbitrary",)),
        cost_estimate=pl.CostEstimate(
            flops=4 * length * length * wide // 3, transcendentals=length * length * wide // 192, bytes_accessed=8 * length * wide
        ),
        name="attend_forward",
    )(starts, joined, joined, joined)


def attend_backward_kernel(
    starts_ref, q_ref, k_ref, v_ref, mixed_ref, grad_ref, lse_ref, out_ref, sums_ref, bias_ref, dk_ref, dv_ref
):
    length = q_ref.shape[0]
    scale = (LANES // 2) ** (-0.5)

    @pl.when(pl.program_id(0) == 0)
    def _():
        fill_bias(starts_ref, bias_ref, length, 1)

    product = grad_ref[...].astype(FLOAT) * mixed_ref[...].astype(FLOAT)
    row = lax.broadcasted_iota(jnp.int32, (8, LANES), 0)
    col = lax.broadcasted_iota(jnp.int32, (8, LANES), 1)
    picks = jnp.where((col < LANES // 2) == (row == 0), 1.0, 0.0).astype(FLOAT)
    inner = precise(picks, product, (1, 1))
    keys = [half_lanes(k_ref[...] * jnp.asarray(scale, HALF), half) for half in range(2)]
    values = [half_lanes(v_ref[...], half) for half in range(2)]
    dk_ref[...] = jnp.zeros_like(dk_ref)
    dv_ref[...] = jnp.zeros_like(dv_ref)
    query_sum = jnp.zeros((1, LANES), FLOAT)
    for block in range(length // BLOCK):
        begin = block * BLOCK
        extent = key_extent(block, length)
        query = q_ref[begin : begin + BLOCK, :]
        grad = grad_ref[begin : begin + BLOCK, :]
        grad_query = 0.0
        for half in range(2):
            scores = mult_rt(keys[half][0:extent, :], query)
            grad_probs = mult_rt(values[half][0:extent, :], grad)
            lse = lse_ref[half : half + 1, begin : begin + BLOCK]
            base = inner[half : half + 1, begin : begin + BLOCK]
            edge = scores[begin:extent, :] + bias_ref[block, 0 : extent - begin, :]
            shifted = edge if begin == 0 else jnp.concatenate([scores[0:begin, :], edge], axis=0)
            probs = jnp.exp(shifted - lse)
            grad_scores = (probs * (grad_probs - base)).astype(HALF)
            grad_half = half_lanes(grad, half)
            query_half = half_lanes(query * jnp.asarray(scale, HALF), half)
            dv_ref[0:extent, :] += mult(probs.astype(HALF), grad_half)
            dk_ref[0:extent, :] += mult(grad_scores, query_half)
            grad_query = grad_query + mult_lt(grad_scores, keys[half][0:extent, :])
        rounded = grad_query.astype(HALF)
        out_ref[0, begin : begin + BLOCK, :] = rounded
        query_sum = query_sum + rounded.astype(FLOAT).sum(axis=0, keepdims=True)
    out_ref[1, :, :] = dk_ref[...].astype(HALF)
    value = dv_ref[...].astype(HALF)
    out_ref[2, :, :] = value
    value_sum = value.astype(FLOAT).sum(axis=0, keepdims=True)
    sums_ref[...] = jnp.where(row == 0, query_sum, value_sum)


def attend_backward(joined, starts, mixed, grad_mixed, lse):
    length, wide = joined.shape
    pairs = wide // 3 // LANES
    return pl.pallas_call(
        attend_backward_kernel,
        grid=(pairs,),
        in_specs=[
            pl.BlockSpec(memory_space=pltpu.SMEM),
            pl.BlockSpec((length, LANES), lambda h: (0, h)),
            pl.BlockSpec((length, LANES), lambda h: (0, pairs + h)),
            pl.BlockSpec((length, LANES), lambda h: (0, 2 * pairs + h)),
            pl.BlockSpec((length, LANES), lambda h: (0, h)),
            pl.BlockSpec((length, LANES), lambda h: (0, h)),
            pl.BlockSpec((8, length), lambda h: (h, 0)),
        ],
        out_specs=[
            pl.BlockSpec((3, length, LANES), lambda h: (0, 0, h)),
            pl.BlockSpec((8, LANES), lambda h: (0, h)),
        ],
        out_shape=[
            jax.ShapeDtypeStruct((3, length, wide // 3), HALF),
            jax.ShapeDtypeStruct((8, wide // 3), FLOAT),
        ],
        scratch_shapes=[
            pltpu.VMEM((length // BLOCK, 2 * BLOCK, BLOCK), FLOAT),
            pltpu.VMEM((length, LANES), FLOAT),
            pltpu.VMEM((length, LANES), FLOAT),
        ],
        compiler_params=params_of(("arbitrary",)),
        cost_estimate=pl.CostEstimate(
            flops=10 * length * length * wide // 3, transcendentals=length * length * wide // 192, bytes_accessed=12 * length * wide
        ),
        name="attend_backward",
    )(starts, joined, joined, joined, mixed, grad_mixed, lse)


def normalise(values):
    middle = values.mean(axis=1, keepdims=True)
    centered = values - middle
    spread = (centered * centered).mean(axis=1, keepdims=True)
    rate = lax.rsqrt(spread + NORM_EPS)
    return centered * rate, rate


def normalise_backward(grad_unit, unit, rate):
    along = grad_unit.mean(axis=1, keepdims=True)
    across = (grad_unit * unit).mean(axis=1, keepdims=True)
    return rate * (grad_unit - along - unit * across)


def gelu_pair(inner):
    size = jnp.abs(inner)
    ratio = 1.0 / (1.0 + (ERF_SLOPE * 2.0**-0.5) * size)
    tail = jnp.full_like(ratio, 0.5 * ERF_TERMS[-1])
    for term in ERF_TERMS[-2::-1]:
        tail = tail * ratio + 0.5 * term
    bell = jnp.exp(-0.5 * inner * inner)
    tail = tail * ratio * bell
    below = jnp.where(inner < 0.0, tail, 1.0 - tail)
    return inner * below, below + inner * (bell * (2.0 * jnp.pi) ** -0.5)


QUERY_B, VALUE_B, OUT_B, GAIN1, SHIFT1, DOWN_B, GAIN2, SHIFT2 = range(8)


def project_kernel(tokens_ref, weight_ref, table_ref, out_ref):
    wide = tokens_ref.shape[1]
    for part in range(3):
        value = mult(tokens_ref[...], weight_ref[:, part * wide : (part + 1) * wide])
        if part == 0:
            value = value + table_ref[QUERY_B : QUERY_B + 1, :]
        elif part == 2:
            value = value + table_ref[VALUE_B : VALUE_B + 1, :]
        out_ref[:, part * wide : (part + 1) * wide] = value.astype(HALF)


def project(tokens, weight, table):
    length, wide = tokens.shape
    return pl.pallas_call(
        project_kernel,
        grid=(length // BLOCK,),
        in_specs=[pl.BlockSpec((BLOCK, wide), lambda i: (i, 0)), whole(weight.shape), whole(table.shape)],
        out_specs=pl.BlockSpec((BLOCK, 3 * wide), lambda i: (i, 0)),
        out_shape=jax.ShapeDtypeStruct((length, 3 * wide), HALF),
        compiler_params=params_of(("arbitrary",)),
        cost_estimate=pl.CostEstimate(flops=6 * length * wide * wide, transcendentals=0, bytes_accessed=8 * length * wide + 6 * wide * wide),
        name="project",
    )(tokens, weight, table)


def feed_kernel(
    mixed_ref, tokens_ref, out_w_ref, up_ref, down_ref, student_w_ref, pool_w_ref, table_ref, up_b_ref, student_b_ref,
    hidden_ref, first_ref, active_ref, slope_ref, unit1_ref, rate1_ref, unit2_ref, rate2_ref, student_ref, pool_ref,
):
    wide = tokens_ref.shape[1]
    line = lambda which: table_ref[which : which + 1, :]
    residual = tokens_ref[...].astype(FLOAT) + (mult(mixed_ref[...], out_w_ref[...]) + line(OUT_B))
    unit, rate = normalise(residual)
    unit1_ref[...] = unit.astype(HALF)
    rate1_ref[...] = jnp.broadcast_to(rate, rate1_ref.shape)
    first = unit * line(GAIN1) + line(SHIFT1)
    first_half = first.astype(HALF)
    first_ref[...] = first_half
    total = first + line(DOWN_B)
    for part in range(up_ref.shape[1] // wide):
        cols = slice(part * wide, (part + 1) * wide)
        inner = mult(first_half, up_ref[:, cols]) + up_b_ref[0:1, cols]
        active, slope = gelu_pair(inner)
        active = active.astype(HALF)
        active_ref[:, cols] = active
        slope_ref[:, cols] = slope.astype(HALF)
        total = total + mult(active, down_ref[cols, :])
    unit, rate = normalise(total)
    unit2_ref[...] = unit.astype(HALF)
    rate2_ref[...] = jnp.broadcast_to(rate, rate2_ref.shape)
    hidden = (unit * line(GAIN2) + line(SHIFT2)).astype(HALF)
    hidden_ref[...] = hidden
    student = (mult(hidden, student_w_ref[...]) + student_b_ref[0:1, :]).astype(HALF)
    student_ref[...] = student
    pool_ref[...] = mult(student, pool_w_ref[...]).astype(HALF)


def feed(mixed, tokens, out_w, up, down, student_w, pool_w, table, up_b, student_b):
    length, wide = tokens.shape
    inner = up.shape[1]
    small = student_w.shape[1]
    rows = lambda cols: pl.BlockSpec((BLOCK, cols), lambda i: (i, 0))
    struct = lambda cols, kind: jax.ShapeDtypeStruct((length, cols), kind)
    weights = (out_w, up, down, student_w, pool_w, table, up_b, student_b)
    return pl.pallas_call(
        feed_kernel,
        grid=(length // BLOCK,),
        in_specs=[rows(wide), rows(wide)] + [whole(w.shape) for w in weights],
        out_specs=[
            rows(wide), rows(wide), rows(inner), rows(inner), rows(wide), rows(LANES), rows(wide), rows(LANES),
            rows(small), rows(3 * small),
        ],
        out_shape=[
            struct(wide, HALF), struct(wide, HALF), struct(inner, HALF), struct(inner, HALF), struct(wide, HALF),
            struct(LANES, FLOAT), struct(wide, HALF), struct(LANES, FLOAT), struct(small, HALF), struct(3 * small, HALF),
        ],
        compiler_params=params_of(("arbitrary",)),
        cost_estimate=pl.CostEstimate(
            flops=2 * length * wide * (wide + 2 * inner), transcendentals=length * inner, bytes_accessed=30 * length * wide
        ),
        name="feed",
    )(mixed, tokens, *weights)


def student_kernel(
    label_ref, cotangent_ref, pool_ref, student_ref, unit2_ref, rate2_ref, student_w_ref, pool_w_ref, dense_ref, class_ref,
    small_b_ref, table_ref,
    logits_ref, grad_pool_ref, grad_student_ref, residual_ref, residual_half_ref, dense_grad_ref, class_grad_ref,
    small_sums_ref, sums_ref,
):
    length, three = pool_ref.shape
    small = three // 3
    scale = (small // POOL_HEADS) ** (-0.5)
    head_of = lambda axis: lax.broadcasted_iota(jnp.int32, (small, small), axis) // (small // POOL_HEADS)
    same = jnp.where(head_of(0) == head_of(1), 1.0, 0.0).astype(FLOAT)
    top = lax.broadcasted_iota(jnp.int32, (8, small), 0) == 0
    query = pool_ref[0:8, 0:small].astype(FLOAT)[0:1, :]
    key = pool_ref[:, small : 2 * small].astype(FLOAT)
    value = pool_ref[:, 2 * small : 3 * small].astype(FLOAT)
    scores = precise(key * query, same, (1, 0)) * scale
    raised = jnp.exp(scores - scores.max(axis=0, keepdims=True))
    weights = raised / raised.sum(axis=0, keepdims=True)
    pooled = (weights * value).sum(axis=0, keepdims=True)
    spread = lambda vector: jnp.where(top, vector, 0.0)
    dense = dense_ref[...].astype(FLOAT)
    classes = class_ref[...].astype(FLOAT)
    before = precise(spread(pooled), dense, (1, 0)) + small_b_ref[1:2, :]
    summary = jnp.tanh(before[0:1, :])
    logits = (precise(spread(summary), classes, (1, 0)) + small_b_ref[2:3, :])[0:1, :]
    lane = lax.broadcasted_iota(jnp.int32, (1, small), 1)
    real = small_b_ref[3:4, :] > 0.5
    masked = jnp.where(real, logits, MASKED_SCORE)
    lifted = jnp.where(real, jnp.exp(masked - masked.max(axis=1, keepdims=True)), 0.0)
    grad_logits = lifted / lifted.sum(axis=1, keepdims=True) - jnp.where(lane == label_ref[0], 1.0, 0.0)
    logits_ref[...] = jnp.broadcast_to(logits, logits_ref.shape)
    class_grad_ref[...] = precise(spread(summary), spread(grad_logits), (0, 0))
    grad_summary = precise(spread(grad_logits), classes, (1, 1))[0:1, :]
    grad_before = grad_summary * (1.0 - summary * summary)
    dense_grad_ref[...] = precise(spread(pooled), spread(grad_before), (0, 0))
    grad_pooled = precise(spread(grad_before), dense, (1, 1))[0:1, :]
    grad_weights = precise(value * grad_pooled, same, (1, 0))
    inner = (weights * grad_weights).sum(axis=0, keepdims=True)
    grad_scores = weights * (grad_weights - inner)
    grad_query = (grad_scores * key).sum(axis=0, keepdims=True) * scale
    first = lax.broadcasted_iota(jnp.int32, (length, small), 0) == 0
    grad_pool_ref[:, 0:small] = jnp.where(first, grad_query, 0.0).astype(HALF)
    grad_pool_ref[:, small : 2 * small] = (grad_scores * query * scale).astype(HALF)
    grad_pool_ref[:, 2 * small : 3 * small] = (weights * grad_pooled).astype(HALF)
    grad_student = mult_rt(grad_pool_ref[...], pool_w_ref[...])
    which = lax.broadcasted_iota(jnp.int32, (8, small), 0)
    student_sum = grad_student.sum(axis=0, keepdims=True)
    small_sums_ref[...] = jnp.where(
        which == 0, student_sum, jnp.where(which == 1, grad_before, jnp.where(which == 2, grad_logits, 0.0))
    )
    grad_student_ref[...] = grad_student.astype(HALF)

    sums_ref[...] = jnp.zeros_like(sums_ref)

    def one_block(block, _):
        rows = pl.ds(pl.multiple_of(block * BLOCK, BLOCK), BLOCK)
        grad = cotangent_ref[rows, :].astype(FLOAT) + mult_rt(grad_student_ref[rows, :], student_w_ref[...])
        unit = unit2_ref[rows, :].astype(FLOAT)
        residual = normalise_backward(grad * table_ref[GAIN2 : GAIN2 + 1, :], unit, rate2_ref[rows, 0:1])
        residual_ref[rows, :] = residual
        residual_half_ref[rows, :] = residual.astype(HALF)
        sums_ref[0:1, :] += (grad * unit).sum(axis=0, keepdims=True)
        sums_ref[1:2, :] += grad.sum(axis=0, keepdims=True)
        sums_ref[2:3, :] += residual.sum(axis=0, keepdims=True)
        return 0

    lax.fori_loop(0, length // BLOCK, one_block, 0)


def student_pass(label, cotangent, pool, student, unit2, rate2, student_w, pool_w, dense, classes, small_b, table):
    length, wide = cotangent.shape
    small = student.shape[1]
    struct = jax.ShapeDtypeStruct
    args = (cotangent, pool, student, unit2, rate2, student_w, pool_w, dense, classes, small_b, table)
    return pl.pallas_call(
        student_kernel,
        in_specs=[pl.BlockSpec(memory_space=pltpu.SMEM)] + [pl.BlockSpec(memory_space=pltpu.VMEM)] * len(args),
        out_specs=[pl.BlockSpec(memory_space=pltpu.VMEM)] * 9,
        out_shape=[
            struct((8, small), FLOAT), struct((length, 3 * small), HALF), struct((length, small), HALF),
            struct((length, wide), FLOAT), struct((length, wide), HALF), struct((small, small), FLOAT),
            struct((small, small), FLOAT), struct((8, small), FLOAT), struct((8, wide), FLOAT),
        ],
        compiler_params=params_of(None),
        cost_estimate=pl.CostEstimate(flops=2 * length * wide * small, transcendentals=length * small, bytes_accessed=16 * length * wide),
        name="student",
    )(label, *args)


def back_kernel(
    half_ref, residual_ref, slope_ref, unit1_ref, rate1_ref, down_ref, up_ref, out_w_ref, table_ref,
    inner_ref, residual1_ref, one_ref, mixed_ref, sums_ref, up_sums_ref,
):
    wide = residual_ref.shape[1]

    @pl.when(pl.program_id(0) == 0)
    def _():
        sums_ref[...] = jnp.zeros_like(sums_ref)
        up_sums_ref[...] = jnp.zeros_like(up_sums_ref)

    total = residual_ref[...]
    for part in range(up_ref.shape[1] // wide):
        cols = slice(part * wide, (part + 1) * wide)
        grad = mult_rt(half_ref[...], down_ref[cols, :]) * slope_ref[:, cols].astype(FLOAT)
        up_sums_ref[0:1, cols] += grad.sum(axis=0, keepdims=True)
        grad = grad.astype(HALF)
        inner_ref[:, cols] = grad
        total = total + mult_rt(grad, up_ref[:, cols])
    unit = unit1_ref[...].astype(FLOAT)
    residual = normalise_backward(total * table_ref[GAIN1 : GAIN1 + 1, :], unit, rate1_ref[:, 0:1])
    residual1_ref[...] = residual
    one = residual.astype(HALF)
    one_ref[...] = one
    mixed_ref[...] = mult_rt(one, out_w_ref[...]).astype(HALF)
    sums_ref[0:1, :] += (total * unit).sum(axis=0, keepdims=True)
    sums_ref[1:2, :] += total.sum(axis=0, keepdims=True)
    sums_ref[2:3, :] += residual.sum(axis=0, keepdims=True)


def back(half, residual, slope, unit1, rate1, down, up, out_w, table):
    length, wide = residual.shape
    inner = up.shape[1]
    rows = lambda cols: pl.BlockSpec((BLOCK, cols), lambda i: (i, 0))
    struct = jax.ShapeDtypeStruct
    weights = (down, up, out_w, table)
    return pl.pallas_call(
        back_kernel,
        grid=(length // BLOCK,),
        in_specs=[rows(wide), rows(wide), rows(inner), rows(wide), rows(LANES)] + [whole(w.shape) for w in weights],
        out_specs=[rows(inner), rows(wide), rows(wide), rows(wide), whole((8, wide)), whole((8, inner))],
        out_shape=[
            struct((length, inner), HALF), struct((length, wide), FLOAT), struct((length, wide), HALF),
            struct((length, wide), HALF), struct((8, wide), FLOAT), struct((8, inner), FLOAT),
        ],
        compiler_params=params_of(("arbitrary",)),
        cost_estimate=pl.CostEstimate(
            flops=2 * length * wide * (wide + 2 * inner), transcendentals=0, bytes_accessed=30 * length * wide
        ),
        name="back",
    )(half, residual, slope, unit1, rate1, *weights)


def input_kernel(joined_ref, residual_ref, weight_ref, out_ref):
    wide = residual_ref.shape[1]
    total = residual_ref[...]
    for part in range(3):
        total = total + mult_rt(joined_ref[part], weight_ref[:, part * wide : (part + 1) * wide])
    out_ref[...] = total


def input_pass(grad_joined, residual, weight):
    length, wide = residual.shape
    return pl.pallas_call(
        input_kernel,
        grid=(length // BLOCK,),
        in_specs=[
            pl.BlockSpec((3, BLOCK, wide), lambda i: (0, i, 0)),
            pl.BlockSpec((BLOCK, wide), lambda i: (i, 0)),
            whole(weight.shape),
        ],
        out_specs=pl.BlockSpec((BLOCK, wide), lambda i: (i, 0)),
        out_shape=jax.ShapeDtypeStruct((length, wide), FLOAT),
        compiler_params=params_of(("arbitrary",)),
        cost_estimate=pl.CostEstimate(flops=6 * length * wide * wide, transcendentals=0, bytes_accessed=14 * length * wide),
        name="input_pass",
    )(grad_joined, residual, weight)


def swap(value, axis, bits):
    size = lax.axis_size(axis)
    return lax.ppermute(value, axis, [(i, i ^ bits) for i in range(size)])


def around(value):
    return [value] + [swap(value, "replica", bits) for bits in (2, 4, 6)]


WIDE = 384
SMALL = (0, 128)
SMALL_ROWS = 16


def rows_of(mat):
    return SMALL_ROWS if mat == SMALL else mat[0] * mat[1] // 4


def all_rows(mats):
    return sum(rows_of(mat) for mat in mats)


def memory(kinds):
    return [pl.BlockSpec(memory_space=kind) for kind in kinds]


def vmem_call(kernel, name, where, inputs, outs, moved):
    return pl.pallas_call(
        kernel,
        in_specs=memory([pltpu.SMEM] + [pltpu.VMEM] * len(inputs)),
        out_specs=memory([pltpu.VMEM] * len(outs)),
        out_shape=outs,
        compiler_params=params_of(None),
        cost_estimate=pl.CostEstimate(flops=0, transcendentals=0, bytes_accessed=moved),
        name=name,
    )(where, *inputs)


def own_pieces(where, shards, mats):
    shard, chip, core = where[0], where[1], where[2]
    parts = []
    for value, mat in zip(shards, mats):
        if mat == SMALL:
            parts.append(lax.dynamic_slice_in_dim(value, (chip * 2 + core) * SMALL_ROWS, SMALL_ROWS, 0))
            continue
        rows = mat[1] // 4
        for chunk in range(mat[0]):
            parts.append(lax.dynamic_slice(value, (chip * rows, chunk * 2 * WIDE + core * WIDE), (rows, WIDE)))
    return jnp.concatenate(parts, axis=0) if len(parts) > 1 else parts[0]


def put_piece(out_ref, ref, step, offset, base, mat, chip, core):
    if mat == SMALL:
        begin = base + (chip * 2 + core) * SMALL_ROWS
        target = pl.ds(pl.multiple_of(begin, SMALL_ROWS), SMALL_ROWS)
        out_ref[target, :] = ref[step, offset : offset + SMALL_ROWS, :].astype(out_ref.dtype)
        return
    rows = mat[1] // 4
    target = pl.ds(pl.multiple_of(base + chip * rows, rows), rows)
    for chunk in range(mat[0]):
        lanes = pl.ds(pl.multiple_of(chunk * 2 * WIDE + core * WIDE, WIDE), WIDE)
        first = offset + chunk * rows
        out_ref[target, lanes] = ref[step, first : first + rows, :].astype(out_ref.dtype)


def place_kernel(place_ref, *refs, mats):
    shard, chip, core = place_ref[0], place_ref[1], place_ref[2]
    count = len(mats)
    pieces, owns, outs = refs[: -2 * count], refs[-2 * count : -count], refs[-count:]
    offset = 0
    for mat, own_ref, out_ref in zip(mats, owns, outs):
        height = mat[1]
        out_ref[pl.ds(pl.multiple_of(shard * height, height), height), :] = own_ref[...]
        for number, ref in enumerate(pieces):
            far, other = number // 2, number % 2
            for step in range(ref.shape[0]):
                base = (shard ^ (step + 1)) * height
                put_piece(out_ref, ref, step, offset, base, mat, chip ^ far, core ^ other)
        offset += rows_of(mat)


def gather_weights(where, shards, mats):
    piece = own_pieces(where, shards, mats)
    groups = lax.axis_size("shard")
    stack = jnp.stack([swap(piece, "shard", bits) for bits in range(1, groups)])
    pieces = []
    for value in around(stack):
        pieces += [value, swap(value, "replica", 1)]
    outs = [jax.ShapeDtypeStruct((groups * s.shape[0], s.shape[1]), s.dtype) for s in shards]
    moved = 4 * groups * sum(s.size for s in shards)
    return vmem_call(partial(place_kernel, mats=mats), "place", where, pieces + list(shards), outs, moved)


def weight_grad_kernel(place_ref, left_ref, right_ref, send_ref, keep_ref, *, stacked):
    core = place_ref[2]
    left = left_ref[...]
    for chunk in range(send_ref.shape[0]):
        base = 0 if stacked else chunk * 2 * WIDE
        for ref, which in ((send_ref, 1 - core), (keep_ref, core)):
            lanes = pl.ds(pl.multiple_of(base + which * WIDE, WIDE), WIDE)
            right = right_ref[chunk, :, lanes] if stacked else right_ref[:, lanes]
            ref[chunk] = mult_lt(left, right).astype(HALF)


def weight_grad(where, left, right, name):
    stacked = right.ndim == 3
    length, height = left.shape
    chunks = right.shape[0] if stacked else right.shape[1] // (2 * WIDE)
    block = 256
    out = jax.ShapeDtypeStruct((chunks, height, WIDE), HALF)
    return pl.pallas_call(
        partial(weight_grad_kernel, stacked=stacked),
        grid=(height // block,),
        in_specs=[
            pl.BlockSpec(memory_space=pltpu.SMEM),
            pl.BlockSpec((length, block), lambda i: (0, i)),
            whole(right.shape),
        ],
        out_specs=[pl.BlockSpec((chunks, block, WIDE), lambda i: (0, i, 0))] * 2,
        out_shape=[out, out],
        compiler_params=params_of(("arbitrary",)),
        cost_estimate=pl.CostEstimate(
            flops=4 * length * height * chunks * WIDE, transcendentals=0, bytes_accessed=2 * (left.size + right.size + 2 * chunks * height * WIDE)
        ),
        name=name,
    )(where, left, right)


def split_kernel(place_ref, *refs, mats):
    chip = place_ref[1]
    count = len(mats)
    keeps, recvs, outs = refs[:count], refs[count : 2 * count], refs[2 * count :]
    offset = 0
    for mat, keep_ref, recv_ref in zip(mats, keeps, recvs):
        chunks = keep_ref.shape[0]
        height = keep_ref.shape[1] // outs[0].shape[0]
        rows = height // 4
        for shard in range(outs[0].shape[0]):
            for far, out_ref in enumerate(outs):
                begin = pl.multiple_of(shard * height + (chip ^ far) * rows, rows)
                for chunk in range(chunks):
                    mine = keep_ref[chunk, pl.ds(begin, rows), :].astype(FLOAT)
                    other = recv_ref[chunk, pl.ds(begin, rows), :].astype(FLOAT)
                    first = offset + chunk * rows
                    out_ref[shard, first : first + rows, :] = (mine + other).astype(HALF)
        offset += chunks * rows


def merge_kernel(place_ref, a_ref, b_ref, c_ref, d_ref, *outs):
    shard = place_ref[0]
    for step, out_ref in enumerate(outs):
        row = shard ^ step
        near = a_ref[row].astype(FLOAT) + b_ref[row].astype(FLOAT)
        out_ref[...] = (near + (c_ref[row].astype(FLOAT) + d_ref[row].astype(FLOAT))).astype(HALF)


def finish_kernel(place_ref, mine_ref, other_ref, *outs, mats):
    chip, core = place_ref[1], place_ref[2]
    offset = 0
    for mat, out_ref in zip(mats, outs):
        for far in range(4):
            put_piece(out_ref, mine_ref, far, offset, 0, mat, chip ^ far, core)
            put_piece(out_ref, other_ref, far, offset, 0, mat, chip ^ far, 1 - core)
        offset += rows_of(mat)


def reduce_grads(where, halves, mats):
    groups, spread = lax.axis_size("shard"), lax.axis_size("replica")
    rows = all_rows(mats)
    keeps = [keep for _, keep in halves]
    recvs = [swap(send, "replica", 1) for send, _ in halves]
    out = jax.ShapeDtypeStruct((groups, rows, WIDE), HALF)
    moved = 2 * groups * rows * WIDE
    parts = vmem_call(partial(split_kernel, mats=mats), "split", where, keeps + recvs, [out] * 4, 12 * moved)
    parts = [parts[0]] + [swap(part, "replica", 2 * far) for far, part in enumerate(parts) if far > 0]
    out = jax.ShapeDtypeStruct((rows, WIDE), HALF)
    parts = vmem_call(merge_kernel, "merge", where, parts, [out] * groups, 5 * moved)
    parts = [parts[0]] + [swap(part, "shard", far) for far, part in enumerate(parts) if far > 0]
    terms = [part.astype(FLOAT) for part in parts]
    bits = groups // 2
    while bits:
        terms = [terms[i] + terms[i ^ bits] for i in range(bits)]
        bits //= 2
    piece = terms[0].astype(HALF)
    bits = 8
    while bits < spread:
        piece = (piece.astype(FLOAT) + swap(piece, "replica", bits).astype(FLOAT)).astype(HALF)
        bits *= 2
    mine = jnp.stack(around(piece))
    other = swap(mine, "replica", 1)
    outs = [
        jax.ShapeDtypeStruct((mat[1], WIDE) if mat == SMALL else (mat[1], mat[0] * 2 * WIDE), FLOAT) for mat in mats
    ]
    return vmem_call(partial(finish_kernel, mats=mats), "finish", where, [mine, other], outs, 8 * moved)


VECTOR_ROWS = 32


def pack_small(student_w, pool_w, dense_w, class_w, vectors, ups, smalls):
    shards = student_w.shape[0] // (student_w.shape[0] // dense_w.shape[0] * 32)
    kind = student_w.dtype
    third = student_w.shape[0] // shards // 3
    student = student_w.reshape(shards, 3, third, LANES).transpose(0, 2, 1, 3).reshape(shards, third, WIDE)
    pool = pool_w.reshape(shards, -1, WIDE)
    dense = dense_w.reshape(shards, -1, LANES)
    classes = class_w.reshape(shards, -1, LANES)
    lines = vectors.reshape(vectors.shape[0], shards, -1).transpose(1, 0, 2)
    lines = jnp.pad(lines, ((0, 0), (0, 0), (0, 2 * LANES - lines.shape[2]))).reshape(shards, -1, LANES)
    ups = ups.reshape(shards, -1, LANES)
    smalls = jnp.stack([jnp.pad(v.reshape(shards, -1), ((0, 0), (0, LANES - v.size // shards))) for v in smalls], axis=1)
    lines = jnp.concatenate([lines, ups, smalls], axis=1)
    lines = jnp.pad(lines, ((0, 0), (0, VECTOR_ROWS - lines.shape[1]), (0, 0))).astype(kind)
    return jnp.concatenate([student, pool, jnp.concatenate([dense, classes, lines], axis=2)], axis=1)


def unpack_small(small, wide, inner, student):
    shards = small.shape[0]
    third = wide // 4 // 3
    student_w = small[:, :third].reshape(shards, third, 3, LANES).transpose(0, 2, 1, 3).reshape(-1, LANES)
    pool_w = small[:, third : third + VECTOR_ROWS].reshape(-1, WIDE)
    rest = small[:, third + VECTOR_ROWS :]
    dense_w = rest[:, :, :LANES].reshape(-1, LANES)
    class_w = rest[:, :, LANES : 2 * LANES].reshape(-1, LANES)
    lines = rest[:, :, 2 * LANES :]
    vectors = lines[:, :16].reshape(shards, 8, 2 * LANES)[:, :, : wide // 4].transpose(1, 0, 2).reshape(8, -1)
    ups = lines[:, 16 : 16 + inner // 4 // LANES].reshape(-1)
    first = 16 + inner // 4 // LANES
    smalls = [lines[:, first + i, : student // 4].reshape(-1) for i in range(2)]
    return student_w, pool_w, dense_w, class_w, vectors, ups, smalls, lines[:, first + 2]


def body(
    tokens, cotangent, piece_starts, labels, qkv_weight, query_bias, value_bias, out_weight, out_bias, attention_gain,
    attention_shift, up_weight, up_bias, down_weight, down_bias, feed_gain, feed_shift, student_weight, student_bias,
    pool_weight, dense_weight, dense_bias, class_weight, class_bias,
):
    count, length, wide = tokens.shape
    inner = up_weight.shape[1]
    student_wide = student_weight.shape[1]
    classes = class_weight.shape[1]
    replica = lax.axis_index("replica")
    where = jnp.stack([lax.axis_index("shard"), (replica >> 1) & 3, replica & 1]).astype(jnp.int32)
    tokens, cotangent = tokens.reshape(length, wide), cotangent.reshape(length, wide)

    pad_class = lambda value: jnp.pad(value, ((0, 0), (0, LANES - classes)))
    vectors = jnp.stack([query_bias, value_bias, out_bias, attention_gain, attention_shift, down_bias, feed_gain, feed_shift])
    small = pack_small(
        student_weight, pool_weight, dense_weight, pad_class(class_weight), vectors, up_bias,
        [student_bias, dense_bias, jnp.zeros_like(dense_bias)],
    )[0]
    qkv_mats = ((3, qkv_weight.shape[0]),)
    rest_mats = ((1, out_weight.shape[0]), (4, up_weight.shape[0]), (1, down_weight.shape[0]))
    qkv, small = gather_weights(where, (qkv_weight, small), qkv_mats + (SMALL,))
    out_w, up, down = gather_weights(where, (out_weight, up_weight, down_weight), rest_mats)
    shards = lax.axis_size("shard")
    student_w, pool_w, dense_w, class_w, table, up_b, smalls, _ = unpack_small(
        small.reshape(shards, -1, WIDE), wide, inner, student_wide
    )
    table = table.astype(FLOAT)
    up_b = jnp.broadcast_to(up_b.astype(FLOAT)[None], (8, inner))
    real = (jnp.arange(LANES) < classes).astype(FLOAT)
    lines = [v.astype(FLOAT) for v in smalls] + [jnp.pad(class_bias.astype(FLOAT), (0, LANES - classes)), real]
    small_b = jnp.pad(jnp.stack(lines), ((0, 4), (0, 0)))

    joined = project(tokens, qkv, table)
    mixed, lse = attend_forward(joined, piece_starts)
    hidden, first, active, slope, unit1, rate1, unit2, rate2, student, pool = feed(
        mixed, tokens, out_w, up, down, student_w, pool_w, table, up_b, small_b
    )
    logits, grad_pool, grad_student, residual2, half2, grad_dense, grad_class, small_sums, sums2 = student_pass(
        labels, cotangent, pool, student, unit2, rate2, student_w, pool_w, dense_w, class_w, small_b, table
    )
    (grad_down,) = reduce_grads(where, [weight_grad(where, active, half2, "grad_down")], rest_mats[2:])
    grad_inner, residual1, half1, grad_mixed, sums1, up_sums = back(
        half2, residual2, slope, unit1, rate1, down, up, out_w, table
    )
    grad_student_w = mult_lt(hidden, grad_student)
    grad_pool_w = mult_lt(student, grad_pool)
    grad_joined, joined_sums = attend_backward(joined, piece_starts, mixed, grad_mixed, lse)

    table_sums = jnp.stack([
        joined_sums[0], joined_sums[1], sums1[2], sums1[0], sums1[1], sums2[2], sums2[0], sums2[1]
    ])
    class_sums = jnp.broadcast_to(small_sums[2, :32][None], (shards, 32))
    small = pack_small(
        grad_student_w, grad_pool_w, grad_dense, grad_class, table_sums, up_sums[0],
        [small_sums[0], small_sums[1], class_sums.reshape(-1)],
    ).astype(HALF)
    core = where[2]
    small = small.reshape(shards * 4, 2, SMALL_ROWS, WIDE)
    small = [
        lax.dynamic_index_in_dim(small, which, 1, keepdims=False).reshape(1, -1, WIDE) for which in (1 - core, core)
    ]
    grad_out, grad_up = reduce_grads(
        where,
        [weight_grad(where, mixed, half1, "grad_out"), weight_grad(where, first, grad_inner, "grad_up")],
        rest_mats[:2],
    )
    grad_qkv, small = reduce_grads(
        where, [weight_grad(where, tokens, grad_joined, "grad_qkv"), small], qkv_mats + (SMALL,)
    )
    input_grad = input_pass(grad_joined, residual1, qkv)
    g_student, g_pool, g_dense, g_class, g_table, g_up_b, g_smalls, g_class_b = unpack_small(
        small[None], wide, inner, student_wide
    )
    return (
        hidden.reshape(count, length, wide), logits[0:1, :classes], input_grad.reshape(count, length, wide),
        grad_qkv, g_table[0], g_table[1], grad_out, g_table[2], g_table[3], g_table[4], grad_up, g_up_b, grad_down,
        g_table[5], g_table[6], g_table[7], g_student, g_smalls[0], g_pool, g_dense, g_smalls[1], g_class[:, :classes],
        g_class_b[0, :classes],
    )


def solution(mesh):
    placed = (
        P(("shard", "replica"), None, None),
        P(("shard", "replica"), None, None),
        P(("shard", "replica"), None),
        P(("shard", "replica")),
        P("shard", None),
        P("shard"),
        P("shard"),
        P("shard", None),
        P("shard"),
        P("shard"),
        P("shard"),
        P("shard", None),
        P("shard"),
        P("shard", None),
        P("shard"),
        P("shard"),
        P("shard"),
        P("shard", None),
        P("shard"),
        P("shard", None),
        P("shard", None),
        P("shard"),
        P("shard", None),
        P(),
    )
    return jax.shard_map(
        body,
        mesh=mesh,
        in_specs=placed,
        out_specs=(
            P(("shard", "replica"), None, None),
            P(("shard", "replica"), None),
            P(("shard", "replica"), None, None),
            P("shard", None),
            P("shard"),
            P("shard"),
            P("shard", None),
            P("shard"),
            P("shard"),
            P("shard"),
            P("shard", None),
            P("shard"),
            P("shard", None),
            P("shard"),
            P("shard"),
            P("shard"),
            P("shard", None),
            P("shard"),
            P("shard", None),
            P("shard", None),
            P("shard"),
            P("shard", None),
            P(),
        ),
        check_vma=False,
    )
```

```python
from functools import partial

import jax
import jax.numpy as jnp
from jax import lax
from jax.experimental import pallas as pl
from jax.experimental.pallas import tpu as pltpu
from jax.sharding import PartitionSpec as P

HEADS = 12
POOL_HEADS = 2
PIECE = 256
NORM_EPS = 1e-06
MASKED_SCORE = -1e30
FLOAT = jnp.float32
HALF = jnp.bfloat16
PRECISE = lax.Precision.HIGHEST
LANES = 128
BLOCK = 256

ERF_SLOPE = 0.42
ERF_TERMS = (
    0.23691840576326206,
    0.2382680869907842,
    0.20182398814655725,
    0.2493386597508521,
    -0.10108083678814953,
    0.4156989047782712,
    -0.3092846516362072,
    0.06831743518928779,
)


LIGHT = pl.CostEstimate(flops=100000, transcendentals=0, bytes_accessed=100000)


def params_of(kinds, limit=60 << 20):
    return pltpu.CompilerParams(dimension_semantics=kinds, vmem_limit_bytes=limit)


def whole(shape, space=None):
    return pl.BlockSpec(shape, lambda *_: (0,) * len(shape))


def memory(kinds):
    return [pl.BlockSpec(memory_space=kind) for kind in kinds]


def mult(left, right):
    return jnp.dot(left, right, preferred_element_type=FLOAT)


def mult_rt(left, right):
    return lax.dot_general(left, right, (((1,), (1,)), ((), ())), preferred_element_type=FLOAT)


def mult_lt(left, right):
    return lax.dot_general(left, right, (((0,), (0,)), ((), ())), preferred_element_type=FLOAT)


def precise(left, right, dims):
    return lax.dot_general(
        left, right, ((dims[:1], dims[1:]), ((), ())), precision=PRECISE, preferred_element_type=FLOAT
    )


def key_extent(block, length):
    return min(length, (block + 2) * BLOCK)


def allowed_block(starts_ref, first_row, first_col, shape, row_axis):
    rows = first_row + lax.broadcasted_iota(jnp.int32, shape, row_axis)
    cols = first_col + lax.broadcasted_iota(jnp.int32, shape, 1 - row_axis)
    allowed = cols <= rows
    for piece in range(starts_ref.shape[1]):
        start = starts_ref[0, piece]
        inside = (rows >= start) & (rows < start + PIECE) & (cols >= start) & (cols < start + PIECE)
        allowed = allowed | inside
    return allowed


def fill_bias(starts_ref, bias_ref, length, row_axis):
    for block in range(length // BLOCK):
        wide = key_extent(block, length) - block * BLOCK
        shape = (BLOCK, wide) if row_axis == 0 else (wide, BLOCK)
        allowed = allowed_block(starts_ref, block * BLOCK, block * BLOCK, shape, row_axis)
        bias = jnp.where(allowed, 0.0, MASKED_SCORE).astype(FLOAT)
        if row_axis == 0:
            bias_ref[block, :, 0:wide] = bias
        else:
            bias_ref[block, 0:wide, :] = bias


def half_lanes(value, half):
    lane = lax.broadcasted_iota(jnp.int32, value.shape, 1)
    keep = (lane < LANES // 2) if half == 0 else (lane >= LANES // 2)
    return jnp.where(keep, value, jnp.zeros_like(value))


def attend_forward_kernel(starts_ref, q_ref, k_ref, v_ref, mixed_ref, flipped_ref, lse_ref, bias_ref):
    length = q_ref.shape[0]
    scale = (LANES // 2) ** (-0.5)

    @pl.when(pl.program_id(0) == 0)
    def _():
        fill_bias(starts_ref, bias_ref, length, 0)

    values = [half_lanes(v_ref[...], half) for half in range(2)]
    lane = lax.broadcasted_iota(jnp.int32, (BLOCK, LANES), 1)
    for block in range(length // BLOCK):
        begin = block * BLOCK
        extent = key_extent(block, length)
        query = q_ref[begin : begin + BLOCK, :] * jnp.asarray(scale, HALF)
        outs = []
        logs = []
        for half in range(2):
            scores = mult_rt(half_lanes(query, half), k_ref[0:extent, :])
            edge = scores[:, begin:extent] + bias_ref[block, :, 0 : extent - begin]
            parts = [edge] if begin == 0 else [scores[:, 0:begin], edge]
            ceiling = parts[0].max(axis=1, keepdims=True)
            for part in parts[1:]:
                ceiling = jnp.maximum(ceiling, part.max(axis=1, keepdims=True))
            total = 0.0
            mixed = 0.0
            place = 0
            for part in parts:
                raised = jnp.exp(part - ceiling)
                total = total + raised.sum(axis=1, keepdims=True)
                mixed = mixed + mult(
                    raised.astype(HALF), values[half][place : place + part.shape[1], :]
                )
                place += part.shape[1]
            outs.append(mixed / total)
            logs.append(ceiling + jnp.log(total))
        rounded = (outs[0] + outs[1]).astype(HALF)
        mixed_ref[begin : begin + BLOCK, :] = rounded
        flipped_ref[:, begin : begin + BLOCK] = rounded.T
        both = jnp.where(lane == 0, logs[0], logs[1])
        lse_ref[:, begin : begin + BLOCK] = both.T[0:8, :]


def attend_forward(joined, starts):
    length, wide = joined.shape
    pairs = wide // 3 // LANES
    return pl.pallas_call(
        attend_forward_kernel,
        grid=(pairs,),
        in_specs=[
            pl.BlockSpec(memory_space=pltpu.SMEM),
            pl.BlockSpec((length, LANES), lambda h: (0, h)),
            pl.BlockSpec((length, LANES), lambda h: (0, pairs + h)),
            pl.BlockSpec((length, LANES), lambda h: (0, 2 * pairs + h)),
        ],
        out_specs=[
            pl.BlockSpec((length, LANES), lambda h: (0, h)),
            pl.BlockSpec((LANES, length), lambda h: (h, 0)),
            pl.BlockSpec((8, length), lambda h: (h, 0)),
        ],
        out_shape=[
            jax.ShapeDtypeStruct((length, wide // 3), HALF),
            jax.ShapeDtypeStruct((wide // 3, length), HALF),
            jax.ShapeDtypeStruct((pairs * 8, length), FLOAT),
        ],
        scratch_shapes=[pltpu.VMEM((length // BLOCK, BLOCK, 2 * BLOCK), FLOAT)],
        compiler_params=params_of(("arbitrary",)),
        cost_estimate=LIGHT,
        name="attend_forward",
    )(starts, joined, joined, joined)


def attend_backward_kernel(
    starts_ref, q_ref, k_ref, v_ref, mixed_ref, grad_ref, lse_ref, out_ref, sums_ref, bias_ref, dk_ref, dv_ref
):
    length = q_ref.shape[0]
    scale = (LANES // 2) ** (-0.5)

    @pl.when(pl.program_id(0) == 0)
    def _():
        fill_bias(starts_ref, bias_ref, length, 1)

    product = grad_ref[...].astype(FLOAT) * mixed_ref[...].astype(FLOAT)
    row = lax.broadcasted_iota(jnp.int32, (8, LANES), 0)
    col = lax.broadcasted_iota(jnp.int32, (8, LANES), 1)
    picks = jnp.where((col < LANES // 2) == (row == 0), 1.0, 0.0).astype(FLOAT)
    inner = precise(picks, product, (1, 1))
    keys = [half_lanes(k_ref[...] * jnp.asarray(scale, HALF), half) for half in range(2)]
    values = [half_lanes(v_ref[...], half) for half in range(2)]
    dk_ref[...] = jnp.zeros_like(dk_ref)
    dv_ref[...] = jnp.zeros_like(dv_ref)
    query_sum = jnp.zeros((1, LANES), FLOAT)
    for block in range(length // BLOCK):
        begin = block * BLOCK
        extent = key_extent(block, length)
        query = q_ref[begin : begin + BLOCK, :]
        grad = grad_ref[begin : begin + BLOCK, :]
        grad_query = 0.0
        for half in range(2):
            scores = mult_rt(keys[half][0:extent, :], query)
            grad_probs = mult_rt(values[half][0:extent, :], grad)
            lse = lse_ref[half : half + 1, begin : begin + BLOCK]
            base = inner[half : half + 1, begin : begin + BLOCK]
            edge = scores[begin:extent, :] + bias_ref[block, 0 : extent - begin, :]
            shifted = edge if begin == 0 else jnp.concatenate([scores[0:begin, :], edge], axis=0)
            probs = jnp.exp(shifted - lse)
            grad_scores = (probs * (grad_probs - base)).astype(HALF)
            grad_half = half_lanes(grad, half)
            query_half = half_lanes(query * jnp.asarray(scale, HALF), half)
            dv_ref[0:extent, :] += mult(probs.astype(HALF), grad_half)
            dk_ref[0:extent, :] += mult(grad_scores, query_half)
            grad_query = grad_query + mult_lt(grad_scores, keys[half][0:extent, :])
        rounded = grad_query.astype(HALF)
        out_ref[0, begin : begin + BLOCK, :] = rounded
        query_sum = query_sum + rounded.astype(FLOAT).sum(axis=0, keepdims=True)
    out_ref[1, :, :] = dk_ref[...].astype(HALF)
    value = dv_ref[...].astype(HALF)
    out_ref[2, :, :] = value
    value_sum = value.astype(FLOAT).sum(axis=0, keepdims=True)
    sums_ref[...] = jnp.where(row == 0, query_sum, value_sum)


def attend_backward(joined, starts, mixed, grad_mixed, lse, part, parts):
    length, wide = joined.shape
    pairs = wide // 3 // LANES
    begin = pairs // parts * part
    wide //= parts
    return pl.pallas_call(
        attend_backward_kernel,
        grid=(pairs // parts,),
        in_specs=[
            pl.BlockSpec(memory_space=pltpu.SMEM),
            pl.BlockSpec((length, LANES), lambda h: (0, begin + h)),
            pl.BlockSpec((length, LANES), lambda h: (0, pairs + begin + h)),
            pl.BlockSpec((length, LANES), lambda h: (0, 2 * pairs + begin + h)),
            pl.BlockSpec((length, LANES), lambda h: (0, begin + h)),
            pl.BlockSpec((length, LANES), lambda h: (0, begin + h)),
            pl.BlockSpec((8, length), lambda h: (begin + h, 0)),
        ],
        out_specs=[
            pl.BlockSpec((3, length, LANES), lambda h: (0, 0, h)),
            pl.BlockSpec((8, LANES), lambda h: (0, h)),
        ],
        out_shape=[
            jax.ShapeDtypeStruct((3, length, wide // 3), HALF),
            jax.ShapeDtypeStruct((8, wide // 3), FLOAT),
        ],
        scratch_shapes=[
            pltpu.VMEM((length // BLOCK, 2 * BLOCK, BLOCK), FLOAT),
            pltpu.VMEM((length, LANES), FLOAT),
            pltpu.VMEM((length, LANES), FLOAT),
        ],
        compiler_params=params_of(("arbitrary",)),
        cost_estimate=LIGHT,
        name="attend_backward",
    )(starts, joined, joined, joined, mixed, grad_mixed, lse)


def normalise(values):
    middle = values.mean(axis=1, keepdims=True)
    centered = values - middle
    spread = (centered * centered).mean(axis=1, keepdims=True)
    rate = lax.rsqrt(spread + NORM_EPS)
    return centered * rate, rate


def normalise_backward(grad_unit, unit, rate):
    along = grad_unit.mean(axis=1, keepdims=True)
    across = (grad_unit * unit).mean(axis=1, keepdims=True)
    return rate * (grad_unit - along - unit * across)


def gelu_pair(inner):
    size = jnp.abs(inner)
    ratio = 1.0 / (1.0 + (ERF_SLOPE * 2.0**-0.5) * size)
    tail = jnp.full_like(ratio, 0.5 * ERF_TERMS[-1])
    for term in ERF_TERMS[-2::-1]:
        tail = tail * ratio + 0.5 * term
    bell = jnp.exp(-0.5 * inner * inner)
    tail = tail * ratio * bell
    below = jnp.where(inner < 0.0, tail, 1.0 - tail)
    return inner * below, below + inner * (bell * (2.0 * jnp.pi) ** -0.5)


QUERY_B, VALUE_B, OUT_B, GAIN1, SHIFT1, DOWN_B, GAIN2, SHIFT2 = range(8)


def flip_kernel(value_ref, out_ref):
    out_ref[...] = value_ref[...].T


def flip(value):
    return pl.pallas_call(
        flip_kernel,
        in_specs=memory([pltpu.VMEM]),
        out_specs=pl.BlockSpec(memory_space=pltpu.VMEM),
        out_shape=jax.ShapeDtypeStruct(value.shape[::-1], value.dtype),
        compiler_params=params_of(None),
        cost_estimate=LIGHT,
        name="flip",
    )(value)


def project_kernel(tokens_ref, weight_ref, table_ref, out_ref):
    wide = tokens_ref.shape[1]
    for part in range(3):
        value = mult(tokens_ref[...], weight_ref[:, part * wide : (part + 1) * wide])
        if part == 0:
            value = value + table_ref[QUERY_B : QUERY_B + 1, :]
        elif part == 2:
            value = value + table_ref[VALUE_B : VALUE_B + 1, :]
        out_ref[:, part * wide : (part + 1) * wide] = value.astype(HALF)


def project(tokens, weight, table):
    length, wide = tokens.shape
    return pl.pallas_call(
        project_kernel,
        grid=(length // BLOCK,),
        in_specs=[pl.BlockSpec((BLOCK, wide), lambda i: (i, 0))] + memory([pltpu.VMEM] * 2),
        out_specs=pl.BlockSpec((BLOCK, 3 * wide), lambda i: (i, 0)),
        out_shape=jax.ShapeDtypeStruct((length, 3 * wide), HALF),
        compiler_params=params_of(("arbitrary",)),
        cost_estimate=LIGHT,
        name="project",
    )(tokens, weight, table)


def feed_up_kernel(
    mixed_ref, tokens_ref, out_w_ref, up_ref, table_ref, up_b_ref,
    first_ref, first_t_ref, active_ref, active_t_ref, slope_ref, unit1_ref, rate1_ref,
):
    wide = tokens_ref.shape[1]
    line = lambda which: table_ref[which : which + 1, :]
    residual = tokens_ref[...].astype(FLOAT) + (mult(mixed_ref[...], out_w_ref[...]) + line(OUT_B))
    unit, rate = normalise(residual)
    unit1_ref[...] = unit.astype(HALF)
    rate1_ref[...] = jnp.broadcast_to(rate, rate1_ref.shape)
    first = unit * line(GAIN1) + line(SHIFT1)
    first_ref[...] = first
    first_half = first.astype(HALF)
    first_t_ref[...] = first_half.T
    for part in range(up_ref.shape[1] // wide):
        cols = slice(part * wide, (part + 1) * wide)
        inner = mult(first_half, up_ref[:, cols]) + up_b_ref[0:1, cols]
        active, slope = gelu_pair(inner)
        active = active.astype(HALF)
        active_ref[:, cols] = active
        active_t_ref[cols, :] = active.T
        slope_ref[:, cols] = slope.astype(HALF)


def block_specs():
    rows = lambda cols: pl.BlockSpec((BLOCK, cols), lambda i: (i, 0))
    flipped = lambda cols: pl.BlockSpec((cols, BLOCK), lambda i: (0, i))
    return rows, flipped


def feed_up(mixed, tokens, out_w, up, table, up_b):
    length, wide = tokens.shape
    inner = up.shape[1]
    rows, flipped = block_specs()
    weights = (out_w, up, table, up_b)
    return pl.pallas_call(
        feed_up_kernel,
        grid=(length // BLOCK,),
        in_specs=[rows(wide), rows(wide)] + memory([pltpu.VMEM] * len(weights)),
        out_specs=[rows(wide), flipped(wide), rows(inner), flipped(inner), rows(inner), rows(wide), rows(LANES)],
        out_shape=[
            struct((length, wide), FLOAT), struct((wide, length)), struct((length, inner)), struct((inner, length)),
            struct((length, inner)), struct((length, wide)), struct((length, LANES), FLOAT),
        ],
        compiler_params=params_of(("arbitrary",)),
        cost_estimate=LIGHT,
        name="feed_up",
    )(mixed, tokens, *weights)


def feed_down_kernel(
    first_ref, active_ref, down_ref, student_w_ref, pool_w_ref, table_ref, student_b_ref,
    hidden_ref, hidden_t_ref, unit2_ref, rate2_ref, student_t_ref, pool_ref,
):
    line = lambda which: table_ref[which : which + 1, :]
    total = first_ref[...] + line(DOWN_B) + mult(active_ref[...], down_ref[...])
    unit, rate = normalise(total)
    unit2_ref[...] = unit.astype(HALF)
    rate2_ref[...] = jnp.broadcast_to(rate, rate2_ref.shape)
    hidden = (unit * line(GAIN2) + line(SHIFT2)).astype(HALF)
    hidden_ref[...] = hidden
    hidden_t_ref[...] = hidden.T
    student = (mult(hidden, student_w_ref[...]) + student_b_ref[0:1, :]).astype(HALF)
    student_t_ref[...] = student.T
    pool_ref[...] = mult(student, pool_w_ref[...]).astype(HALF)


def feed_down(first, active, down, student_w, pool_w, table, student_b):
    length, wide = first.shape
    small = student_w.shape[1]
    rows, flipped = block_specs()
    weights = (down, student_w, pool_w, table, student_b)
    return pl.pallas_call(
        feed_down_kernel,
        grid=(length // BLOCK,),
        in_specs=[rows(wide), rows(active.shape[1])] + memory([pltpu.VMEM] * len(weights)),
        out_specs=[rows(wide), flipped(wide), rows(wide), rows(LANES), flipped(small), rows(3 * small)],
        out_shape=[
            struct((length, wide)), struct((wide, length)), struct((length, wide)), struct((length, LANES), FLOAT),
            struct((small, length)), struct((length, 3 * small)),
        ],
        compiler_params=params_of(("arbitrary",)),
        cost_estimate=LIGHT,
        name="feed_down",
    )(first, active, *weights)


def student_kernel(
    label_ref, cotangent_ref, pool_ref, unit2_ref, rate2_ref, student_w_ref, pool_w_ref, dense_ref, class_ref,
    small_b_ref, table_ref,
    logits_ref, grad_pool_ref, grad_student_ref, residual_ref, residual_half_ref, dense_grad_ref, class_grad_ref,
    small_sums_ref, sums_ref,
):
    length, three = pool_ref.shape
    small = three // 3
    scale = (small // POOL_HEADS) ** (-0.5)
    head_of = lambda axis: lax.broadcasted_iota(jnp.int32, (small, small), axis) // (small // POOL_HEADS)
    same = jnp.where(head_of(0) == head_of(1), 1.0, 0.0).astype(FLOAT)
    top = lax.broadcasted_iota(jnp.int32, (8, small), 0) == 0
    query = pool_ref[0:8, 0:small].astype(FLOAT)[0:1, :]
    key = pool_ref[:, small : 2 * small].astype(FLOAT)
    value = pool_ref[:, 2 * small : 3 * small].astype(FLOAT)
    scores = precise(key * query, same, (1, 0)) * scale
    raised = jnp.exp(scores - scores.max(axis=0, keepdims=True))
    weights = raised / raised.sum(axis=0, keepdims=True)
    pooled = (weights * value).sum(axis=0, keepdims=True)
    spread = lambda vector: jnp.where(top, vector, 0.0)
    dense = dense_ref[...].astype(FLOAT)
    classes = class_ref[...].astype(FLOAT)
    before = precise(spread(pooled), dense, (1, 0)) + small_b_ref[1:2, :]
    summary = jnp.tanh(before[0:1, :])
    logits = (precise(spread(summary), classes, (1, 0)) + small_b_ref[2:3, :])[0:1, :]
    lane = lax.broadcasted_iota(jnp.int32, (1, small), 1)
    real = small_b_ref[3:4, :] > 0.5
    masked = jnp.where(real, logits, MASKED_SCORE)
    lifted = jnp.where(real, jnp.exp(masked - masked.max(axis=1, keepdims=True)), 0.0)
    grad_logits = lifted / lifted.sum(axis=1, keepdims=True) - jnp.where(lane == label_ref[0], 1.0, 0.0)
    logits_ref[...] = logits[:, 0 : logits_ref.shape[1]]
    class_grad_ref[...] = precise(spread(summary), spread(grad_logits), (0, 0))
    grad_summary = precise(spread(grad_logits), classes, (1, 1))[0:1, :]
    grad_before = grad_summary * (1.0 - summary * summary)
    dense_grad_ref[...] = precise(spread(pooled), spread(grad_before), (0, 0))
    grad_pooled = precise(spread(grad_before), dense, (1, 1))[0:1, :]
    grad_weights = precise(value * grad_pooled, same, (1, 0))
    inner = (weights * grad_weights).sum(axis=0, keepdims=True)
    grad_scores = weights * (grad_weights - inner)
    grad_query = (grad_scores * key).sum(axis=0, keepdims=True) * scale
    first = lax.broadcasted_iota(jnp.int32, (length, small), 0) == 0
    grad_pool_ref[:, 0:small] = jnp.where(first, grad_query, 0.0).astype(HALF)
    grad_pool_ref[:, small : 2 * small] = (grad_scores * query * scale).astype(HALF)
    grad_pool_ref[:, 2 * small : 3 * small] = (weights * grad_pooled).astype(HALF)
    grad_student = mult_rt(grad_pool_ref[...], pool_w_ref[...])
    which = lax.broadcasted_iota(jnp.int32, (8, small), 0)
    student_sum = grad_student.sum(axis=0, keepdims=True)
    small_sums_ref[...] = jnp.where(
        which == 0, student_sum, jnp.where(which == 1, grad_before, jnp.where(which == 2, grad_logits, 0.0))
    )
    grad_student_ref[...] = grad_student.astype(HALF)

    sums_ref[...] = jnp.zeros_like(sums_ref)

    def one_block(block, _):
        rows = pl.ds(pl.multiple_of(block * BLOCK, BLOCK), BLOCK)
        grad = cotangent_ref[rows, :].astype(FLOAT) + mult_rt(grad_student_ref[rows, :], student_w_ref[...])
        unit = unit2_ref[rows, :].astype(FLOAT)
        residual = normalise_backward(grad * table_ref[GAIN2 : GAIN2 + 1, :], unit, rate2_ref[rows, 0:1])
        residual_ref[rows, :] = residual
        residual_half_ref[rows, :] = residual.astype(HALF)
        sums_ref[0:1, :] += (grad * unit).sum(axis=0, keepdims=True)
        sums_ref[1:2, :] += grad.sum(axis=0, keepdims=True)
        sums_ref[2:3, :] += residual.sum(axis=0, keepdims=True)
        return 0

    lax.fori_loop(0, length // BLOCK, one_block, 0)


def student_pass(label, cotangent, pool, unit2, rate2, student_w, pool_w, dense, classes, small_b, table, count):
    length, wide = cotangent.shape
    small = student_w.shape[1]
    struct = jax.ShapeDtypeStruct
    args = (cotangent, pool, unit2, rate2, student_w, pool_w, dense, classes, small_b, table)
    return pl.pallas_call(
        student_kernel,
        in_specs=memory([pltpu.SMEM] + [pltpu.VMEM] * len(args)),
        out_specs=memory([pltpu.VMEM] * 9),
        out_shape=[
            struct((1, count), FLOAT), struct((length, 3 * small), HALF), struct((length, small), HALF),
            struct((length, wide), FLOAT), struct((length, wide), HALF), struct((small, small), FLOAT),
            struct((small, small), FLOAT), struct((8, small), FLOAT), struct((8, wide), FLOAT),
        ],
        compiler_params=params_of(None),
        cost_estimate=LIGHT,
        name="student",
    )(label, *args)


def back_kernel(
    half_ref, residual_ref, slope_ref, unit1_ref, rate1_ref, down_ref, up_ref, out_w_ref, table_ref,
    inner_ref, residual1_ref, one_ref, mixed_ref, sums_ref, up_sums_ref,
):
    wide = residual_ref.shape[1]

    @pl.when(pl.program_id(0) == 0)
    def _():
        sums_ref[...] = jnp.zeros_like(sums_ref)
        up_sums_ref[...] = jnp.zeros_like(up_sums_ref)

    total = residual_ref[...]
    for part in range(up_ref.shape[1] // wide):
        cols = slice(part * wide, (part + 1) * wide)
        grad = mult_rt(half_ref[...], down_ref[cols, :]) * slope_ref[:, cols].astype(FLOAT)
        up_sums_ref[0:1, cols] += grad.sum(axis=0, keepdims=True)
        grad = grad.astype(HALF)
        inner_ref[:, cols] = grad
        total = total + mult_rt(grad, up_ref[:, cols])
    unit = unit1_ref[...].astype(FLOAT)
    residual = normalise_backward(total * table_ref[GAIN1 : GAIN1 + 1, :], unit, rate1_ref[:, 0:1])
    residual1_ref[...] = residual
    one = residual.astype(HALF)
    one_ref[...] = one
    mixed_ref[...] = mult_rt(one, out_w_ref[...]).astype(HALF)
    sums_ref[0:1, :] += (total * unit).sum(axis=0, keepdims=True)
    sums_ref[1:2, :] += total.sum(axis=0, keepdims=True)
    sums_ref[2:3, :] += residual.sum(axis=0, keepdims=True)


def back(half, residual, slope, unit1, rate1, down, up, out_w, table):
    length, wide = residual.shape
    inner = up.shape[1]
    rows = lambda cols: pl.BlockSpec((BLOCK, cols), lambda i: (i, 0))
    struct = jax.ShapeDtypeStruct
    weights = (down, up, out_w, table)
    return pl.pallas_call(
        back_kernel,
        grid=(length // BLOCK,),
        in_specs=[rows(wide), rows(wide), rows(inner), rows(wide), rows(LANES)] + memory([pltpu.VMEM] * len(weights)),
        out_specs=[rows(inner), rows(wide), rows(wide), rows(wide), whole((8, wide)), whole((8, inner))],
        out_shape=[
            struct((length, inner), HALF), struct((length, wide), FLOAT), struct((length, wide), HALF),
            struct((length, wide), HALF), struct((8, wide), FLOAT), struct((8, inner), FLOAT),
        ],
        compiler_params=params_of(("arbitrary",)),
        cost_estimate=LIGHT,
        name="back",
    )(half, residual, slope, unit1, rate1, *weights)


def input_kernel(low_ref, high_ref, residual_ref, weight_ref, out_ref):
    wide = residual_ref.shape[1]
    half = low_ref.shape[2]
    total = residual_ref[...]
    for part in range(3):
        for side, ref in enumerate((low_ref, high_ref)):
            begin = part * wide + side * half
            total = total + mult_rt(ref[part], weight_ref[:, begin : begin + half])
    out_ref[...] = total


def input_pass(halves, residual, weight):
    length, wide = residual.shape
    return pl.pallas_call(
        input_kernel,
        grid=(length // BLOCK,),
        in_specs=[pl.BlockSpec((3, BLOCK, wide // 2), lambda i: (0, i, 0))] * 2
        + [pl.BlockSpec((BLOCK, wide), lambda i: (i, 0)), pl.BlockSpec(memory_space=pltpu.VMEM)],
        out_specs=pl.BlockSpec((BLOCK, wide), lambda i: (i, 0)),
        out_shape=jax.ShapeDtypeStruct((length, wide), FLOAT),
        compiler_params=params_of(("arbitrary",)),
        cost_estimate=LIGHT,
        name="input_pass",
    )(*halves, residual, weight)


def swap(value, axis, bits):
    size = lax.axis_size(axis)
    return lax.ppermute(value, axis, [(i, i ^ bits) for i in range(size)])


def around(value):
    return [value] + [swap(value, "replica", bits) for bits in (2, 4, 6)]


WIDE = 384
SMALL = (0, 128)
SMALL_ROWS = 16
VECTOR_ROWS = 32


def rows_of(mat):
    return SMALL_ROWS if mat == SMALL else mat[0] * mat[1] // 4


def all_rows(mats):
    return sum(rows_of(mat) for mat in mats)


def after(value, *others):
    return lax.optimization_barrier((value,) + others)[0]


def vmem_call(kernel, name, where, inputs, outs, moved, scratch=()):
    return pl.pallas_call(
        kernel,
        in_specs=memory([pltpu.SMEM] + [pltpu.VMEM] * len(inputs)),
        out_specs=memory([pltpu.VMEM] * len(outs)),
        out_shape=outs,
        scratch_shapes=list(scratch),
        compiler_params=params_of(None),
        cost_estimate=LIGHT,
        name=name,
    )(where, *inputs)


def struct(shape, kind=HALF):
    return jax.ShapeDtypeStruct(shape, kind)


def aligned(begin, rows):
    return pl.ds(pl.multiple_of(begin, rows), rows)


def small_places(student_rows):
    third = student_rows // 3
    return third, third + 32


def fold_small(block_ref, base, student_ref, pool_ref, dense_ref, class_ref):
    third, last = small_places(student_ref.shape[0])
    for part in range(3):
        block_ref[base : base + third, part * LANES : (part + 1) * LANES] = student_ref[part * third : (part + 1) * third, :]
    block_ref[base + third : base + last, :] = pool_ref[...]
    rest = slice(base + last, base + 128)
    block_ref[rest, :] = jnp.zeros((128 - last, WIDE), block_ref.dtype)
    block_ref[rest, 0:LANES] = dense_ref[...]
    block_ref[rest, LANES : LANES + class_ref.shape[1]] = class_ref[...]


def unfold_small(block_ref, shard, student_ref, pool_ref, dense_ref, class_ref, rows):
    third, last = small_places(rows)
    base, short = shard * 128, 128 - last
    for part in range(3):
        begin = shard * rows + part * third
        student_ref[begin : begin + third, :] = block_ref[base : base + third, part * LANES : (part + 1) * LANES].astype(student_ref.dtype)
    target = slice(shard * short, (shard + 1) * short)
    pool_ref[target, :] = block_ref[base + third : base + last, :].astype(pool_ref.dtype)
    dense_ref[target, :] = block_ref[base + last : base + 128, 0:LANES].astype(dense_ref.dtype)
    classes = class_ref.shape[1]
    class_ref[target, :] = block_ref[base + last : base + 128, LANES : LANES + classes].astype(class_ref.dtype)


def pack_kernel(place_ref, *refs, mats, lines):
    chip, core = place_ref[1], place_ref[2]
    piece_ref = refs[-1]
    offset = 0
    if lines:
        base = all_rows(mats)
        for half in range(2):
            piece_ref[base : base + 16, half * LANES : (half + 1) * LANES] = refs[-2][half * 16 : half * 16 + 16, :]
        piece_ref[base : base + 16, 2 * LANES :] = jnp.zeros((16, WIDE - 2 * LANES), HALF)
    for mat, ref in zip(mats, refs):
        if mat == SMALL:
            small_ref = refs[-2]
            fold_small(small_ref, 0, *refs[len(mats) - 1 : len(mats) + 3])
            piece_ref[offset : offset + SMALL_ROWS, :] = small_ref[aligned((chip * 2 + core) * SMALL_ROWS, SMALL_ROWS), :]
            continue
        rows = mat[1] // 4
        for chunk in range(mat[0]):
            lanes = aligned(chunk * 2 * WIDE + core * WIDE, WIDE)
            piece_ref[offset : offset + rows, :] = ref[aligned(chip * rows, rows), lanes]
            offset += rows


def pack(where, shards, mats, lines=None):
    outs = [struct((all_rows(mats) + (0 if lines is None else 16), WIDE))]
    shards = list(shards) + ([] if lines is None else [lines])
    if SMALL in mats:
        outs = [struct(SMALL[1:] + (WIDE,))] + outs
    return vmem_call(partial(pack_kernel, mats=mats, lines=lines is not None), "pack", where, shards, outs, 2 * sum(s.size for s in shards))


def put_piece(out_ref, ref, step, offset, base, mat, chip, core):
    if mat == SMALL:
        target = aligned(base + (chip * 2 + core) * SMALL_ROWS, SMALL_ROWS)
        out_ref[target, :] = ref[step, offset : offset + SMALL_ROWS, :].astype(out_ref.dtype)
        return
    rows = mat[1] // 4
    for chunk in range(mat[0]):
        lanes = aligned(chunk * 2 * WIDE + core * WIDE, WIDE)
        first = offset + chunk * rows
        out_ref[aligned(base + chip * rows, rows), lanes] = ref[step, first : first + rows, :].astype(out_ref.dtype)


def place_kernel(place_ref, *refs, mats, rows):
    shard, chip, core = place_ref[0], place_ref[1], place_ref[2]
    count = len(mats)
    pieces, owns, outs = refs[:8], refs[8 : 8 + count], list(refs[8 + count :])
    if SMALL in mats:
        block_ref = outs.pop()
        smalls, outs = outs[count - 1 :], outs[: count - 1] + [block_ref]
    offset = 0
    for mat, own_ref, out_ref in zip(mats, owns, outs):
        height = mat[1]
        out_ref[aligned(shard * height, height), :] = own_ref[...]
        for number, ref in enumerate(pieces):
            far, other = number // 2, number % 2
            for step in range(ref.shape[0]):
                base = (shard ^ (step + 1)) * height
                put_piece(out_ref, ref, step, offset, base, mat, chip ^ far, core ^ other)
        offset += rows_of(mat)
    if SMALL in mats:
        for step in range(pieces[0].shape[0] + 1):
            unfold_small(block_ref, step, *smalls, rows)


def place(where, pieces, owns, outs, mats, rows=0):
    shards = pieces[0].shape[0] + 1
    scratch = [pltpu.VMEM((shards * SMALL[1], WIDE), HALF)] if SMALL in mats else []
    moved = 4 * shards * sum(own.size for own in owns)
    return vmem_call(partial(place_kernel, mats=mats, rows=rows), "place", where, pieces + list(owns), outs, moved, scratch)


def table_kernel(place_ref, *refs, classes, base):
    *lines, table_ref, up_ref, short_ref = refs
    shard = place_ref[0]
    wide, inner = table_ref.shape[1], up_ref.shape[1]
    shards = len(lines)
    ups = inner // shards // LANES
    table = jnp.zeros(table_ref.shape, FLOAT)
    shorts = jnp.zeros((8, LANES), FLOAT)
    for step, ref in enumerate(lines):
        target = shard ^ step
        if step == 0:
            block = ref[...].astype(FLOAT)
        else:
            block = jnp.concatenate([ref[base : base + 16, half * LANES : half * LANES + LANES] for half in range(2)], axis=0)
            block = block.astype(FLOAT)
        both = jnp.concatenate([block[0:8], block[8:16], jnp.zeros((8, wide - 2 * LANES), FLOAT)], axis=1)
        table = table + pltpu.roll(both, target * (wide // shards), 1)
        for line in range(ups):
            row = block[16 + line : 17 + line]
            up_ref[:, aligned(target * (inner // shards) + line * LANES, LANES)] = jnp.broadcast_to(row, (8, LANES))
        shorts = shorts + pltpu.roll(block[16 : 24], target * (LANES // shards), 1)
    table_ref[...] = table
    lane = lax.broadcasted_iota(jnp.int32, (1, LANES), 1)
    short_ref[0:2, :] = shorts[6:8]
    short_ref[2:3, :] = lines[0][...].astype(FLOAT)[24:25]
    short_ref[3:4, :] = jnp.where(lane < classes, 1.0, 0.0)
    short_ref[4:8, :] = jnp.zeros((4, LANES), FLOAT)


def lines_kernel(place_ref, *refs):
    *vectors, up_ref, student_ref, dense_ref, class_ref, out_ref, full_ref = refs
    full_ref[...] = jnp.zeros_like(full_ref)

    def put(row, value):
        full_ref[row : row + 1, 0 : value.shape[0]] = value.astype(FLOAT).reshape(1, value.shape[0])

    for line, ref in enumerate(vectors):
        put(line, ref[0:LANES])
        put(8 + line, ref[LANES:])
    for line in range(up_ref.shape[0] // LANES):
        put(16 + line, up_ref[line * LANES : (line + 1) * LANES])
    put(22, student_ref[...])
    put(23, dense_ref[...])
    put(24, class_ref[...])
    out_ref[...] = full_ref[...].astype(HALF)


def vector_lines(where, vectors, up_bias, shorts, class_bias):
    inputs = [*vectors, up_bias, *shorts, class_bias]
    (lines,) = vmem_call(lines_kernel, "lines", where, inputs, [struct((32, LANES))], 0, [pltpu.VMEM((32, LANES), FLOAT)])
    return lines


def from_shards(value):
    return [swap(value, "shard", bits) for bits in range(1, lax.axis_size("shard"))]


def both_cores(values):
    return [piece for value in values for piece in (value, swap(value, "replica", 1))]


def weight_grad_kernel(place_ref, left_ref, *refs):
    *rights, send_ref, keep_ref = refs
    core = place_ref[2]
    left = left_ref[...]
    if len(rights) == 2:
        for side, right_ref in enumerate(rights):
            for chunk in range(send_ref.shape[0]):
                value = mult(left, right_ref[chunk]).astype(HALF)

                @pl.when(core == side)
                def _():
                    keep_ref[chunk] = value

                @pl.when(core != side)
                def _():
                    send_ref[chunk] = value

        return
    for chunk in range(send_ref.shape[0]):
        for ref, which in ((send_ref, 1 - core), (keep_ref, core)):
            lanes = aligned(chunk * 2 * WIDE + which * WIDE, WIDE)
            ref[chunk] = mult(left, rights[0][:, lanes]).astype(HALF)


def weight_grad(where, left, rights, name):
    height, length = left.shape
    chunks = rights[0].shape[0] if len(rights) == 2 else rights[0].shape[1] // (2 * WIDE)
    block = 256
    out = struct((chunks, height, WIDE))
    return pl.pallas_call(
        weight_grad_kernel,
        grid=(height // block,),
        in_specs=[pl.BlockSpec(memory_space=pltpu.SMEM), pl.BlockSpec((block, length), lambda i: (i, 0))]
        + memory([pltpu.VMEM] * len(rights)),
        out_specs=[pl.BlockSpec((chunks, block, WIDE), lambda i: (0, i, 0))] * 2,
        out_shape=[out, out],
        compiler_params=params_of(("arbitrary",)),
        cost_estimate=LIGHT,
        name=name,
    )(where, left, *rights)


def small_grad_kernel(place_ref, hidden_ref, grad_student_ref, student_ref, grad_pool_ref, dense_ref, class_ref, send_ref, keep_ref, block_ref, first_ref, pool_ref):
    core = place_ref[2]
    shards = send_ref.shape[1] // (4 * SMALL_ROWS)
    first_ref[...] = mult(hidden_ref[...], grad_student_ref[...])
    pool_ref[...] = mult(student_ref[...], grad_pool_ref[...])
    part = lambda ref, shard: ref.at[pl.ds(shard * (ref.shape[0] // shards), ref.shape[0] // shards)]
    for shard in range(shards):
        fold_small(block_ref, shard * 128, *(part(ref, shard) for ref in (first_ref, pool_ref, dense_ref, class_ref)))
    for shard in range(shards):
        for chip in range(4):
            target = pl.ds((shard * 4 + chip) * SMALL_ROWS, SMALL_ROWS)
            for ref, which in ((send_ref, 1 - core), (keep_ref, core)):
                ref[0, target, :] = block_ref[aligned(shard * 128 + (chip * 2 + which) * SMALL_ROWS, SMALL_ROWS), :].astype(HALF)


def small_grad(where, hidden, grad_student, student, grad_pool, dense, classes, shards):
    outs = [struct((1, shards * 4 * SMALL_ROWS, WIDE))] * 2
    scratch = [
        pltpu.VMEM((shards * 128, WIDE), FLOAT), pltpu.VMEM((hidden.shape[0], LANES), FLOAT), pltpu.VMEM((LANES, WIDE), FLOAT)
    ]
    inputs = [hidden, grad_student, student, grad_pool, dense, classes]
    return vmem_call(small_grad_kernel, "small_grad", where, inputs, outs, 4 * hidden.size, scratch)


def vector_kernel(place_ref, low_ref, high_ref, one_ref, two_ref, up_ref, short_ref, half_ref, out_ref):
    half = low_ref.shape[1]
    for side, ref in enumerate((low_ref, high_ref)):
        lanes = slice(side * half, (side + 1) * half)
        lines = [ref[0:1, :], ref[1:2, :], one_ref[2:3, lanes], one_ref[0:1, lanes], one_ref[1:2, lanes]]
        lines += [two_ref[2:3, lanes], two_ref[0:1, lanes], two_ref[1:2, lanes]]
        for row, line in enumerate(lines):
            out_ref[side * 8 + row : side * 8 + row + 1, :] = line
    for row in range(up_ref.shape[1] // WIDE):
        out_ref[16 + row : 17 + row, :] = up_ref[0:1, row * WIDE : (row + 1) * WIDE]
    out_ref[24:32, :] = jnp.zeros((8, WIDE), FLOAT)
    for part in range(3):
        out_ref[24:25, part * LANES : (part + 1) * LANES] = short_ref[part : part + 1, :]
    half_ref[...] = out_ref[...].astype(HALF)


def split_kernel(place_ref, *refs, count, shards, vectors):
    chip = place_ref[1]
    keeps, recvs, outs = refs[:count], refs[count : 2 * count], refs[-4:]
    total = sum(keep.shape[0] * keep.shape[1] for keep in keeps) // (4 * shards)
    offset = 0
    for keep_ref, recv_ref in zip(keeps, recvs):
        height = keep_ref.shape[1] // shards
        rows = height // 4
        for chunk in range(keep_ref.shape[0]):
            for shard in range(shards):
                for far, out_ref in enumerate(outs):
                    source = aligned(shard * height + (chip ^ far) * rows, rows)
                    value = keep_ref[chunk, source, :].astype(FLOAT) + recv_ref[chunk, source, :].astype(FLOAT)
                    first = shard * total + offset
                    out_ref[first : first + rows, :] = value.astype(HALF)
            offset += rows
    if vectors:
        value = (refs[2 * count][...].astype(FLOAT) + refs[2 * count + 1][...].astype(FLOAT)).astype(HALF)
        for out_ref in outs:
            out_ref[shards * total : shards * total + VECTOR_ROWS, :] = value


def split(where, keeps, recvs, shards, vectors=()):
    total = sum(keep.shape[0] * keep.shape[1] for keep in keeps) // 4 + (VECTOR_ROWS if vectors else 0)
    kernel = partial(split_kernel, count=len(keeps), shards=shards, vectors=bool(vectors))
    inputs = list(keeps) + list(recvs) + list(vectors)
    return vmem_call(kernel, "split", where, inputs, [struct((total, WIDE))] * 4, 20 * total * WIDE)


def merge_kernel(place_ref, *refs, shards, vectors):
    shard = place_ref[0]
    parts, outs = refs[: -shards], refs[-shards:]
    offset = 0
    for group in range(len(parts) // 4):
        four = parts[4 * group : 4 * group + 4]
        last = vectors and group == len(parts) // 4 - 1
        rows = (four[0].shape[0] - (VECTOR_ROWS if last else 0)) // shards

        def total(source):
            a, b, c, d = (ref[source, :].astype(FLOAT) for ref in four)
            return ((a + b) + (c + d)).astype(HALF)

        for step, out_ref in enumerate(outs):
            out_ref[offset : offset + rows, :] = total(aligned((shard ^ step) * rows, rows))
        offset += rows
        if last:
            value = total(slice(shards * rows, shards * rows + VECTOR_ROWS))
            for out_ref in outs:
                out_ref[offset : offset + VECTOR_ROWS, :] = value


def merge(where, groups, shards, vectors=False):
    extra = VECTOR_ROWS if vectors else 0
    rows = (sum(four[0].shape[0] for four in groups) - extra) // shards + extra
    kernel = partial(merge_kernel, shards=shards, vectors=vectors)
    inputs = [part for four in groups for part in four]
    return vmem_call(kernel, "merge", where, inputs, [struct((rows, WIDE))] * shards, 10 * shards * rows * WIDE)


def total_kernel(place_ref, *refs, shards):
    parts, outs = refs[:shards], refs[shards:]
    offset = 0
    for out_ref in outs:
        rows = slice(offset, offset + out_ref.shape[0])
        terms = [ref[rows, :].astype(FLOAT) for ref in parts]
        while len(terms) > 1:
            half = len(terms) // 2
            terms = [terms[i] + terms[i + half] for i in range(half)]
        out_ref[...] = terms[0].astype(HALF)
        offset += out_ref.shape[0]


def total(where, parts, vectors=False):
    rows = parts[0].shape[0] - (VECTOR_ROWS if vectors else 0)
    outs = [struct((rows, WIDE))] + ([struct((VECTOR_ROWS, WIDE))] if vectors else [])
    outs = vmem_call(partial(total_kernel, shards=len(parts)), "total", where, parts, outs, 10 * rows * WIDE)
    bits = 8
    while bits < lax.axis_size("replica"):
        outs = [(v.astype(FLOAT) + swap(v, "replica", bits).astype(FLOAT)).astype(HALF) for v in outs]
        bits *= 2
    return outs


def finish_kernel(place_ref, *refs, mats, rows):
    chip, core = place_ref[1], place_ref[2]
    pieces, outs = refs[:8], list(refs[8:])
    if SMALL in mats:
        block_ref = outs.pop()
        smalls, outs = outs[len(mats) - 1 :], outs[: len(mats) - 1] + [block_ref]
    offset = 0
    for mat, out_ref in zip(mats, outs):
        for number, ref in enumerate(pieces):
            put_piece(out_ref, ref, 0, offset, 0, mat, chip ^ (number // 2), core ^ (number % 2))
        offset += rows_of(mat)
    if SMALL in mats:
        unfold_small(block_ref, 0, *smalls, rows)


def finish(where, pieces, mats, outs, rows=0):
    pieces = [piece[None] for piece in pieces]
    scratch = [pltpu.VMEM(SMALL[1:] + (WIDE,), FLOAT)] if SMALL in mats else []
    moved = 6 * sum(out.size for out in outs)
    return vmem_call(partial(finish_kernel, mats=mats, rows=rows), "finish", where, pieces, outs, moved, scratch)


def vector_out_kernel(place_ref, total_ref, *refs):
    tables, up_ref, shorts, class_ref = refs[:8], refs[8], refs[9:11], refs[11]
    shard = place_ref[0]
    wide = 2 * WIDE
    each = tables[0].shape[0]
    shards = wide // each
    values = total_ref[...].astype(FLOAT)
    table = jnp.concatenate([values[0:8], values[8:16]], axis=1)
    table = pltpu.roll(table, (shards - shard) * each, 1)[:, :each]
    for line, ref in enumerate(tables):
        ref[...] = table[line : line + 1].reshape(each)
    lines = up_ref.shape[0] // WIDE
    for line in range(lines):
        row = jnp.zeros((1, WIDE), FLOAT)
        for which in range(shards):
            row = row + jnp.where(shard == which, values[16 + which * lines + line : 17 + which * lines + line], 0.0)
        up_ref[line * WIDE : (line + 1) * WIDE] = row.reshape(WIDE)
    each = shorts[0].shape[0]
    for part, ref in enumerate(shorts):
        row = pltpu.roll(values[24:32, part * LANES : (part + 1) * LANES], (shards - shard) * each, 1)
        ref[...] = row[0:1, :each].reshape(each)
    class_ref[...] = values[24:25, 2 * LANES : 2 * LANES + class_ref.shape[0]].reshape(class_ref.shape[0])


def vector_out(where, value, shards, inner, classes):
    outs = [struct((2 * WIDE // shards,), FLOAT)] * 8 + [struct((inner // shards,), FLOAT)]
    outs += [struct((LANES // shards,), FLOAT)] * 2 + [struct((classes,), FLOAT)]
    return vmem_call(vector_out_kernel, "vector_out", where, [value], outs, 4 * value.size)


def body(
    tokens, cotangent, piece_starts, labels, qkv_weight, query_bias, value_bias, out_weight, out_bias, attention_gain,
    attention_shift, up_weight, up_bias, down_weight, down_bias, feed_gain, feed_shift, student_weight, student_bias,
    pool_weight, dense_weight, dense_bias, class_weight, class_bias,
):
    count, length, wide = tokens.shape
    inner = up_weight.shape[1]
    classes = class_weight.shape[1]
    student_rows = student_weight.shape[0]
    shards = lax.axis_size("shard")
    replica = lax.axis_index("replica")
    where = jnp.stack([lax.axis_index("shard"), (replica >> 1) & 3, replica & 1]).astype(jnp.int32)
    tokens, cotangent = tokens.reshape(length, wide), cotangent.reshape(length, wide)
    qkv_mats = ((3, qkv_weight.shape[0]),)
    up_mats = ((1, out_weight.shape[0]), (4, up_weight.shape[0]))
    down_mats = ((1, down_weight.shape[0]), SMALL)

    (piece,) = pack(where, [qkv_weight], qkv_mats)
    near = from_shards(piece)
    lines = vector_lines(
        where,
        [query_bias, value_bias, out_bias, attention_gain, attention_shift, down_bias, feed_gain, feed_shift],
        up_bias, [student_bias, dense_bias], class_bias,
    )
    near_stack = jnp.stack(near)
    qkv_around = around(near_stack)
    (up_piece,) = pack(where, [after(out_weight, *qkv_around[1:]), up_weight], up_mats, lines)
    up_near = from_shards(up_piece)
    tokens_t = flip(after(tokens, up_piece))
    qkv_pieces = both_cores(qkv_around)
    (qkv,) = place(where, qkv_pieces, [qkv_weight], [struct((shards * qkv_weight.shape[0], 3 * wide))], qkv_mats)
    up_near[0] = after(up_near[0], qkv, tokens_t)
    table, up_b, small_b = vmem_call(
        partial(table_kernel, classes=classes, base=all_rows(up_mats)), "table", where, [lines] + up_near,
        [struct((8, wide), FLOAT), struct((8, inner), FLOAT), struct((8, LANES), FLOAT)], 8 * 8 * inner,
    )
    up_stack = jnp.stack(up_near)
    small, down_piece = pack(
        where, [after(down_weight, up_stack), student_weight, pool_weight, dense_weight, class_weight], down_mats
    )
    up_around = around(up_stack)
    down_near = [swap(down_piece, "shard", bits) for bits in range(1, shards - 1)]
    qkv = after(qkv, up_stack, tokens_t, down_piece)
    joined = project(tokens, qkv, table)
    joined, down_piece, up_around[1] = lax.optimization_barrier((joined, down_piece, up_around[1]))
    down_near.append(swap(down_piece, "shard", shards - 1))
    mixed, mixed_t, lse = attend_forward(joined, piece_starts)
    whole_of = lambda shard: struct((shards * shard.shape[0], shard.shape[1]))
    mixed, *arrived = lax.optimization_barrier((mixed, *down_near, *up_around))
    down_near, up_around = arrived[: shards - 1], arrived[shards - 1 :]
    down_stack = jnp.stack(down_near)
    down_around = around(after(down_stack, mixed))
    out_w, up = place(
        where, both_cores(up_around), [out_weight, up_weight], [whole_of(out_weight), whole_of(up_weight)], up_mats
    )

    first, first_t, active, active_t, slope, unit1, rate1 = feed_up(
        mixed, tokens, after(out_w, down_stack), up, table, up_b
    )
    rest = [whole_of(s) for s in (down_weight, student_weight, pool_weight, dense_weight)]
    rest.append(struct((shards * class_weight.shape[0], LANES)))
    active, *down_around = lax.optimization_barrier((active, *down_around))
    down, student_w, pool_w, dense_w, class_w = place(
        where, both_cores(down_around), [down_weight, small], rest, down_mats, student_rows
    )
    hidden, hidden_t, unit2, rate2, student_t, pool = feed_down(
        first, active, down, student_w, pool_w, table, small_b
    )
    logits, grad_pool, grad_student, residual2, half2, grad_dense, grad_class, small_sums, sums2 = student_pass(
        labels, cotangent, pool, unit2, rate2, student_w, pool_w, dense_w, class_w, small_b, table, classes
    )
    core_swap = lambda value: swap(value, "replica", 1)
    exchange = lambda parts: [parts[0]] + [swap(part, "replica", 2 * far) for far, part in enumerate(parts) if far > 0]
    spread = lambda parts: [parts[0]] + [swap(part, "shard", far) for far, part in enumerate(parts) if far > 0]
    send_down, keep_down = weight_grad(where, active_t, [half2], "grad_down")
    send_small, keep_small = small_grad(
        where, after(hidden_t, send_down), grad_student, student_t, grad_pool, grad_dense, grad_class, shards
    )
    parts_a = split(where, [keep_down], [core_swap(send_down)], shards)
    exchanged_a = exchange(parts_a)
    grad_inner, residual1, half1, grad_mixed, sums1, up_sums = back(
        after(half2, parts_a[0], keep_small), residual2, slope, unit1, rate1, down, up, out_w, table
    )
    send_up, keep_up = weight_grad(where, first_t, [grad_inner], "grad_up")
    swapped_small = core_swap(send_small)
    send_up, mixed_t, swapped_small, *exchanged_a = lax.optimization_barrier((send_up, mixed_t, swapped_small, *exchanged_a))
    send_out, keep_out = weight_grad(where, mixed_t, [half1], "grad_out")
    parts_b = split(where, [keep_out, keep_up], [core_swap(send_out), core_swap(send_up)], shards)
    exchanged_b = exchange(parts_b)
    low, low_sums = attend_backward(joined, piece_starts, mixed, after(grad_mixed, parts_b[0]), lse, 0, 2)
    high, high_sums = attend_backward(joined, piece_starts, mixed, after(grad_mixed, low), lse, 1, 2)
    high, *exchanged_b = lax.optimization_barrier((high, *exchanged_b))
    ready = merge(where, [exchanged_b, exchanged_a], shards)
    near_ab = spread(ready)
    send_qkv, keep_qkv = weight_grad(where, after(tokens_t, ready[0]), [low, high], "grad_qkv")
    (vectors,) = vmem_call(
        vector_kernel, "vectors", where,
        [low_sums, high_sums, sums1, sums2, up_sums, small_sums], [struct((VECTOR_ROWS, WIDE))], 4 * VECTOR_ROWS * WIDE,
        [pltpu.VMEM((VECTOR_ROWS, WIDE), FLOAT)],
    )
    parts_c = split(
        where, [keep_qkv, keep_small], [core_swap(send_qkv), swapped_small], shards, (vectors, core_swap(vectors))
    )
    exchanged_c = exchange(parts_c)
    input_grad = input_pass((after(low, parts_c[0]), high), residual1, qkv)
    near_ab[0] = after(near_ab[0], input_grad)
    (piece_ab,) = total(where, near_ab)
    piece_ab, *exchanged_c = lax.optimization_barrier((piece_ab, *exchanged_c))
    ready = merge(where, [exchanged_c], shards, True)
    near_c = spread(ready)
    around_ab = around(after(piece_ab, ready[0]))
    near_c[0], *around_ab = lax.optimization_barrier((near_c[0], *around_ab))
    pieces_ab = both_cores(around_ab)
    piece_c, vectors = total(where, near_c, True)
    pieces_c = both_cores(around(piece_c))
    full = lambda shard: struct(shard.shape, FLOAT)
    ab_mats = up_mats + down_mats[:1]
    grad_out, grad_up, grad_down = finish(
        where, pieces_ab, ab_mats, [full(s) for s in (out_weight, up_weight, down_weight)]
    )
    *g_table, g_up_b, g_student_b, g_dense_b, g_class_b = vector_out(where, vectors, shards, inner, classes)
    grad_qkv, g_student, g_pool, g_dense, g_class = finish(
        where, pieces_c, qkv_mats + (SMALL,),
        [full(s) for s in (qkv_weight, student_weight, pool_weight, dense_weight, class_weight)], student_rows,
    )
    return (
        hidden.reshape(count, length, wide), logits, input_grad.reshape(count, length, wide),
        grad_qkv, g_table[0], g_table[1], grad_out, g_table[2], g_table[3], g_table[4], grad_up, g_up_b, grad_down,
        g_table[5], g_table[6], g_table[7], g_student, g_student_b, g_pool, g_dense, g_dense_b, g_class, g_class_b,
    )


def solution(mesh):
    placed = (
        P(("shard", "replica"), None, None),
        P(("shard", "replica"), None, None),
        P(("shard", "replica"), None),
        P(("shard", "replica")),
        P("shard", None),
        P("shard"),
        P("shard"),
        P("shard", None),
        P("shard"),
        P("shard"),
        P("shard"),
        P("shard", None),
        P("shard"),
        P("shard", None),
        P("shard"),
        P("shard"),
        P("shard"),
        P("shard", None),
        P("shard"),
        P("shard", None),
        P("shard", None),
        P("shard"),
        P("shard", None),
        P(),
    )
    return jax.shard_map(
        body,
        mesh=mesh,
        in_specs=placed,
        out_specs=(
            P(("shard", "replica"), None, None),
            P(("shard", "replica"), None),
            P(("shard", "replica"), None, None),
            P("shard", None),
            P("shard"),
            P("shard"),
            P("shard", None),
            P("shard"),
            P("shard"),
            P("shard"),
            P("shard", None),
            P("shard"),
            P("shard", None),
            P("shard"),
            P("shard"),
            P("shard"),
            P("shard", None),
            P("shard"),
            P("shard", None),
            P("shard", None),
            P("shard"),
            P("shard", None),
            P(),
        ),
        check_vma=False,
    )
```

```python
from functools import partial

import jax
import jax.numpy as jnp
from jax import lax
from jax.experimental import pallas as pl
from jax.experimental.pallas import tpu as pltpu
from jax.sharding import PartitionSpec as P

HEADS = 12
POOL_HEADS = 2
PIECE = 256
NORM_EPS = 1e-06
MASKED_SCORE = -1e30
FLOAT = jnp.float32
HALF = jnp.bfloat16
PRECISE = lax.Precision.HIGHEST
LANES = 128
BLOCK = 256

ERF_SLOPE = 0.42
ERF_TERMS = (
    0.23691840576326206,
    0.2382680869907842,
    0.20182398814655725,
    0.2493386597508521,
    -0.10108083678814953,
    0.4156989047782712,
    -0.3092846516362072,
    0.06831743518928779,
)


LIGHT = pl.CostEstimate(flops=100000, transcendentals=0, bytes_accessed=100000)


def params_of(kinds, limit=44 << 20):
    return pltpu.CompilerParams(dimension_semantics=kinds, vmem_limit_bytes=limit)


def whole(shape, space=None):
    return pl.BlockSpec(shape, lambda *_: (0,) * len(shape))


def memory(kinds):
    return [pl.BlockSpec(memory_space=kind) for kind in kinds]


def mult(left, right):
    return jnp.dot(left, right, preferred_element_type=FLOAT)


def mult_rt(left, right):
    return lax.dot_general(left, right, (((1,), (1,)), ((), ())), preferred_element_type=FLOAT)


def mult_lt(left, right):
    return lax.dot_general(left, right, (((0,), (0,)), ((), ())), preferred_element_type=FLOAT)


def precise(left, right, dims):
    return lax.dot_general(
        left, right, ((dims[:1], dims[1:]), ((), ())), precision=PRECISE, preferred_element_type=FLOAT
    )


def key_extent(block, length):
    return min(length, (block + 2) * BLOCK)


def allowed_block(starts_ref, first_row, first_col, shape, row_axis):
    rows = first_row + lax.broadcasted_iota(jnp.int32, shape, row_axis)
    cols = first_col + lax.broadcasted_iota(jnp.int32, shape, 1 - row_axis)
    allowed = cols <= rows
    for piece in range(starts_ref.shape[1]):
        start = starts_ref[0, piece]
        inside = (rows >= start) & (rows < start + PIECE) & (cols >= start) & (cols < start + PIECE)
        allowed = allowed | inside
    return allowed


def fill_bias(starts_ref, bias_ref, length, row_axis):
    for block in range(length // BLOCK):
        wide = key_extent(block, length) - block * BLOCK
        shape = (BLOCK, wide) if row_axis == 0 else (wide, BLOCK)
        allowed = allowed_block(starts_ref, block * BLOCK, block * BLOCK, shape, row_axis)
        bias = jnp.where(allowed, 0.0, MASKED_SCORE).astype(FLOAT)
        if row_axis == 0:
            bias_ref[block, :, 0:wide] = bias
        else:
            bias_ref[block, 0:wide, :] = bias


def half_lanes(value, half):
    lane = lax.broadcasted_iota(jnp.int32, value.shape, 1)
    keep = (lane < LANES // 2) if half == 0 else (lane >= LANES // 2)
    return jnp.where(keep, value, jnp.zeros_like(value))


def attend_forward_kernel(starts_ref, q_ref, k_ref, v_ref, mixed_ref, flipped_ref, lse_ref, bias_ref):
    length = q_ref.shape[0]
    scale = (LANES // 2) ** (-0.5)

    @pl.when(pl.program_id(0) == 0)
    def _():
        fill_bias(starts_ref, bias_ref, length, 0)

    values = [half_lanes(v_ref[...], half) for half in range(2)]
    lane = lax.broadcasted_iota(jnp.int32, (BLOCK, LANES), 1)
    for block in range(length // BLOCK):
        begin = block * BLOCK
        extent = key_extent(block, length)
        query = q_ref[begin : begin + BLOCK, :] * jnp.asarray(scale, HALF)
        outs = []
        logs = []
        for half in range(2):
            scores = mult_rt(half_lanes(query, half), k_ref[0:extent, :])
            edge = scores[:, begin:extent] + bias_ref[block, :, 0 : extent - begin]
            parts = [edge] if begin == 0 else [scores[:, 0:begin], edge]
            ceiling = parts[0].max(axis=1, keepdims=True)
            for part in parts[1:]:
                ceiling = jnp.maximum(ceiling, part.max(axis=1, keepdims=True))
            total = 0.0
            mixed = 0.0
            place = 0
            for part in parts:
                raised = jnp.exp(part - ceiling)
                total = total + raised.sum(axis=1, keepdims=True)
                mixed = mixed + mult(
                    raised.astype(HALF), values[half][place : place + part.shape[1], :]
                )
                place += part.shape[1]
            outs.append(mixed / total)
            logs.append(ceiling + jnp.log(total))
        rounded = (outs[0] + outs[1]).astype(HALF)
        mixed_ref[begin : begin + BLOCK, :] = rounded
        flipped_ref[:, begin : begin + BLOCK] = rounded.T
        both = jnp.where(lane == 0, logs[0], logs[1])
        lse_ref[:, begin : begin + BLOCK] = both.T[0:8, :]


def attend_forward(joined, starts):
    length, wide = joined.shape
    pairs = wide // 3 // LANES
    return pl.pallas_call(
        attend_forward_kernel,
        grid=(pairs,),
        in_specs=[
            pl.BlockSpec(memory_space=pltpu.SMEM),
            pl.BlockSpec((length, LANES), lambda h: (0, h)),
            pl.BlockSpec((length, LANES), lambda h: (0, pairs + h)),
            pl.BlockSpec((length, LANES), lambda h: (0, 2 * pairs + h)),
        ],
        out_specs=[
            pl.BlockSpec((length, LANES), lambda h: (0, h)),
            pl.BlockSpec((LANES, length), lambda h: (h, 0)),
            pl.BlockSpec((8, length), lambda h: (h, 0)),
        ],
        out_shape=[
            jax.ShapeDtypeStruct((length, wide // 3), HALF),
            jax.ShapeDtypeStruct((wide // 3, length), HALF),
            jax.ShapeDtypeStruct((pairs * 8, length), FLOAT),
        ],
        scratch_shapes=[pltpu.VMEM((length // BLOCK, BLOCK, 2 * BLOCK), FLOAT)],
        compiler_params=params_of(("arbitrary",)),
        cost_estimate=LIGHT,
        name="attend_forward",
    )(starts, joined, joined, joined)


def attend_backward_kernel(
    starts_ref, q_ref, k_ref, v_ref, mixed_ref, grad_ref, lse_ref, out_ref, sums_ref, bias_ref, dk_ref, dv_ref
):
    length = q_ref.shape[0]
    scale = (LANES // 2) ** (-0.5)

    @pl.when(pl.program_id(0) == 0)
    def _():
        fill_bias(starts_ref, bias_ref, length, 1)

    product = grad_ref[...].astype(FLOAT) * mixed_ref[...].astype(FLOAT)
    row = lax.broadcasted_iota(jnp.int32, (8, LANES), 0)
    col = lax.broadcasted_iota(jnp.int32, (8, LANES), 1)
    picks = jnp.where((col < LANES // 2) == (row == 0), 1.0, 0.0).astype(FLOAT)
    inner = precise(picks, product, (1, 1))
    keys = [half_lanes(k_ref[...] * jnp.asarray(scale, HALF), half) for half in range(2)]
    values = [half_lanes(v_ref[...], half) for half in range(2)]
    dk_ref[...] = jnp.zeros_like(dk_ref)
    dv_ref[...] = jnp.zeros_like(dv_ref)
    query_sum = jnp.zeros((1, LANES), FLOAT)
    for block in range(length // BLOCK):
        begin = block * BLOCK
        extent = key_extent(block, length)
        query = q_ref[begin : begin + BLOCK, :]
        grad = grad_ref[begin : begin + BLOCK, :]
        grad_query = 0.0
        for half in range(2):
            scores = mult_rt(keys[half][0:extent, :], query)
            grad_probs = mult_rt(values[half][0:extent, :], grad)
            lse = lse_ref[half : half + 1, begin : begin + BLOCK]
            base = inner[half : half + 1, begin : begin + BLOCK]
            edge = scores[begin:extent, :] + bias_ref[block, 0 : extent - begin, :]
            shifted = edge if begin == 0 else jnp.concatenate([scores[0:begin, :], edge], axis=0)
            probs = jnp.exp(shifted - lse)
            grad_scores = (probs * (grad_probs - base)).astype(HALF)
            grad_half = half_lanes(grad, half)
            query_half = half_lanes(query * jnp.asarray(scale, HALF), half)
            dv_ref[0:extent, :] += mult(probs.astype(HALF), grad_half)
            dk_ref[0:extent, :] += mult(grad_scores, query_half)
            grad_query = grad_query + mult_lt(grad_scores, keys[half][0:extent, :])
        rounded = grad_query.astype(HALF)
        out_ref[0, begin : begin + BLOCK, :] = rounded
        query_sum = query_sum + rounded.astype(FLOAT).sum(axis=0, keepdims=True)
    out_ref[1, :, :] = dk_ref[...].astype(HALF)
    value = dv_ref[...].astype(HALF)
    out_ref[2, :, :] = value
    value_sum = value.astype(FLOAT).sum(axis=0, keepdims=True)
    sums_ref[...] = jnp.where(row == 0, query_sum, value_sum)


def attend_backward(joined, starts, mixed, grad_mixed, lse, part, parts):
    length, wide = joined.shape
    pairs = wide // 3 // LANES
    begin = pairs // parts * part
    wide //= parts
    return pl.pallas_call(
        attend_backward_kernel,
        grid=(pairs // parts,),
        in_specs=[
            pl.BlockSpec(memory_space=pltpu.SMEM),
            pl.BlockSpec((length, LANES), lambda h: (0, begin + h)),
            pl.BlockSpec((length, LANES), lambda h: (0, pairs + begin + h)),
            pl.BlockSpec((length, LANES), lambda h: (0, 2 * pairs + begin + h)),
            pl.BlockSpec((length, LANES), lambda h: (0, begin + h)),
            pl.BlockSpec((length, LANES), lambda h: (0, begin + h)),
            pl.BlockSpec((8, length), lambda h: (begin + h, 0)),
        ],
        out_specs=[
            pl.BlockSpec((3, length, LANES), lambda h: (0, 0, h)),
            pl.BlockSpec((8, LANES), lambda h: (0, h)),
        ],
        out_shape=[
            jax.ShapeDtypeStruct((3, length, wide // 3), HALF),
            jax.ShapeDtypeStruct((8, wide // 3), FLOAT),
        ],
        scratch_shapes=[
            pltpu.VMEM((length // BLOCK, 2 * BLOCK, BLOCK), FLOAT),
            pltpu.VMEM((length, LANES), FLOAT),
            pltpu.VMEM((length, LANES), FLOAT),
        ],
        compiler_params=params_of(("arbitrary",)),
        cost_estimate=LIGHT,
        name="attend_backward",
    )(starts, joined, joined, joined, mixed, grad_mixed, lse)


def normalise(values):
    middle = values.mean(axis=1, keepdims=True)
    centered = values - middle
    spread = (centered * centered).mean(axis=1, keepdims=True)
    rate = lax.rsqrt(spread + NORM_EPS)
    return centered * rate, rate


def normalise_backward(grad_unit, unit, rate):
    along = grad_unit.mean(axis=1, keepdims=True)
    across = (grad_unit * unit).mean(axis=1, keepdims=True)
    return rate * (grad_unit - along - unit * across)


def gelu_pair(inner):
    size = jnp.abs(inner)
    ratio = 1.0 / (1.0 + (ERF_SLOPE * 2.0**-0.5) * size)
    tail = jnp.full_like(ratio, 0.5 * ERF_TERMS[-1])
    for term in ERF_TERMS[-2::-1]:
        tail = tail * ratio + 0.5 * term
    bell = jnp.exp(-0.5 * inner * inner)
    tail = tail * ratio * bell
    below = jnp.where(inner < 0.0, tail, 1.0 - tail)
    return inner * below, below + inner * (bell * (2.0 * jnp.pi) ** -0.5)


QUERY_B, VALUE_B, OUT_B, GAIN1, SHIFT1, DOWN_B, GAIN2, SHIFT2 = range(8)


def flip_kernel(value_ref, out_ref):
    out_ref[...] = value_ref[...].T


def flip(value):
    return pl.pallas_call(
        flip_kernel,
        in_specs=memory([pltpu.VMEM]),
        out_specs=pl.BlockSpec(memory_space=pltpu.VMEM),
        out_shape=jax.ShapeDtypeStruct(value.shape[::-1], value.dtype),
        compiler_params=params_of(None),
        cost_estimate=LIGHT,
        name="flip",
    )(value)


def project_kernel(tokens_ref, weight_ref, table_ref, out_ref):
    wide = tokens_ref.shape[1]
    for part in range(3):
        value = mult(tokens_ref[...], weight_ref[:, part * wide : (part + 1) * wide])
        if part == 0:
            value = value + table_ref[QUERY_B : QUERY_B + 1, :]
        elif part == 2:
            value = value + table_ref[VALUE_B : VALUE_B + 1, :]
        out_ref[:, part * wide : (part + 1) * wide] = value.astype(HALF)


def project(tokens, weight, table):
    length, wide = tokens.shape
    return pl.pallas_call(
        project_kernel,
        grid=(length // BLOCK,),
        in_specs=[pl.BlockSpec((BLOCK, wide), lambda i: (i, 0))] + memory([pltpu.VMEM] * 2),
        out_specs=pl.BlockSpec((BLOCK, 3 * wide), lambda i: (i, 0)),
        out_shape=jax.ShapeDtypeStruct((length, 3 * wide), HALF),
        compiler_params=params_of(("arbitrary",)),
        cost_estimate=LIGHT,
        name="project",
    )(tokens, weight, table)


def feed_up_kernel(
    mixed_ref, tokens_ref, out_w_ref, up_ref, table_ref, up_b_ref,
    first_ref, first_t_ref, active_ref, active_t_ref, slope_ref, unit1_ref, rate1_ref,
):
    wide = tokens_ref.shape[1]
    line = lambda which: table_ref[which : which + 1, :]
    residual = tokens_ref[...].astype(FLOAT) + (mult(mixed_ref[...], out_w_ref[...]) + line(OUT_B))
    unit, rate = normalise(residual)
    unit1_ref[...] = unit.astype(HALF)
    rate1_ref[...] = jnp.broadcast_to(rate, rate1_ref.shape)
    first = unit * line(GAIN1) + line(SHIFT1)
    first_ref[...] = first
    first_half = first.astype(HALF)
    first_t_ref[...] = first_half.T
    for part in range(up_ref.shape[1] // wide):
        cols = slice(part * wide, (part + 1) * wide)
        inner = mult(first_half, up_ref[:, cols]) + up_b_ref[0:1, cols]
        active, slope = gelu_pair(inner)
        active = active.astype(HALF)
        active_ref[:, cols] = active
        active_t_ref[cols, :] = active.T
        slope_ref[:, cols] = slope.astype(HALF)


def block_specs():
    rows = lambda cols: pl.BlockSpec((BLOCK, cols), lambda i: (i, 0))
    flipped = lambda cols: pl.BlockSpec((cols, BLOCK), lambda i: (0, i))
    return rows, flipped


def feed_up(mixed, tokens, out_w, up, table, up_b):
    length, wide = tokens.shape
    inner = up.shape[1]
    rows, flipped = block_specs()
    weights = (out_w, up, table, up_b)
    return pl.pallas_call(
        feed_up_kernel,
        grid=(length // BLOCK,),
        in_specs=[rows(wide), rows(wide)] + memory([pltpu.VMEM] * len(weights)),
        out_specs=[rows(wide), flipped(wide), rows(inner), flipped(inner), rows(inner), rows(wide), rows(LANES)],
        out_shape=[
            struct((length, wide), FLOAT), struct((wide, length)), struct((length, inner)), struct((inner, length)),
            struct((length, inner)), struct((length, wide)), struct((length, LANES), FLOAT),
        ],
        compiler_params=params_of(("arbitrary",)),
        cost_estimate=LIGHT,
        name="feed_up",
    )(mixed, tokens, *weights)


def feed_down_kernel(
    first_ref, active_ref, down_ref, student_w_ref, pool_w_ref, table_ref, student_b_ref,
    hidden_ref, hidden_t_ref, unit2_ref, rate2_ref, student_t_ref, pool_ref,
):
    line = lambda which: table_ref[which : which + 1, :]
    total = first_ref[...] + line(DOWN_B) + mult(active_ref[...], down_ref[...])
    unit, rate = normalise(total)
    unit2_ref[...] = unit.astype(HALF)
    rate2_ref[...] = jnp.broadcast_to(rate, rate2_ref.shape)
    hidden = (unit * line(GAIN2) + line(SHIFT2)).astype(HALF)
    hidden_ref[...] = hidden
    hidden_t_ref[...] = hidden.T
    student = (mult(hidden, student_w_ref[...]) + student_b_ref[0:1, :]).astype(HALF)
    student_t_ref[...] = student.T
    pool_ref[...] = mult(student, pool_w_ref[...]).astype(HALF)


def feed_down(first, active, down, student_w, pool_w, table, student_b):
    length, wide = first.shape
    small = student_w.shape[1]
    rows, flipped = block_specs()
    weights = (down, student_w, pool_w, table, student_b)
    return pl.pallas_call(
        feed_down_kernel,
        grid=(length // BLOCK,),
        in_specs=[rows(wide), rows(active.shape[1])] + memory([pltpu.VMEM] * len(weights)),
        out_specs=[rows(wide), flipped(wide), rows(wide), rows(LANES), flipped(small), rows(3 * small)],
        out_shape=[
            struct((length, wide)), struct((wide, length)), struct((length, wide)), struct((length, LANES), FLOAT),
            struct((small, length)), struct((length, 3 * small)),
        ],
        compiler_params=params_of(("arbitrary",)),
        cost_estimate=LIGHT,
        name="feed_down",
    )(first, active, *weights)


def student_kernel(
    label_ref, cotangent_ref, pool_ref, unit2_ref, rate2_ref, student_w_ref, pool_w_ref, dense_ref, class_ref,
    small_b_ref, table_ref,
    logits_ref, grad_pool_ref, grad_student_ref, residual_ref, residual_half_ref, dense_grad_ref, class_grad_ref,
    small_sums_ref, sums_ref,
):
    length, three = pool_ref.shape
    small = three // 3
    scale = (small // POOL_HEADS) ** (-0.5)
    head_of = lambda axis: lax.broadcasted_iota(jnp.int32, (small, small), axis) // (small // POOL_HEADS)
    same = jnp.where(head_of(0) == head_of(1), 1.0, 0.0).astype(FLOAT)
    top = lax.broadcasted_iota(jnp.int32, (8, small), 0) == 0
    query = pool_ref[0:8, 0:small].astype(FLOAT)[0:1, :]
    key = pool_ref[:, small : 2 * small].astype(FLOAT)
    value = pool_ref[:, 2 * small : 3 * small].astype(FLOAT)
    scores = precise(key * query, same, (1, 0)) * scale
    raised = jnp.exp(scores - scores.max(axis=0, keepdims=True))
    weights = raised / raised.sum(axis=0, keepdims=True)
    pooled = (weights * value).sum(axis=0, keepdims=True)
    spread = lambda vector: jnp.where(top, vector, 0.0)
    dense = dense_ref[...].astype(FLOAT)
    classes = class_ref[...].astype(FLOAT)
    before = precise(spread(pooled), dense, (1, 0)) + small_b_ref[1:2, :]
    summary = jnp.tanh(before[0:1, :])
    logits = (precise(spread(summary), classes, (1, 0)) + small_b_ref[2:3, :])[0:1, :]
    lane = lax.broadcasted_iota(jnp.int32, (1, small), 1)
    real = small_b_ref[3:4, :] > 0.5
    masked = jnp.where(real, logits, MASKED_SCORE)
    lifted = jnp.where(real, jnp.exp(masked - masked.max(axis=1, keepdims=True)), 0.0)
    grad_logits = lifted / lifted.sum(axis=1, keepdims=True) - jnp.where(lane == label_ref[0], 1.0, 0.0)
    logits_ref[...] = logits[:, 0 : logits_ref.shape[1]]
    class_grad_ref[...] = precise(spread(summary), spread(grad_logits), (0, 0))
    grad_summary = precise(spread(grad_logits), classes, (1, 1))[0:1, :]
    grad_before = grad_summary * (1.0 - summary * summary)
    dense_grad_ref[...] = precise(spread(pooled), spread(grad_before), (0, 0))
    grad_pooled = precise(spread(grad_before), dense, (1, 1))[0:1, :]
    grad_weights = precise(value * grad_pooled, same, (1, 0))
    inner = (weights * grad_weights).sum(axis=0, keepdims=True)
    grad_scores = weights * (grad_weights - inner)
    grad_query = (grad_scores * key).sum(axis=0, keepdims=True) * scale
    first = lax.broadcasted_iota(jnp.int32, (length, small), 0) == 0
    grad_pool_ref[:, 0:small] = jnp.where(first, grad_query, 0.0).astype(HALF)
    grad_pool_ref[:, small : 2 * small] = (grad_scores * query * scale).astype(HALF)
    grad_pool_ref[:, 2 * small : 3 * small] = (weights * grad_pooled).astype(HALF)
    grad_student = mult_rt(grad_pool_ref[...], pool_w_ref[...])
    which = lax.broadcasted_iota(jnp.int32, (8, small), 0)
    student_sum = grad_student.sum(axis=0, keepdims=True)
    small_sums_ref[...] = jnp.where(
        which == 0, student_sum, jnp.where(which == 1, grad_before, jnp.where(which == 2, grad_logits, 0.0))
    )
    grad_student_ref[...] = grad_student.astype(HALF)

    sums_ref[...] = jnp.zeros_like(sums_ref)

    def one_block(block, _):
        rows = pl.ds(pl.multiple_of(block * BLOCK, BLOCK), BLOCK)
        grad = cotangent_ref[rows, :].astype(FLOAT) + mult_rt(grad_student_ref[rows, :], student_w_ref[...])
        unit = unit2_ref[rows, :].astype(FLOAT)
        residual = normalise_backward(grad * table_ref[GAIN2 : GAIN2 + 1, :], unit, rate2_ref[rows, 0:1])
        residual_ref[rows, :] = residual
        residual_half_ref[rows, :] = residual.astype(HALF)
        sums_ref[0:1, :] += (grad * unit).sum(axis=0, keepdims=True)
        sums_ref[1:2, :] += grad.sum(axis=0, keepdims=True)
        sums_ref[2:3, :] += residual.sum(axis=0, keepdims=True)
        return 0

    lax.fori_loop(0, length // BLOCK, one_block, 0)


def student_pass(label, cotangent, pool, unit2, rate2, student_w, pool_w, dense, classes, small_b, table, count):
    length, wide = cotangent.shape
    small = student_w.shape[1]
    struct = jax.ShapeDtypeStruct
    args = (cotangent, pool, unit2, rate2, student_w, pool_w, dense, classes, small_b, table)
    return pl.pallas_call(
        student_kernel,
        in_specs=memory([pltpu.SMEM] + [pltpu.VMEM] * len(args)),
        out_specs=memory([pltpu.VMEM] * 9),
        out_shape=[
            struct((1, count), FLOAT), struct((length, 3 * small), HALF), struct((length, small), HALF),
            struct((length, wide), FLOAT), struct((length, wide), HALF), struct((small, small), FLOAT),
            struct((small, small), FLOAT), struct((8, small), FLOAT), struct((8, wide), FLOAT),
        ],
        compiler_params=params_of(None),
        cost_estimate=LIGHT,
        name="student",
    )(label, *args)


def back_kernel(
    half_ref, residual_ref, slope_ref, unit1_ref, rate1_ref, down_ref, up_ref, out_w_ref, table_ref,
    inner_ref, residual1_ref, one_ref, mixed_ref, sums_ref, up_sums_ref,
):
    wide = residual_ref.shape[1]

    @pl.when(pl.program_id(0) == 0)
    def _():
        sums_ref[...] = jnp.zeros_like(sums_ref)
        up_sums_ref[...] = jnp.zeros_like(up_sums_ref)

    total = residual_ref[...]
    for part in range(up_ref.shape[1] // wide):
        cols = slice(part * wide, (part + 1) * wide)
        grad = mult_rt(half_ref[...], down_ref[cols, :]) * slope_ref[:, cols].astype(FLOAT)
        up_sums_ref[0:1, cols] += grad.sum(axis=0, keepdims=True)
        grad = grad.astype(HALF)
        inner_ref[:, cols] = grad
        total = total + mult_rt(grad, up_ref[:, cols])
    unit = unit1_ref[...].astype(FLOAT)
    residual = normalise_backward(total * table_ref[GAIN1 : GAIN1 + 1, :], unit, rate1_ref[:, 0:1])
    residual1_ref[...] = residual
    one = residual.astype(HALF)
    one_ref[...] = one
    mixed_ref[...] = mult_rt(one, out_w_ref[...]).astype(HALF)
    sums_ref[0:1, :] += (total * unit).sum(axis=0, keepdims=True)
    sums_ref[1:2, :] += total.sum(axis=0, keepdims=True)
    sums_ref[2:3, :] += residual.sum(axis=0, keepdims=True)


def back(half, residual, slope, unit1, rate1, down, up, out_w, table):
    length, wide = residual.shape
    inner = up.shape[1]
    rows = lambda cols: pl.BlockSpec((BLOCK, cols), lambda i: (i, 0))
    struct = jax.ShapeDtypeStruct
    weights = (down, up, out_w, table)
    return pl.pallas_call(
        back_kernel,
        grid=(length // BLOCK,),
        in_specs=[rows(wide), rows(wide), rows(inner), rows(wide), rows(LANES)] + memory([pltpu.VMEM] * len(weights)),
        out_specs=[rows(inner), rows(wide), rows(wide), rows(wide), whole((8, wide)), whole((8, inner))],
        out_shape=[
            struct((length, inner), HALF), struct((length, wide), FLOAT), struct((length, wide), HALF),
            struct((length, wide), HALF), struct((8, wide), FLOAT), struct((8, inner), FLOAT),
        ],
        compiler_params=params_of(("arbitrary",)),
        cost_estimate=LIGHT,
        name="back",
    )(half, residual, slope, unit1, rate1, *weights)


def input_kernel(low_ref, high_ref, residual_ref, weight_ref, out_ref):
    wide = residual_ref.shape[1]
    half = low_ref.shape[2]
    total = residual_ref[...]
    for part in range(3):
        for side, ref in enumerate((low_ref, high_ref)):
            begin = part * wide + side * half
            total = total + mult_rt(ref[part], weight_ref[:, begin : begin + half])
    out_ref[...] = total


def input_pass(halves, residual, weight):
    length, wide = residual.shape
    return pl.pallas_call(
        input_kernel,
        grid=(length // BLOCK,),
        in_specs=[pl.BlockSpec((3, BLOCK, wide // 2), lambda i: (0, i, 0))] * 2
        + [pl.BlockSpec((BLOCK, wide), lambda i: (i, 0)), pl.BlockSpec(memory_space=pltpu.VMEM)],
        out_specs=pl.BlockSpec((BLOCK, wide), lambda i: (i, 0)),
        out_shape=jax.ShapeDtypeStruct((length, wide), FLOAT),
        compiler_params=params_of(("arbitrary",)),
        cost_estimate=LIGHT,
        name="input_pass",
    )(*halves, residual, weight)


def swap(value, axis, bits):
    size = lax.axis_size(axis)
    return lax.ppermute(value, axis, [(i, i ^ bits) for i in range(size)])


def around(value):
    return [value] + [swap(value, "replica", bits) for bits in (2, 4, 6)]


WIDE = 384
SMALL = (0, 128)
SMALL_ROWS = 16
VECTOR_ROWS = 32


def rows_of(mat):
    return SMALL_ROWS if mat == SMALL else mat[0] * mat[1] // 4


def all_rows(mats):
    return sum(rows_of(mat) for mat in mats)


def after(value, *others):
    return lax.optimization_barrier((value,) + others)[0]


def vmem_call(kernel, name, where, inputs, outs, moved, scratch=()):
    return pl.pallas_call(
        kernel,
        in_specs=memory([pltpu.SMEM] + [pltpu.VMEM] * len(inputs)),
        out_specs=memory([pltpu.VMEM] * len(outs)),
        out_shape=outs,
        scratch_shapes=list(scratch),
        compiler_params=params_of(None),
        cost_estimate=LIGHT,
        name=name,
    )(where, *inputs)


def struct(shape, kind=HALF):
    return jax.ShapeDtypeStruct(shape, kind)


def aligned(begin, rows):
    return pl.ds(pl.multiple_of(begin, rows), rows)


def small_places(student_rows):
    third = student_rows // 3
    return third, third + 32


def fold_small(block_ref, base, student_ref, pool_ref, dense_ref, class_ref):
    third, last = small_places(student_ref.shape[0])
    for part in range(3):
        block_ref[base : base + third, part * LANES : (part + 1) * LANES] = student_ref[part * third : (part + 1) * third, :]
    block_ref[base + third : base + last, :] = pool_ref[...]
    rest = slice(base + last, base + 128)
    block_ref[rest, :] = jnp.zeros((128 - last, WIDE), block_ref.dtype)
    block_ref[rest, 0:LANES] = dense_ref[...]
    block_ref[rest, LANES : LANES + class_ref.shape[1]] = class_ref[...]


def unfold_small(block_ref, shard, student_ref, pool_ref, dense_ref, class_ref, rows):
    third, last = small_places(rows)
    base, short = shard * 128, 128 - last
    for part in range(3):
        begin = shard * rows + part * third
        student_ref[begin : begin + third, :] = block_ref[base : base + third, part * LANES : (part + 1) * LANES].astype(student_ref.dtype)
    target = slice(shard * short, (shard + 1) * short)
    pool_ref[target, :] = block_ref[base + third : base + last, :].astype(pool_ref.dtype)
    dense_ref[target, :] = block_ref[base + last : base + 128, 0:LANES].astype(dense_ref.dtype)
    classes = class_ref.shape[1]
    class_ref[target, :] = block_ref[base + last : base + 128, LANES : LANES + classes].astype(class_ref.dtype)


def pack_kernel(place_ref, *refs, mats, lines):
    chip, core = place_ref[1], place_ref[2]
    piece_ref = refs[-1]
    offset = 0
    if lines:
        base = all_rows(mats)
        for half in range(2):
            piece_ref[base : base + 16, half * LANES : (half + 1) * LANES] = refs[-2][half * 16 : half * 16 + 16, :]
        piece_ref[base : base + 16, 2 * LANES :] = jnp.zeros((16, WIDE - 2 * LANES), HALF)
    for mat, ref in zip(mats, refs):
        if mat == SMALL:
            small_ref = refs[-2]
            fold_small(small_ref, 0, *refs[len(mats) - 1 : len(mats) + 3])
            piece_ref[offset : offset + SMALL_ROWS, :] = small_ref[aligned((chip * 2 + core) * SMALL_ROWS, SMALL_ROWS), :]
            continue
        rows = mat[1] // 4
        for chunk in range(mat[0]):
            lanes = aligned(chunk * 2 * WIDE + core * WIDE, WIDE)
            piece_ref[offset : offset + rows, :] = ref[aligned(chip * rows, rows), lanes]
            offset += rows


def pack(where, shards, mats, lines=None):
    outs = [struct((all_rows(mats) + (0 if lines is None else 16), WIDE))]
    shards = list(shards) + ([] if lines is None else [lines])
    if SMALL in mats:
        outs = [struct(SMALL[1:] + (WIDE,))] + outs
    return vmem_call(partial(pack_kernel, mats=mats, lines=lines is not None), "pack", where, shards, outs, 2 * sum(s.size for s in shards))


def put_piece(out_ref, ref, step, offset, base, mat, chip, core):
    if mat == SMALL:
        target = aligned(base + (chip * 2 + core) * SMALL_ROWS, SMALL_ROWS)
        out_ref[target, :] = ref[step, offset : offset + SMALL_ROWS, :].astype(out_ref.dtype)
        return
    rows = mat[1] // 4
    for chunk in range(mat[0]):
        lanes = aligned(chunk * 2 * WIDE + core * WIDE, WIDE)
        first = offset + chunk * rows
        out_ref[aligned(base + chip * rows, rows), lanes] = ref[step, first : first + rows, :].astype(out_ref.dtype)


def place_kernel(place_ref, *refs, mats, rows):
    shard, chip, core = place_ref[0], place_ref[1], place_ref[2]
    count = len(mats)
    pieces, owns, outs = refs[:8], refs[8 : 8 + count], list(refs[8 + count :])
    if SMALL in mats:
        block_ref = outs.pop()
        smalls, outs = outs[count - 1 :], outs[: count - 1] + [block_ref]
    offset = 0
    for mat, own_ref, out_ref in zip(mats, owns, outs):
        height = mat[1]
        out_ref[aligned(shard * height, height), :] = own_ref[...]
        for number, ref in enumerate(pieces):
            far, other = number // 2, number % 2
            for step in range(ref.shape[0]):
                base = (shard ^ (step + 1)) * height
                put_piece(out_ref, ref, step, offset, base, mat, chip ^ far, core ^ other)
        offset += rows_of(mat)
    if SMALL in mats:
        for step in range(pieces[0].shape[0] + 1):
            unfold_small(block_ref, step, *smalls, rows)


def place(where, pieces, owns, outs, mats, rows=0):
    shards = pieces[0].shape[0] + 1
    scratch = [pltpu.VMEM((shards * SMALL[1], WIDE), HALF)] if SMALL in mats else []
    moved = 4 * shards * sum(own.size for own in owns)
    return vmem_call(partial(place_kernel, mats=mats, rows=rows), "place", where, pieces + list(owns), outs, moved, scratch)


def table_kernel(place_ref, *refs, classes, base):
    *lines, table_ref, up_ref, short_ref = refs
    shard = place_ref[0]
    wide, inner = table_ref.shape[1], up_ref.shape[1]
    shards = len(lines)
    ups = inner // shards // LANES
    table = jnp.zeros(table_ref.shape, FLOAT)
    shorts = jnp.zeros((8, LANES), FLOAT)
    for step, ref in enumerate(lines):
        target = shard ^ step
        if step == 0:
            block = ref[...].astype(FLOAT)
        else:
            block = jnp.concatenate([ref[base : base + 16, half * LANES : half * LANES + LANES] for half in range(2)], axis=0)
            block = block.astype(FLOAT)
        both = jnp.concatenate([block[0:8], block[8:16], jnp.zeros((8, wide - 2 * LANES), FLOAT)], axis=1)
        table = table + pltpu.roll(both, target * (wide // shards), 1)
        for line in range(ups):
            row = block[16 + line : 17 + line]
            up_ref[:, aligned(target * (inner // shards) + line * LANES, LANES)] = jnp.broadcast_to(row, (8, LANES))
        shorts = shorts + pltpu.roll(block[16 : 24], target * (LANES // shards), 1)
    table_ref[...] = table
    lane = lax.broadcasted_iota(jnp.int32, (1, LANES), 1)
    short_ref[0:2, :] = shorts[6:8]
    short_ref[2:3, :] = lines[0][...].astype(FLOAT)[24:25]
    short_ref[3:4, :] = jnp.where(lane < classes, 1.0, 0.0)
    short_ref[4:8, :] = jnp.zeros((4, LANES), FLOAT)


def lines_kernel(place_ref, *refs):
    *vectors, up_ref, student_ref, dense_ref, class_ref, out_ref, full_ref = refs
    full_ref[...] = jnp.zeros_like(full_ref)

    def put(row, value):
        full_ref[row : row + 1, 0 : value.shape[0]] = value.astype(FLOAT).reshape(1, value.shape[0])

    for line, ref in enumerate(vectors):
        put(line, ref[0:LANES])
        put(8 + line, ref[LANES:])
    for line in range(up_ref.shape[0] // LANES):
        put(16 + line, up_ref[line * LANES : (line + 1) * LANES])
    put(22, student_ref[...])
    put(23, dense_ref[...])
    put(24, class_ref[...])
    out_ref[...] = full_ref[...].astype(HALF)


def vector_lines(where, vectors, up_bias, shorts, class_bias):
    inputs = [*vectors, up_bias, *shorts, class_bias]
    (lines,) = vmem_call(lines_kernel, "lines", where, inputs, [struct((32, LANES))], 0, [pltpu.VMEM((32, LANES), FLOAT)])
    return lines


def from_shards(value):
    return [swap(value, "shard", bits) for bits in range(1, lax.axis_size("shard"))]


def both_cores(values):
    return [piece for value in values for piece in (value, swap(value, "replica", 1))]


def weight_grad_kernel(place_ref, left_ref, *refs):
    *rights, send_ref, keep_ref = refs
    core = place_ref[2]
    left = left_ref[...]
    if len(rights) == 2:
        for side, right_ref in enumerate(rights):
            for chunk in range(send_ref.shape[0]):
                value = mult(left, right_ref[chunk]).astype(HALF)

                @pl.when(core == side)
                def _():
                    keep_ref[chunk] = value

                @pl.when(core != side)
                def _():
                    send_ref[chunk] = value

        return
    for chunk in range(send_ref.shape[0]):
        for ref, which in ((send_ref, 1 - core), (keep_ref, core)):
            lanes = aligned(chunk * 2 * WIDE + which * WIDE, WIDE)
            ref[chunk] = mult(left, rights[0][:, lanes]).astype(HALF)


def weight_grad(where, left, rights, name):
    height, length = left.shape
    chunks = rights[0].shape[0] if len(rights) == 2 else rights[0].shape[1] // (2 * WIDE)
    block = 256
    out = struct((chunks, height, WIDE))
    return pl.pallas_call(
        weight_grad_kernel,
        grid=(height // block,),
        in_specs=[pl.BlockSpec(memory_space=pltpu.SMEM), pl.BlockSpec((block, length), lambda i: (i, 0))]
        + memory([pltpu.VMEM] * len(rights)),
        out_specs=[pl.BlockSpec((chunks, block, WIDE), lambda i: (0, i, 0))] * 2,
        out_shape=[out, out],
        compiler_params=params_of(("arbitrary",)),
        cost_estimate=LIGHT,
        name=name,
    )(where, left, *rights)


def small_grad_kernel(place_ref, hidden_ref, grad_student_ref, student_ref, grad_pool_ref, dense_ref, class_ref, send_ref, keep_ref, block_ref, first_ref, pool_ref):
    core = place_ref[2]
    shards = send_ref.shape[1] // (4 * SMALL_ROWS)
    first_ref[...] = mult(hidden_ref[...], grad_student_ref[...])
    pool_ref[...] = mult(student_ref[...], grad_pool_ref[...])
    part = lambda ref, shard: ref.at[pl.ds(shard * (ref.shape[0] // shards), ref.shape[0] // shards)]
    for shard in range(shards):
        fold_small(block_ref, shard * 128, *(part(ref, shard) for ref in (first_ref, pool_ref, dense_ref, class_ref)))
    for shard in range(shards):
        for chip in range(4):
            target = pl.ds((shard * 4 + chip) * SMALL_ROWS, SMALL_ROWS)
            for ref, which in ((send_ref, 1 - core), (keep_ref, core)):
                ref[0, target, :] = block_ref[aligned(shard * 128 + (chip * 2 + which) * SMALL_ROWS, SMALL_ROWS), :].astype(HALF)


def small_grad(where, hidden, grad_student, student, grad_pool, dense, classes, shards):
    outs = [struct((1, shards * 4 * SMALL_ROWS, WIDE))] * 2
    scratch = [
        pltpu.VMEM((shards * 128, WIDE), FLOAT), pltpu.VMEM((hidden.shape[0], LANES), FLOAT), pltpu.VMEM((LANES, WIDE), FLOAT)
    ]
    inputs = [hidden, grad_student, student, grad_pool, dense, classes]
    return vmem_call(small_grad_kernel, "small_grad", where, inputs, outs, 4 * hidden.size, scratch)


def vector_kernel(place_ref, low_ref, high_ref, one_ref, two_ref, up_ref, short_ref, half_ref, out_ref):
    half = low_ref.shape[1]
    for side, ref in enumerate((low_ref, high_ref)):
        lanes = slice(side * half, (side + 1) * half)
        lines = [ref[0:1, :], ref[1:2, :], one_ref[2:3, lanes], one_ref[0:1, lanes], one_ref[1:2, lanes]]
        lines += [two_ref[2:3, lanes], two_ref[0:1, lanes], two_ref[1:2, lanes]]
        for row, line in enumerate(lines):
            out_ref[side * 8 + row : side * 8 + row + 1, :] = line
    for row in range(up_ref.shape[1] // WIDE):
        out_ref[16 + row : 17 + row, :] = up_ref[0:1, row * WIDE : (row + 1) * WIDE]
    out_ref[24:32, :] = jnp.zeros((8, WIDE), FLOAT)
    for part in range(3):
        out_ref[24:25, part * LANES : (part + 1) * LANES] = short_ref[part : part + 1, :]
    half_ref[...] = out_ref[...].astype(HALF)


def split_kernel(place_ref, *refs, count, shards, vectors):
    chip = place_ref[1]
    keeps, recvs, outs = refs[:count], refs[count : 2 * count], refs[-4:]
    total = sum(keep.shape[0] * keep.shape[1] for keep in keeps) // (4 * shards)
    offset = 0
    for keep_ref, recv_ref in zip(keeps, recvs):
        height = keep_ref.shape[1] // shards
        rows = height // 4
        for chunk in range(keep_ref.shape[0]):
            for shard in range(shards):
                for far, out_ref in enumerate(outs):
                    source = aligned(shard * height + (chip ^ far) * rows, rows)
                    value = keep_ref[chunk, source, :].astype(FLOAT) + recv_ref[chunk, source, :].astype(FLOAT)
                    first = shard * total + offset
                    out_ref[first : first + rows, :] = value.astype(HALF)
            offset += rows
    if vectors:
        value = (refs[2 * count][...].astype(FLOAT) + refs[2 * count + 1][...].astype(FLOAT)).astype(HALF)
        for out_ref in outs:
            out_ref[shards * total : shards * total + VECTOR_ROWS, :] = value


def split(where, keeps, recvs, shards, vectors=()):
    total = sum(keep.shape[0] * keep.shape[1] for keep in keeps) // 4 + (VECTOR_ROWS if vectors else 0)
    kernel = partial(split_kernel, count=len(keeps), shards=shards, vectors=bool(vectors))
    inputs = list(keeps) + list(recvs) + list(vectors)
    return vmem_call(kernel, "split", where, inputs, [struct((total, WIDE))] * 4, 20 * total * WIDE)


def merge_kernel(place_ref, *refs, shards, vectors):
    shard = place_ref[0]
    parts, outs = refs[: -shards], refs[-shards:]
    offset = 0
    for group in range(len(parts) // 4):
        four = parts[4 * group : 4 * group + 4]
        last = vectors and group == len(parts) // 4 - 1
        rows = (four[0].shape[0] - (VECTOR_ROWS if last else 0)) // shards

        def total(source):
            a, b, c, d = (ref[source, :].astype(FLOAT) for ref in four)
            return ((a + b) + (c + d)).astype(HALF)

        for step, out_ref in enumerate(outs):
            out_ref[offset : offset + rows, :] = total(aligned((shard ^ step) * rows, rows))
        offset += rows
        if last:
            value = total(slice(shards * rows, shards * rows + VECTOR_ROWS))
            for out_ref in outs:
                out_ref[offset : offset + VECTOR_ROWS, :] = value


def merge(where, groups, shards, vectors=False):
    extra = VECTOR_ROWS if vectors else 0
    rows = (sum(four[0].shape[0] for four in groups) - extra) // shards + extra
    kernel = partial(merge_kernel, shards=shards, vectors=vectors)
    inputs = [part for four in groups for part in four]
    return vmem_call(kernel, "merge", where, inputs, [struct((rows, WIDE))] * shards, 10 * shards * rows * WIDE)


def total_kernel(place_ref, *refs, shards):
    parts, outs = refs[:shards], refs[shards:]
    offset = 0
    for out_ref in outs:
        rows = slice(offset, offset + out_ref.shape[0])
        terms = [ref[rows, :].astype(FLOAT) for ref in parts]
        while len(terms) > 1:
            half = len(terms) // 2
            terms = [terms[i] + terms[i + half] for i in range(half)]
        out_ref[...] = terms[0].astype(HALF)
        offset += out_ref.shape[0]


def total(where, parts, vectors=False):
    rows = parts[0].shape[0] - (VECTOR_ROWS if vectors else 0)
    outs = [struct((rows, WIDE))] + ([struct((VECTOR_ROWS, WIDE))] if vectors else [])
    outs = vmem_call(partial(total_kernel, shards=len(parts)), "total", where, parts, outs, 10 * rows * WIDE)
    bits = 8
    while bits < lax.axis_size("replica"):
        outs = [(v.astype(FLOAT) + swap(v, "replica", bits).astype(FLOAT)).astype(HALF) for v in outs]
        bits *= 2
    return outs


def finish_kernel(place_ref, *refs, mats, rows):
    chip, core = place_ref[1], place_ref[2]
    pieces, outs = refs[:8], list(refs[8:])
    if SMALL in mats:
        block_ref = outs.pop()
        smalls, outs = outs[len(mats) - 1 :], outs[: len(mats) - 1] + [block_ref]
    offset = 0
    for mat, out_ref in zip(mats, outs):
        for number, ref in enumerate(pieces):
            put_piece(out_ref, ref, 0, offset, 0, mat, chip ^ (number // 2), core ^ (number % 2))
        offset += rows_of(mat)
    if SMALL in mats:
        unfold_small(block_ref, 0, *smalls, rows)


def finish(where, pieces, mats, outs, rows=0):
    pieces = [piece[None] for piece in pieces]
    scratch = [pltpu.VMEM(SMALL[1:] + (WIDE,), FLOAT)] if SMALL in mats else []
    moved = 6 * sum(out.size for out in outs)
    return vmem_call(partial(finish_kernel, mats=mats, rows=rows), "finish", where, pieces, outs, moved, scratch)


def vector_out_kernel(place_ref, total_ref, *refs):
    tables, up_ref, shorts, class_ref = refs[:8], refs[8], refs[9:11], refs[11]
    shard = place_ref[0]
    wide = 2 * WIDE
    each = tables[0].shape[0]
    shards = wide // each
    values = total_ref[...].astype(FLOAT)
    table = jnp.concatenate([values[0:8], values[8:16]], axis=1)
    table = pltpu.roll(table, (shards - shard) * each, 1)[:, :each]
    for line, ref in enumerate(tables):
        ref[...] = table[line : line + 1].reshape(each)
    lines = up_ref.shape[0] // WIDE
    for line in range(lines):
        row = jnp.zeros((1, WIDE), FLOAT)
        for which in range(shards):
            row = row + jnp.where(shard == which, values[16 + which * lines + line : 17 + which * lines + line], 0.0)
        up_ref[line * WIDE : (line + 1) * WIDE] = row.reshape(WIDE)
    each = shorts[0].shape[0]
    for part, ref in enumerate(shorts):
        row = pltpu.roll(values[24:32, part * LANES : (part + 1) * LANES], (shards - shard) * each, 1)
        ref[...] = row[0:1, :each].reshape(each)
    class_ref[...] = values[24:25, 2 * LANES : 2 * LANES + class_ref.shape[0]].reshape(class_ref.shape[0])


def vector_out(where, value, shards, inner, classes):
    outs = [struct((2 * WIDE // shards,), FLOAT)] * 8 + [struct((inner // shards,), FLOAT)]
    outs += [struct((LANES // shards,), FLOAT)] * 2 + [struct((classes,), FLOAT)]
    return vmem_call(vector_out_kernel, "vector_out", where, [value], outs, 4 * value.size)


def body(
    tokens, cotangent, piece_starts, labels, qkv_weight, query_bias, value_bias, out_weight, out_bias, attention_gain,
    attention_shift, up_weight, up_bias, down_weight, down_bias, feed_gain, feed_shift, student_weight, student_bias,
    pool_weight, dense_weight, dense_bias, class_weight, class_bias,
):
    count, length, wide = tokens.shape
    inner = up_weight.shape[1]
    classes = class_weight.shape[1]
    student_rows = student_weight.shape[0]
    shards = lax.axis_size("shard")
    replica = lax.axis_index("replica")
    where = jnp.stack([lax.axis_index("shard"), (replica >> 1) & 3, replica & 1]).astype(jnp.int32)
    tokens, cotangent = tokens.reshape(length, wide), cotangent.reshape(length, wide)
    qkv_mats = ((3, qkv_weight.shape[0]),)
    up_mats = ((1, out_weight.shape[0]), (4, up_weight.shape[0]))
    down_mats = ((1, down_weight.shape[0]), SMALL)

    (piece,) = pack(where, [qkv_weight], qkv_mats)
    near = from_shards(piece)
    lines = vector_lines(
        where,
        [query_bias, value_bias, out_bias, attention_gain, attention_shift, down_bias, feed_gain, feed_shift],
        up_bias, [student_bias, dense_bias], class_bias,
    )
    near_stack = jnp.stack(near)
    qkv_around = around(near_stack)
    (up_piece,) = pack(where, [after(out_weight, *qkv_around[1:]), up_weight], up_mats, lines)
    up_near = from_shards(up_piece)
    tokens_t = flip(after(tokens, up_piece))
    qkv_pieces = both_cores(qkv_around)
    (qkv,) = place(where, qkv_pieces, [qkv_weight], [struct((shards * qkv_weight.shape[0], 3 * wide))], qkv_mats)
    up_near[0] = after(up_near[0], qkv, tokens_t)
    table, up_b, small_b = vmem_call(
        partial(table_kernel, classes=classes, base=all_rows(up_mats)), "table", where, [lines] + up_near,
        [struct((8, wide), FLOAT), struct((8, inner), FLOAT), struct((8, LANES), FLOAT)], 8 * 8 * inner,
    )
    up_stack = jnp.stack(up_near)
    small, down_piece = pack(
        where, [after(down_weight, up_stack), student_weight, pool_weight, dense_weight, class_weight], down_mats
    )
    up_around = around(up_stack)
    down_near = [swap(down_piece, "shard", bits) for bits in range(1, shards - 1)]
    qkv = after(qkv, up_stack, tokens_t, down_piece)
    joined = project(tokens, qkv, table)
    joined, down_piece, up_around[1] = lax.optimization_barrier((joined, down_piece, up_around[1]))
    down_near.append(swap(down_piece, "shard", shards - 1))
    mixed, mixed_t, lse = attend_forward(joined, piece_starts)
    whole_of = lambda shard: struct((shards * shard.shape[0], shard.shape[1]))
    mixed, *arrived = lax.optimization_barrier((mixed, *down_near, *up_around))
    down_near, up_around = arrived[: shards - 1], arrived[shards - 1 :]
    down_stack = jnp.stack(down_near)
    down_around = around(after(down_stack, mixed))
    out_w, up = place(
        where, both_cores(up_around), [out_weight, up_weight], [whole_of(out_weight), whole_of(up_weight)], up_mats
    )

    first, first_t, active, active_t, slope, unit1, rate1 = feed_up(
        mixed, tokens, after(out_w, down_stack), up, table, up_b
    )
    rest = [whole_of(s) for s in (down_weight, student_weight, pool_weight, dense_weight)]
    rest.append(struct((shards * class_weight.shape[0], LANES)))
    active, *down_around = lax.optimization_barrier((active, *down_around))
    down, student_w, pool_w, dense_w, class_w = place(
        where, both_cores(down_around), [down_weight, small], rest, down_mats, student_rows
    )
    hidden, hidden_t, unit2, rate2, student_t, pool = feed_down(
        first, active, down, student_w, pool_w, table, small_b
    )
    logits, grad_pool, grad_student, residual2, half2, grad_dense, grad_class, small_sums, sums2 = student_pass(
        labels, cotangent, pool, unit2, rate2, student_w, pool_w, dense_w, class_w, small_b, table, classes
    )
    core_swap = lambda value: swap(value, "replica", 1)
    exchange = lambda parts: [parts[0]] + [swap(part, "replica", 2 * far) for far, part in enumerate(parts) if far > 0]
    spread = lambda parts: [parts[0]] + [swap(part, "shard", far) for far, part in enumerate(parts) if far > 0]
    send_down, keep_down = weight_grad(where, active_t, [half2], "grad_down")
    send_small, keep_small = small_grad(
        where, after(hidden_t, send_down), grad_student, student_t, grad_pool, grad_dense, grad_class, shards
    )
    parts_a = split(where, [keep_down], [core_swap(send_down)], shards)
    exchanged_a = exchange(parts_a)
    grad_inner, residual1, half1, grad_mixed, sums1, up_sums = back(
        after(half2, parts_a[0], keep_small), residual2, slope, unit1, rate1, down, up, out_w, table
    )
    send_up, keep_up = weight_grad(where, first_t, [grad_inner], "grad_up")
    swapped_small = core_swap(send_small)
    send_up, mixed_t, swapped_small, *exchanged_a = lax.optimization_barrier((send_up, mixed_t, swapped_small, *exchanged_a))
    send_out, keep_out = weight_grad(where, mixed_t, [half1], "grad_out")
    parts_b = split(where, [keep_out, keep_up], [core_swap(send_out), core_swap(send_up)], shards)
    exchanged_b = exchange(parts_b)
    low, low_sums = attend_backward(joined, piece_starts, mixed, after(grad_mixed, parts_b[0]), lse, 0, 2)
    high, high_sums = attend_backward(joined, piece_starts, mixed, after(grad_mixed, low), lse, 1, 2)
    high, *exchanged_b = lax.optimization_barrier((high, *exchanged_b))
    ready = merge(where, [exchanged_b, exchanged_a], shards)
    near_ab = spread(ready)
    send_qkv, keep_qkv = weight_grad(where, after(tokens_t, ready[0]), [low, high], "grad_qkv")
    (vectors,) = vmem_call(
        vector_kernel, "vectors", where,
        [low_sums, high_sums, sums1, sums2, up_sums, small_sums], [struct((VECTOR_ROWS, WIDE))], 4 * VECTOR_ROWS * WIDE,
        [pltpu.VMEM((VECTOR_ROWS, WIDE), FLOAT)],
    )
    parts_c = split(
        where, [keep_qkv, keep_small], [core_swap(send_qkv), swapped_small], shards, (vectors, core_swap(vectors))
    )
    exchanged_c = exchange(parts_c)
    input_grad = input_pass((after(low, parts_c[0]), high), residual1, qkv)
    near_ab[0] = after(near_ab[0], input_grad)
    (piece_ab,) = total(where, near_ab)
    piece_ab, *exchanged_c = lax.optimization_barrier((piece_ab, *exchanged_c))
    ready = merge(where, [exchanged_c], shards, True)
    near_c = spread(ready)
    around_ab = around(after(piece_ab, ready[0]))
    near_c[0], *around_ab = lax.optimization_barrier((near_c[0], *around_ab))
    pieces_ab = both_cores(around_ab)
    piece_c, vectors = total(where, near_c, True)
    pieces_c = both_cores(around(piece_c))
    full = lambda shard: struct(shard.shape, FLOAT)
    ab_mats = up_mats + down_mats[:1]
    grad_out, grad_up, grad_down = finish(
        where, pieces_ab, ab_mats, [full(s) for s in (out_weight, up_weight, down_weight)]
    )
    *g_table, g_up_b, g_student_b, g_dense_b, g_class_b = vector_out(where, vectors, shards, inner, classes)
    grad_qkv, g_student, g_pool, g_dense, g_class = finish(
        where, pieces_c, qkv_mats + (SMALL,),
        [full(s) for s in (qkv_weight, student_weight, pool_weight, dense_weight, class_weight)], student_rows,
    )
    return (
        hidden.reshape(count, length, wide), logits, input_grad.reshape(count, length, wide),
        grad_qkv, g_table[0], g_table[1], grad_out, g_table[2], g_table[3], g_table[4], grad_up, g_up_b, grad_down,
        g_table[5], g_table[6], g_table[7], g_student, g_student_b, g_pool, g_dense, g_dense_b, g_class, g_class_b,
    )


def solution(mesh):
    placed = (
        P(("shard", "replica"), None, None),
        P(("shard", "replica"), None, None),
        P(("shard", "replica"), None),
        P(("shard", "replica")),
        P("shard", None),
        P("shard"),
        P("shard"),
        P("shard", None),
        P("shard"),
        P("shard"),
        P("shard"),
        P("shard", None),
        P("shard"),
        P("shard", None),
        P("shard"),
        P("shard"),
        P("shard"),
        P("shard", None),
        P("shard"),
        P("shard", None),
        P("shard", None),
        P("shard"),
        P("shard", None),
        P(),
    )
    return jax.shard_map(
        body,
        mesh=mesh,
        in_specs=placed,
        out_specs=(
            P(("shard", "replica"), None, None),
            P(("shard", "replica"), None),
            P(("shard", "replica"), None, None),
            P("shard", None),
            P("shard"),
            P("shard"),
            P("shard", None),
            P("shard"),
            P("shard"),
            P("shard"),
            P("shard", None),
            P("shard"),
            P("shard", None),
            P("shard"),
            P("shard"),
            P("shard"),
            P("shard", None),
            P("shard"),
            P("shard", None),
            P("shard", None),
            P("shard"),
            P("shard", None),
            P(),
        ),
        check_vma=False,
    )
```

```python
from functools import partial

import jax
import jax.numpy as jnp
from jax import lax
from jax.experimental import pallas as pl
from jax.experimental.pallas import tpu as pltpu
from jax.sharding import PartitionSpec as P

HEADS = 12
POOL_HEADS = 2
PIECE = 256
NORM_EPS = 1e-06
MASKED_SCORE = -1e30
FLOAT = jnp.float32
HALF = jnp.bfloat16
PRECISE = lax.Precision.HIGHEST
LANES = 128
BLOCK = 256

ERF_SLOPE = 0.42
ERF_TERMS = (
    0.23691840576326206,
    0.2382680869907842,
    0.20182398814655725,
    0.2493386597508521,
    -0.10108083678814953,
    0.4156989047782712,
    -0.3092846516362072,
    0.06831743518928779,
)


LIGHT = pl.CostEstimate(flops=100000, transcendentals=0, bytes_accessed=100000)


def params_of(kinds, limit=44 << 20):
    return pltpu.CompilerParams(dimension_semantics=kinds, vmem_limit_bytes=limit)


def whole(shape, space=None):
    return pl.BlockSpec(shape, lambda *_: (0,) * len(shape))


def memory(kinds):
    return [pl.BlockSpec(memory_space=kind) for kind in kinds]


def mult(left, right):
    return jnp.dot(left, right, preferred_element_type=FLOAT)


def mult_rt(left, right):
    return lax.dot_general(left, right, (((1,), (1,)), ((), ())), preferred_element_type=FLOAT)


def mult_lt(left, right):
    return lax.dot_general(left, right, (((0,), (0,)), ((), ())), preferred_element_type=FLOAT)


def precise(left, right, dims):
    return lax.dot_general(
        left, right, ((dims[:1], dims[1:]), ((), ())), precision=PRECISE, preferred_element_type=FLOAT
    )


def key_extent(block, length):
    return min(length, (block + 2) * BLOCK)


def allowed_block(starts_ref, first_row, first_col, shape, row_axis):
    rows = first_row + lax.broadcasted_iota(jnp.int32, shape, row_axis)
    cols = first_col + lax.broadcasted_iota(jnp.int32, shape, 1 - row_axis)
    allowed = cols <= rows
    for piece in range(starts_ref.shape[1]):
        start = starts_ref[0, piece]
        inside = (rows >= start) & (rows < start + PIECE) & (cols >= start) & (cols < start + PIECE)
        allowed = allowed | inside
    return allowed


def fill_bias(starts_ref, bias_ref, length, row_axis):
    for block in range(length // BLOCK):
        wide = key_extent(block, length) - block * BLOCK
        shape = (BLOCK, wide) if row_axis == 0 else (wide, BLOCK)
        allowed = allowed_block(starts_ref, block * BLOCK, block * BLOCK, shape, row_axis)
        bias = jnp.where(allowed, 0.0, MASKED_SCORE).astype(FLOAT)
        if row_axis == 0:
            bias_ref[block, :, 0:wide] = bias
        else:
            bias_ref[block, 0:wide, :] = bias


def half_lanes(value, half):
    lane = lax.broadcasted_iota(jnp.int32, value.shape, 1)
    keep = (lane < LANES // 2) if half == 0 else (lane >= LANES // 2)
    return jnp.where(keep, value, jnp.zeros_like(value))


def attend_forward_kernel(starts_ref, q_ref, k_ref, v_ref, mixed_ref, flipped_ref, lse_ref, bias_ref):
    length = q_ref.shape[0]
    scale = (LANES // 2) ** (-0.5)

    @pl.when(pl.program_id(0) == 0)
    def _():
        fill_bias(starts_ref, bias_ref, length, 0)

    values = [half_lanes(v_ref[...], half) for half in range(2)]
    lane = lax.broadcasted_iota(jnp.int32, (BLOCK, LANES), 1)
    for block in range(length // BLOCK):
        begin = block * BLOCK
        extent = key_extent(block, length)
        query = q_ref[begin : begin + BLOCK, :] * jnp.asarray(scale, HALF)
        outs = []
        logs = []
        for half in range(2):
            scores = mult_rt(half_lanes(query, half), k_ref[0:extent, :])
            edge = scores[:, begin:extent] + bias_ref[block, :, 0 : extent - begin]
            parts = [edge] if begin == 0 else [scores[:, 0:begin], edge]
            ceiling = parts[0].max(axis=1, keepdims=True)
            for part in parts[1:]:
                ceiling = jnp.maximum(ceiling, part.max(axis=1, keepdims=True))
            total = 0.0
            mixed = 0.0
            place = 0
            for part in parts:
                raised = jnp.exp(part - ceiling)
                total = total + raised.sum(axis=1, keepdims=True)
                mixed = mixed + mult(
                    raised.astype(HALF), values[half][place : place + part.shape[1], :]
                )
                place += part.shape[1]
            outs.append(mixed / total)
            logs.append(ceiling + jnp.log(total))
        rounded = (outs[0] + outs[1]).astype(HALF)
        mixed_ref[begin : begin + BLOCK, :] = rounded
        flipped_ref[:, begin : begin + BLOCK] = rounded.T
        both = jnp.where(lane == 0, logs[0], logs[1])
        lse_ref[:, begin : begin + BLOCK] = both.T[0:8, :]


def attend_forward(joined, starts):
    length, wide = joined.shape
    pairs = wide // 3 // LANES
    return pl.pallas_call(
        attend_forward_kernel,
        grid=(pairs,),
        in_specs=[
            pl.BlockSpec(memory_space=pltpu.SMEM),
            pl.BlockSpec((length, LANES), lambda h: (0, h)),
            pl.BlockSpec((length, LANES), lambda h: (0, pairs + h)),
            pl.BlockSpec((length, LANES), lambda h: (0, 2 * pairs + h)),
        ],
        out_specs=[
            pl.BlockSpec((length, LANES), lambda h: (0, h)),
            pl.BlockSpec((LANES, length), lambda h: (h, 0)),
            pl.BlockSpec((8, length), lambda h: (h, 0)),
        ],
        out_shape=[
            jax.ShapeDtypeStruct((length, wide // 3), HALF),
            jax.ShapeDtypeStruct((wide // 3, length), HALF),
            jax.ShapeDtypeStruct((pairs * 8, length), FLOAT),
        ],
        scratch_shapes=[pltpu.VMEM((length // BLOCK, BLOCK, 2 * BLOCK), FLOAT)],
        compiler_params=params_of(("arbitrary",)),
        cost_estimate=LIGHT,
        name="attend_forward",
    )(starts, joined, joined, joined)


def attend_backward_kernel(
    starts_ref, q_ref, k_ref, v_ref, mixed_ref, grad_ref, lse_ref, out_ref, sums_ref, bias_ref, dk_ref, dv_ref
):
    length = q_ref.shape[0]
    scale = (LANES // 2) ** (-0.5)

    @pl.when(pl.program_id(0) == 0)
    def _():
        fill_bias(starts_ref, bias_ref, length, 1)

    product = grad_ref[...].astype(FLOAT) * mixed_ref[...].astype(FLOAT)
    row = lax.broadcasted_iota(jnp.int32, (8, LANES), 0)
    col = lax.broadcasted_iota(jnp.int32, (8, LANES), 1)
    picks = jnp.where((col < LANES // 2) == (row == 0), 1.0, 0.0).astype(FLOAT)
    inner = precise(picks, product, (1, 1))
    keys = [half_lanes(k_ref[...] * jnp.asarray(scale, HALF), half) for half in range(2)]
    values = [half_lanes(v_ref[...], half) for half in range(2)]
    dk_ref[...] = jnp.zeros_like(dk_ref)
    dv_ref[...] = jnp.zeros_like(dv_ref)
    query_sum = jnp.zeros((1, LANES), FLOAT)
    for block in range(length // BLOCK):
        begin = block * BLOCK
        extent = key_extent(block, length)
        query = q_ref[begin : begin + BLOCK, :]
        grad = grad_ref[begin : begin + BLOCK, :]
        grad_query = 0.0
        for half in range(2):
            scores = mult_rt(keys[half][0:extent, :], query)
            grad_probs = mult_rt(values[half][0:extent, :], grad)
            lse = lse_ref[half : half + 1, begin : begin + BLOCK]
            base = inner[half : half + 1, begin : begin + BLOCK]
            edge = scores[begin:extent, :] + bias_ref[block, 0 : extent - begin, :]
            shifted = edge if begin == 0 else jnp.concatenate([scores[0:begin, :], edge], axis=0)
            probs = jnp.exp(shifted - lse)
            grad_scores = (probs * (grad_probs - base)).astype(HALF)
            grad_half = half_lanes(grad, half)
            query_half = half_lanes(query * jnp.asarray(scale, HALF), half)
            dv_ref[0:extent, :] += mult(probs.astype(HALF), grad_half)
            dk_ref[0:extent, :] += mult(grad_scores, query_half)
            grad_query = grad_query + mult_lt(grad_scores, keys[half][0:extent, :])
        rounded = grad_query.astype(HALF)
        out_ref[0, begin : begin + BLOCK, :] = rounded
        query_sum = query_sum + rounded.astype(FLOAT).sum(axis=0, keepdims=True)
    out_ref[1, :, :] = dk_ref[...].astype(HALF)
    value = dv_ref[...].astype(HALF)
    out_ref[2, :, :] = value
    value_sum = value.astype(FLOAT).sum(axis=0, keepdims=True)
    sums_ref[...] = jnp.where(row == 0, query_sum, value_sum)


def attend_backward(joined, starts, mixed, grad_mixed, lse):
    length, wide = joined.shape
    pairs = wide // 3 // LANES
    return pl.pallas_call(
        attend_backward_kernel,
        grid=(pairs,),
        in_specs=[
            pl.BlockSpec(memory_space=pltpu.SMEM),
            pl.BlockSpec((length, LANES), lambda h: (0, h)),
            pl.BlockSpec((length, LANES), lambda h: (0, pairs + h)),
            pl.BlockSpec((length, LANES), lambda h: (0, 2 * pairs + h)),
            pl.BlockSpec((length, LANES), lambda h: (0, h)),
            pl.BlockSpec((length, LANES), lambda h: (0, h)),
            pl.BlockSpec((8, length), lambda h: (h, 0)),
        ],
        out_specs=[
            pl.BlockSpec((3, length, LANES), lambda h: (0, 0, h)),
            pl.BlockSpec((8, LANES), lambda h: (0, h)),
        ],
        out_shape=[
            jax.ShapeDtypeStruct((3, length, wide // 3), HALF),
            jax.ShapeDtypeStruct((8, wide // 3), FLOAT),
        ],
        scratch_shapes=[
            pltpu.VMEM((length // BLOCK, 2 * BLOCK, BLOCK), FLOAT),
            pltpu.VMEM((length, LANES), FLOAT),
            pltpu.VMEM((length, LANES), FLOAT),
        ],
        compiler_params=params_of(("arbitrary",)),
        cost_estimate=LIGHT,
        name="attend_backward",
    )(starts, joined, joined, joined, mixed, grad_mixed, lse)


def normalise(values):
    middle = values.mean(axis=1, keepdims=True)
    centered = values - middle
    spread = (centered * centered).mean(axis=1, keepdims=True)
    rate = lax.rsqrt(spread + NORM_EPS)
    return centered * rate, rate


def normalise_backward(grad_unit, unit, rate):
    along = grad_unit.mean(axis=1, keepdims=True)
    across = (grad_unit * unit).mean(axis=1, keepdims=True)
    return rate * (grad_unit - along - unit * across)


def gelu_pair(inner):
    size = jnp.abs(inner)
    ratio = 1.0 / (1.0 + (ERF_SLOPE * 2.0**-0.5) * size)
    tail = jnp.full_like(ratio, 0.5 * ERF_TERMS[-1])
    for term in ERF_TERMS[-2::-1]:
        tail = tail * ratio + 0.5 * term
    bell = jnp.exp(-0.5 * inner * inner)
    tail = tail * ratio * bell
    below = jnp.where(inner < 0.0, tail, 1.0 - tail)
    return inner * below, below + inner * (bell * (2.0 * jnp.pi) ** -0.5)


QUERY_B, VALUE_B, OUT_B, GAIN1, SHIFT1, DOWN_B, GAIN2, SHIFT2 = range(8)


def flip_kernel(value_ref, out_ref):
    out_ref[...] = value_ref[...].T


def flip(value):
    return pl.pallas_call(
        flip_kernel,
        in_specs=memory([pltpu.VMEM]),
        out_specs=pl.BlockSpec(memory_space=pltpu.VMEM),
        out_shape=jax.ShapeDtypeStruct(value.shape[::-1], value.dtype),
        compiler_params=params_of(None, FULL),
        cost_estimate=LIGHT,
        name="flip",
    )(value)


def project_kernel(tokens_ref, weight_ref, table_ref, out_ref):
    wide = tokens_ref.shape[1]
    for part in range(3):
        value = mult(tokens_ref[...], weight_ref[:, part * wide : (part + 1) * wide])
        if part == 0:
            value = value + table_ref[QUERY_B : QUERY_B + 1, :]
        elif part == 2:
            value = value + table_ref[VALUE_B : VALUE_B + 1, :]
        out_ref[:, part * wide : (part + 1) * wide] = value.astype(HALF)


def project(tokens, weight, table):
    length, wide = tokens.shape
    return pl.pallas_call(
        project_kernel,
        grid=(length // BLOCK,),
        in_specs=[pl.BlockSpec((BLOCK, wide), lambda i: (i, 0))] + memory([pltpu.VMEM] * 2),
        out_specs=pl.BlockSpec((BLOCK, 3 * wide), lambda i: (i, 0)),
        out_shape=jax.ShapeDtypeStruct((length, 3 * wide), HALF),
        compiler_params=params_of(("arbitrary",)),
        cost_estimate=LIGHT,
        name="project",
    )(tokens, weight, table)


def feed_up_kernel(
    mixed_ref, tokens_ref, out_w_ref, up_ref, table_ref, up_b_ref,
    first_ref, first_t_ref, active_ref, active_t_ref, slope_ref, unit1_ref, rate1_ref,
):
    wide = tokens_ref.shape[1]
    line = lambda which: table_ref[which : which + 1, :]
    residual = tokens_ref[...].astype(FLOAT) + (mult(mixed_ref[...], out_w_ref[...]) + line(OUT_B))
    unit, rate = normalise(residual)
    unit1_ref[...] = unit.astype(HALF)
    rate1_ref[...] = jnp.broadcast_to(rate, rate1_ref.shape)
    first = unit * line(GAIN1) + line(SHIFT1)
    first_ref[...] = first
    first_half = first.astype(HALF)
    first_t_ref[...] = first_half.T
    for part in range(up_ref.shape[1] // wide):
        cols = slice(part * wide, (part + 1) * wide)
        inner = mult(first_half, up_ref[:, cols]) + up_b_ref[0:1, cols]
        active, slope = gelu_pair(inner)
        active = active.astype(HALF)
        active_ref[:, cols] = active
        active_t_ref[cols, :] = active.T
        slope_ref[:, cols] = slope.astype(HALF)


def block_specs():
    rows = lambda cols: pl.BlockSpec((BLOCK, cols), lambda i: (i, 0))
    flipped = lambda cols: pl.BlockSpec((cols, BLOCK), lambda i: (0, i))
    return rows, flipped


def feed_up(mixed, tokens, out_w, up, table, up_b):
    length, wide = tokens.shape
    inner = up.shape[1]
    rows, flipped = block_specs()
    weights = (out_w, up, table, up_b)
    return pl.pallas_call(
        feed_up_kernel,
        grid=(length // BLOCK,),
        in_specs=[rows(wide), rows(wide)] + memory([pltpu.VMEM] * len(weights)),
        out_specs=[rows(wide), flipped(wide), rows(inner), flipped(inner), rows(inner), rows(wide), rows(LANES)],
        out_shape=[
            struct((length, wide), FLOAT), struct((wide, length)), struct((length, inner)), struct((inner, length)),
            struct((length, inner)), struct((length, wide)), struct((length, LANES), FLOAT),
        ],
        compiler_params=params_of(("arbitrary",)),
        cost_estimate=LIGHT,
        name="feed_up",
    )(mixed, tokens, *weights)


def feed_down_kernel(
    first_ref, active_ref, down_ref, student_w_ref, pool_w_ref, table_ref, student_b_ref,
    hidden_ref, hidden_t_ref, unit2_ref, rate2_ref, student_t_ref, pool_ref,
):
    line = lambda which: table_ref[which : which + 1, :]
    total = first_ref[...] + line(DOWN_B) + mult(active_ref[...], down_ref[...])
    unit, rate = normalise(total)
    unit2_ref[...] = unit.astype(HALF)
    rate2_ref[...] = jnp.broadcast_to(rate, rate2_ref.shape)
    hidden = (unit * line(GAIN2) + line(SHIFT2)).astype(HALF)
    hidden_ref[...] = hidden
    hidden_t_ref[...] = hidden.T
    student = (mult(hidden, student_w_ref[...]) + student_b_ref[0:1, :]).astype(HALF)
    student_t_ref[...] = student.T
    pool_ref[...] = mult(student, pool_w_ref[...]).astype(HALF)


def feed_down(first, active, down, student_w, pool_w, table, student_b):
    length, wide = first.shape
    small = student_w.shape[1]
    rows, flipped = block_specs()
    weights = (down, student_w, pool_w, table, student_b)
    return pl.pallas_call(
        feed_down_kernel,
        grid=(length // BLOCK,),
        in_specs=[rows(wide), rows(active.shape[1])] + memory([pltpu.VMEM] * len(weights)),
        out_specs=[rows(wide), flipped(wide), rows(wide), rows(LANES), flipped(small), rows(3 * small)],
        out_shape=[
            struct((length, wide)), struct((wide, length)), struct((length, wide)), struct((length, LANES), FLOAT),
            struct((small, length)), struct((length, 3 * small)),
        ],
        compiler_params=params_of(("arbitrary",)),
        cost_estimate=LIGHT,
        name="feed_down",
    )(first, active, *weights)


def student_kernel(
    label_ref, cotangent_ref, pool_ref, unit2_ref, rate2_ref, student_w_ref, pool_w_ref, dense_ref, class_ref,
    small_b_ref, table_ref,
    logits_ref, grad_pool_ref, grad_student_ref, residual_ref, residual_half_ref, dense_grad_ref, class_grad_ref,
    small_sums_ref, sums_ref,
):
    length, three = pool_ref.shape
    small = three // 3
    scale = (small // POOL_HEADS) ** (-0.5)
    head_of = lambda axis: lax.broadcasted_iota(jnp.int32, (small, small), axis) // (small // POOL_HEADS)
    same = jnp.where(head_of(0) == head_of(1), 1.0, 0.0).astype(FLOAT)
    top = lax.broadcasted_iota(jnp.int32, (8, small), 0) == 0
    query = pool_ref[0:8, 0:small].astype(FLOAT)[0:1, :]
    key = pool_ref[:, small : 2 * small].astype(FLOAT)
    value = pool_ref[:, 2 * small : 3 * small].astype(FLOAT)
    scores = precise(key * query, same, (1, 0)) * scale
    raised = jnp.exp(scores - scores.max(axis=0, keepdims=True))
    weights = raised / raised.sum(axis=0, keepdims=True)
    pooled = (weights * value).sum(axis=0, keepdims=True)
    spread = lambda vector: jnp.where(top, vector, 0.0)
    dense = dense_ref[...].astype(FLOAT)
    classes = class_ref[...].astype(FLOAT)
    before = precise(spread(pooled), dense, (1, 0)) + small_b_ref[1:2, :]
    summary = jnp.tanh(before[0:1, :])
    logits = (precise(spread(summary), classes, (1, 0)) + small_b_ref[2:3, :])[0:1, :]
    lane = lax.broadcasted_iota(jnp.int32, (1, small), 1)
    real = small_b_ref[3:4, :] > 0.5
    masked = jnp.where(real, logits, MASKED_SCORE)
    lifted = jnp.where(real, jnp.exp(masked - masked.max(axis=1, keepdims=True)), 0.0)
    grad_logits = lifted / lifted.sum(axis=1, keepdims=True) - jnp.where(lane == label_ref[0], 1.0, 0.0)
    logits_ref[...] = logits[:, 0 : logits_ref.shape[1]]
    class_grad_ref[...] = precise(spread(summary), spread(grad_logits), (0, 0))
    grad_summary = precise(spread(grad_logits), classes, (1, 1))[0:1, :]
    grad_before = grad_summary * (1.0 - summary * summary)
    dense_grad_ref[...] = precise(spread(pooled), spread(grad_before), (0, 0))
    grad_pooled = precise(spread(grad_before), dense, (1, 1))[0:1, :]
    grad_weights = precise(value * grad_pooled, same, (1, 0))
    inner = (weights * grad_weights).sum(axis=0, keepdims=True)
    grad_scores = weights * (grad_weights - inner)
    grad_query = (grad_scores * key).sum(axis=0, keepdims=True) * scale
    first = lax.broadcasted_iota(jnp.int32, (length, small), 0) == 0
    grad_pool_ref[:, 0:small] = jnp.where(first, grad_query, 0.0).astype(HALF)
    grad_pool_ref[:, small : 2 * small] = (grad_scores * query * scale).astype(HALF)
    grad_pool_ref[:, 2 * small : 3 * small] = (weights * grad_pooled).astype(HALF)
    grad_student = mult_rt(grad_pool_ref[...], pool_w_ref[...])
    which = lax.broadcasted_iota(jnp.int32, (8, small), 0)
    student_sum = grad_student.sum(axis=0, keepdims=True)
    small_sums_ref[...] = jnp.where(
        which == 0, student_sum, jnp.where(which == 1, grad_before, jnp.where(which == 2, grad_logits, 0.0))
    )
    grad_student_ref[...] = grad_student.astype(HALF)

    sums_ref[...] = jnp.zeros_like(sums_ref)

    def one_block(block, _):
        rows = pl.ds(pl.multiple_of(block * BLOCK, BLOCK), BLOCK)
        grad = cotangent_ref[rows, :].astype(FLOAT) + mult_rt(grad_student_ref[rows, :], student_w_ref[...])
        unit = unit2_ref[rows, :].astype(FLOAT)
        residual = normalise_backward(grad * table_ref[GAIN2 : GAIN2 + 1, :], unit, rate2_ref[rows, 0:1])
        residual_ref[rows, :] = residual
        residual_half_ref[rows, :] = residual.astype(HALF)
        sums_ref[0:1, :] += (grad * unit).sum(axis=0, keepdims=True)
        sums_ref[1:2, :] += grad.sum(axis=0, keepdims=True)
        sums_ref[2:3, :] += residual.sum(axis=0, keepdims=True)
        return 0

    lax.fori_loop(0, length // BLOCK, one_block, 0)


def student_pass(label, cotangent, pool, unit2, rate2, student_w, pool_w, dense, classes, small_b, table, count):
    length, wide = cotangent.shape
    small = student_w.shape[1]
    struct = jax.ShapeDtypeStruct
    args = (cotangent, pool, unit2, rate2, student_w, pool_w, dense, classes, small_b, table)
    return pl.pallas_call(
        student_kernel,
        in_specs=memory([pltpu.SMEM] + [pltpu.VMEM] * len(args)),
        out_specs=memory([pltpu.VMEM] * 9),
        out_shape=[
            struct((1, count), FLOAT), struct((length, 3 * small), HALF), struct((length, small), HALF),
            struct((length, wide), FLOAT), struct((length, wide), HALF), struct((small, small), FLOAT),
            struct((small, small), FLOAT), struct((8, small), FLOAT), struct((8, wide), FLOAT),
        ],
        compiler_params=params_of(None),
        cost_estimate=LIGHT,
        name="student",
    )(label, *args)


def back_kernel(
    half_ref, residual_ref, slope_ref, unit1_ref, rate1_ref, down_ref, up_ref, out_w_ref, table_ref,
    inner_ref, residual1_ref, one_ref, mixed_ref, sums_ref, up_sums_ref,
):
    wide = residual_ref.shape[1]

    @pl.when(pl.program_id(0) == 0)
    def _():
        sums_ref[...] = jnp.zeros_like(sums_ref)
        up_sums_ref[...] = jnp.zeros_like(up_sums_ref)

    total = residual_ref[...]
    for part in range(up_ref.shape[1] // wide):
        cols = slice(part * wide, (part + 1) * wide)
        grad = mult_rt(half_ref[...], down_ref[cols, :]) * slope_ref[:, cols].astype(FLOAT)
        up_sums_ref[0:1, cols] += grad.sum(axis=0, keepdims=True)
        grad = grad.astype(HALF)
        inner_ref[:, cols] = grad
        total = total + mult_rt(grad, up_ref[:, cols])
    unit = unit1_ref[...].astype(FLOAT)
    residual = normalise_backward(total * table_ref[GAIN1 : GAIN1 + 1, :], unit, rate1_ref[:, 0:1])
    residual1_ref[...] = residual
    one = residual.astype(HALF)
    one_ref[...] = one
    mixed_ref[...] = mult_rt(one, out_w_ref[...]).astype(HALF)
    sums_ref[0:1, :] += (total * unit).sum(axis=0, keepdims=True)
    sums_ref[1:2, :] += total.sum(axis=0, keepdims=True)
    sums_ref[2:3, :] += residual.sum(axis=0, keepdims=True)


def back(half, residual, slope, unit1, rate1, down, up, out_w, table):
    length, wide = residual.shape
    inner = up.shape[1]
    rows = lambda cols: pl.BlockSpec((BLOCK, cols), lambda i: (i, 0))
    struct = jax.ShapeDtypeStruct
    weights = (down, up, out_w, table)
    return pl.pallas_call(
        back_kernel,
        grid=(length // BLOCK,),
        in_specs=[rows(wide), rows(wide), rows(inner), rows(wide), rows(LANES)] + memory([pltpu.VMEM] * len(weights)),
        out_specs=[rows(inner), rows(wide), rows(wide), rows(wide), whole((8, wide)), whole((8, inner))],
        out_shape=[
            struct((length, inner), HALF), struct((length, wide), FLOAT), struct((length, wide), HALF),
            struct((length, wide), HALF), struct((8, wide), FLOAT), struct((8, inner), FLOAT),
        ],
        compiler_params=params_of(("arbitrary",)),
        cost_estimate=LIGHT,
        name="back",
    )(half, residual, slope, unit1, rate1, *weights)


def input_kernel(grad_ref, residual_ref, weight_ref, out_ref):
    wide = residual_ref.shape[1]
    total = residual_ref[...]
    for part in range(3):
        total = total + mult_rt(grad_ref[part], weight_ref[:, part * wide : (part + 1) * wide])
    out_ref[...] = total


def input_pass(grad, residual, weight):
    length, wide = residual.shape
    return pl.pallas_call(
        input_kernel,
        grid=(length // BLOCK,),
        in_specs=[
            pl.BlockSpec((3, BLOCK, wide), lambda i: (0, i, 0)), pl.BlockSpec((BLOCK, wide), lambda i: (i, 0)),
            pl.BlockSpec(memory_space=pltpu.VMEM),
        ],
        out_specs=pl.BlockSpec((BLOCK, wide), lambda i: (i, 0)),
        out_shape=jax.ShapeDtypeStruct((length, wide), FLOAT),
        compiler_params=params_of(("arbitrary",)),
        cost_estimate=LIGHT,
        name="input_pass",
    )(grad, residual, weight)


def swap(value, axis, bits):
    size = lax.axis_size(axis)
    return lax.ppermute(value, axis, [(i, i ^ bits) for i in range(size)])


def around(value):
    return [value] + [swap(value, "replica", bits) for bits in (2, 4, 6)]


WIDE = 384
SMALL = (0, 128)
SMALL_ROWS = 16
VECTOR_ROWS = 32


def rows_of(mat):
    return SMALL_ROWS if mat == SMALL else mat[0] * mat[1] // 4


def all_rows(mats):
    return sum(rows_of(mat) for mat in mats)


def after(value, *others):
    return lax.optimization_barrier((value,) + others)[0]


FULL = 60 << 20


def vmem_call(kernel, name, where, inputs, outs, moved, scratch=(), limit=32 << 20):
    return pl.pallas_call(
        kernel,
        in_specs=memory([pltpu.SMEM] + [pltpu.VMEM] * len(inputs)),
        out_specs=memory([pltpu.VMEM] * len(outs)),
        out_shape=outs,
        scratch_shapes=list(scratch),
        compiler_params=params_of(None, limit),
        cost_estimate=LIGHT,
        name=name,
    )(where, *inputs)


def struct(shape, kind=HALF):
    return jax.ShapeDtypeStruct(shape, kind)


def aligned(begin, rows):
    return pl.ds(pl.multiple_of(begin, rows), rows)


def small_places(student_rows):
    third = student_rows // 3
    return third, third + 32


def fold_small(block_ref, base, student_ref, pool_ref, dense_ref, class_ref):
    third, last = small_places(student_ref.shape[0])
    for part in range(3):
        block_ref[base : base + third, part * LANES : (part + 1) * LANES] = student_ref[part * third : (part + 1) * third, :]
    block_ref[base + third : base + last, :] = pool_ref[...]
    rest = slice(base + last, base + 128)
    block_ref[rest, :] = jnp.zeros((128 - last, WIDE), block_ref.dtype)
    block_ref[rest, 0:LANES] = dense_ref[...]
    block_ref[rest, LANES : LANES + class_ref.shape[1]] = class_ref[...]


def unfold_small(block_ref, shard, student_ref, pool_ref, dense_ref, class_ref, rows):
    third, last = small_places(rows)
    base, short = shard * 128, 128 - last
    for part in range(3):
        begin = shard * rows + part * third
        student_ref[begin : begin + third, :] = block_ref[base : base + third, part * LANES : (part + 1) * LANES].astype(student_ref.dtype)
    target = slice(shard * short, (shard + 1) * short)
    pool_ref[target, :] = block_ref[base + third : base + last, :].astype(pool_ref.dtype)
    dense_ref[target, :] = block_ref[base + last : base + 128, 0:LANES].astype(dense_ref.dtype)
    classes = class_ref.shape[1]
    class_ref[target, :] = block_ref[base + last : base + 128, LANES : LANES + classes].astype(class_ref.dtype)


def pack_kernel(place_ref, *refs, mats, lines):
    chip, core = place_ref[1], place_ref[2]
    piece_ref = refs[-1]
    offset = 0
    if lines:
        base = all_rows(mats)
        for half in range(2):
            piece_ref[base : base + 16, half * LANES : (half + 1) * LANES] = refs[-2][half * 16 : half * 16 + 16, :]
        piece_ref[base : base + 16, 2 * LANES :] = jnp.zeros((16, WIDE - 2 * LANES), HALF)
    for mat, ref in zip(mats, refs):
        if mat == SMALL:
            small_ref = refs[-2]
            fold_small(small_ref, 0, *refs[len(mats) - 1 : len(mats) + 3])
            piece_ref[offset : offset + SMALL_ROWS, :] = small_ref[aligned((chip * 2 + core) * SMALL_ROWS, SMALL_ROWS), :]
            continue
        rows = mat[1] // 4
        for chunk in range(mat[0]):
            lanes = aligned(chunk * 2 * WIDE + core * WIDE, WIDE)
            piece_ref[offset : offset + rows, :] = ref[aligned(chip * rows, rows), lanes]
            offset += rows


def pack(where, shards, mats, lines=None):
    outs = [struct((all_rows(mats) + (0 if lines is None else 16), WIDE))]
    shards = list(shards) + ([] if lines is None else [lines])
    if SMALL in mats:
        outs = [struct(SMALL[1:] + (WIDE,))] + outs
    return vmem_call(partial(pack_kernel, mats=mats, lines=lines is not None), "pack", where, shards, outs, 2 * sum(s.size for s in shards), limit=FULL)


def put_piece(out_ref, ref, step, offset, base, mat, chip, core):
    if mat == SMALL:
        target = aligned(base + (chip * 2 + core) * SMALL_ROWS, SMALL_ROWS)
        out_ref[target, :] = ref[step, offset : offset + SMALL_ROWS, :].astype(out_ref.dtype)
        return
    rows = mat[1] // 4
    for chunk in range(mat[0]):
        lanes = aligned(chunk * 2 * WIDE + core * WIDE, WIDE)
        first = offset + chunk * rows
        out_ref[aligned(base + chip * rows, rows), lanes] = ref[step, first : first + rows, :].astype(out_ref.dtype)


def place_kernel(place_ref, *refs, mats, rows):
    shard, chip, core = place_ref[0], place_ref[1], place_ref[2]
    count = len(mats)
    pieces, owns, outs = refs[:8], refs[8 : 8 + count], list(refs[8 + count :])
    if SMALL in mats:
        block_ref = outs.pop()
        smalls, outs = outs[count - 1 :], outs[: count - 1] + [block_ref]
    offset = 0
    for mat, own_ref, out_ref in zip(mats, owns, outs):
        height = mat[1]
        out_ref[aligned(shard * height, height), :] = own_ref[...]
        for number, ref in enumerate(pieces):
            far, other = number // 2, number % 2
            for step in range(ref.shape[0]):
                base = (shard ^ (step + 1)) * height
                put_piece(out_ref, ref, step, offset, base, mat, chip ^ far, core ^ other)
        offset += rows_of(mat)
    if SMALL in mats:
        for step in range(pieces[0].shape[0] + 1):
            unfold_small(block_ref, step, *smalls, rows)


def place(where, pieces, owns, outs, mats, rows=0):
    shards = pieces[0].shape[0] + 1
    scratch = [pltpu.VMEM((shards * SMALL[1], WIDE), HALF)] if SMALL in mats else []
    moved = 4 * shards * sum(own.size for own in owns)
    return vmem_call(partial(place_kernel, mats=mats, rows=rows), "place", where, pieces + list(owns), outs, moved, scratch)


def table_kernel(place_ref, *refs, classes, base):
    *lines, table_ref, up_ref, short_ref, stack_ref = refs
    shard = place_ref[0]
    wide, inner = table_ref.shape[1], up_ref.shape[1]
    shards = len(lines)
    ups = inner // shards // LANES
    table = jnp.zeros(table_ref.shape, FLOAT)
    shorts = jnp.zeros((8, LANES), FLOAT)
    for step, ref in enumerate(lines):
        target = shard ^ step
        if step == 0:
            block = ref[...].astype(FLOAT)
        else:
            stack_ref[step - 1] = ref[...]
            block = jnp.concatenate([ref[base : base + 16, half * LANES : half * LANES + LANES] for half in range(2)], axis=0)
            block = block.astype(FLOAT)
        both = jnp.concatenate([block[0:8], block[8:16], jnp.zeros((8, wide - 2 * LANES), FLOAT)], axis=1)
        table = table + pltpu.roll(both, target * (wide // shards), 1)
        for line in range(ups):
            row = block[16 + line : 17 + line]
            up_ref[:, aligned(target * (inner // shards) + line * LANES, LANES)] = jnp.broadcast_to(row, (8, LANES))
        shorts = shorts + pltpu.roll(block[16 : 24], target * (LANES // shards), 1)
    table_ref[...] = table
    lane = lax.broadcasted_iota(jnp.int32, (1, LANES), 1)
    short_ref[0:2, :] = shorts[6:8]
    short_ref[2:3, :] = lines[0][...].astype(FLOAT)[24:25]
    short_ref[3:4, :] = jnp.where(lane < classes, 1.0, 0.0)
    short_ref[4:8, :] = jnp.zeros((4, LANES), FLOAT)


def lines_kernel(place_ref, *refs):
    *vectors, up_ref, student_ref, dense_ref, class_ref, out_ref, full_ref = refs
    full_ref[...] = jnp.zeros_like(full_ref)

    def put(row, value):
        full_ref[row : row + 1, 0 : value.shape[0]] = value.astype(FLOAT).reshape(1, value.shape[0])

    for line, ref in enumerate(vectors):
        put(line, ref[0:LANES])
        put(8 + line, ref[LANES:])
    for line in range(up_ref.shape[0] // LANES):
        put(16 + line, up_ref[line * LANES : (line + 1) * LANES])
    put(22, student_ref[...])
    put(23, dense_ref[...])
    put(24, class_ref[...])
    out_ref[...] = full_ref[...].astype(HALF)


def vector_lines(where, vectors, up_bias, shorts, class_bias):
    inputs = [*vectors, up_bias, *shorts, class_bias]
    (lines,) = vmem_call(lines_kernel, "lines", where, inputs, [struct((32, LANES))], 0, [pltpu.VMEM((32, LANES), FLOAT)], FULL)
    return lines


def from_shards(value):
    return [swap(value, "shard", bits) for bits in range(1, lax.axis_size("shard"))]


def both_cores(values):
    return [piece for value in values for piece in (value, swap(value, "replica", 1))]


def weight_grad_kernel(place_ref, left_ref, right_ref, send_ref, keep_ref):
    core = place_ref[2]
    left = left_ref[...]
    for chunk in range(send_ref.shape[0]):
        for ref, which in ((send_ref, 1 - core), (keep_ref, core)):
            if len(right_ref.shape) == 3:
                right = right_ref[chunk, :, aligned(which * WIDE, WIDE)]
            else:
                right = right_ref[:, aligned(chunk * 2 * WIDE + which * WIDE, WIDE)]
            ref[chunk] = mult(left, right).astype(HALF)


def weight_grad(where, left, right, name, block=256):
    height, length = left.shape
    chunks = right.shape[0] if right.ndim == 3 else right.shape[1] // (2 * WIDE)
    out = struct((chunks, height, WIDE))
    return pl.pallas_call(
        weight_grad_kernel,
        grid=(height // block,),
        in_specs=[pl.BlockSpec(memory_space=pltpu.SMEM), pl.BlockSpec((block, length), lambda i: (i, 0))]
        + memory([pltpu.VMEM]),
        out_specs=[pl.BlockSpec((chunks, block, WIDE), lambda i: (0, i, 0))] * 2,
        out_shape=[out, out],
        compiler_params=params_of(("arbitrary",)),
        cost_estimate=LIGHT,
        name=name,
    )(where, left, right)


def small_grad_kernel(place_ref, hidden_ref, grad_student_ref, student_ref, grad_pool_ref, dense_ref, class_ref, send_ref, keep_ref, block_ref, first_ref, pool_ref):
    core = place_ref[2]
    shards = send_ref.shape[1] // (4 * SMALL_ROWS)
    first_ref[...] = mult(hidden_ref[...], grad_student_ref[...])
    pool_ref[...] = mult(student_ref[...], grad_pool_ref[...])
    part = lambda ref, shard: ref.at[pl.ds(shard * (ref.shape[0] // shards), ref.shape[0] // shards)]
    for shard in range(shards):
        fold_small(block_ref, shard * 128, *(part(ref, shard) for ref in (first_ref, pool_ref, dense_ref, class_ref)))
    for shard in range(shards):
        for chip in range(4):
            target = pl.ds((shard * 4 + chip) * SMALL_ROWS, SMALL_ROWS)
            for ref, which in ((send_ref, 1 - core), (keep_ref, core)):
                ref[0, target, :] = block_ref[aligned(shard * 128 + (chip * 2 + which) * SMALL_ROWS, SMALL_ROWS), :].astype(HALF)


def small_grad(where, hidden, grad_student, student, grad_pool, dense, classes, shards):
    outs = [struct((1, shards * 4 * SMALL_ROWS, WIDE))] * 2
    scratch = [
        pltpu.VMEM((shards * 128, WIDE), FLOAT), pltpu.VMEM((hidden.shape[0], LANES), FLOAT), pltpu.VMEM((LANES, WIDE), FLOAT)
    ]
    inputs = [hidden, grad_student, student, grad_pool, dense, classes]
    return vmem_call(small_grad_kernel, "small_grad", where, inputs, outs, 4 * hidden.size, scratch)


def vector_kernel(place_ref, heads_ref, one_ref, two_ref, up_ref, short_ref, half_ref, out_ref):
    half = heads_ref.shape[1] // 2
    for side in range(2):
        lanes = slice(side * half, (side + 1) * half)
        lines = [heads_ref[0:1, lanes], heads_ref[1:2, lanes], one_ref[2:3, lanes], one_ref[0:1, lanes], one_ref[1:2, lanes]]
        lines += [two_ref[2:3, lanes], two_ref[0:1, lanes], two_ref[1:2, lanes]]
        for row, line in enumerate(lines):
            out_ref[side * 8 + row : side * 8 + row + 1, :] = line
    for row in range(up_ref.shape[1] // WIDE):
        out_ref[16 + row : 17 + row, :] = up_ref[0:1, row * WIDE : (row + 1) * WIDE]
    out_ref[24:32, :] = jnp.zeros((8, WIDE), FLOAT)
    for part in range(3):
        out_ref[24:25, part * LANES : (part + 1) * LANES] = short_ref[part : part + 1, :]
    half_ref[...] = out_ref[...].astype(HALF)


def split_kernel(place_ref, *refs, count, shards, vectors):
    chip = place_ref[1]
    keeps, recvs, outs = refs[:count], refs[count : 2 * count], refs[-4:]
    total = sum(keep.shape[0] * keep.shape[1] for keep in keeps) // (4 * shards)
    offset = 0
    for keep_ref, recv_ref in zip(keeps, recvs):
        height = keep_ref.shape[1] // shards
        rows = height // 4
        for chunk in range(keep_ref.shape[0]):
            for shard in range(shards):
                for far, out_ref in enumerate(outs):
                    source = aligned(shard * height + (chip ^ far) * rows, rows)
                    value = keep_ref[chunk, source, :].astype(FLOAT) + recv_ref[chunk, source, :].astype(FLOAT)
                    first = shard * total + offset
                    out_ref[first : first + rows, :] = value.astype(HALF)
            offset += rows
    if vectors:
        value = (refs[2 * count][...].astype(FLOAT) + refs[2 * count + 1][...].astype(FLOAT)).astype(HALF)
        for out_ref in outs:
            out_ref[shards * total : shards * total + VECTOR_ROWS, :] = value


def split(where, keeps, recvs, shards, vectors=()):
    total = sum(keep.shape[0] * keep.shape[1] for keep in keeps) // 4 + (VECTOR_ROWS if vectors else 0)
    kernel = partial(split_kernel, count=len(keeps), shards=shards, vectors=bool(vectors))
    inputs = list(keeps) + list(recvs) + list(vectors)
    return vmem_call(kernel, "split", where, inputs, [struct((total, WIDE))] * 4, 20 * total * WIDE)


def merge_kernel(place_ref, *refs, shards, vectors):
    shard = place_ref[0]
    parts, outs = refs[: -shards], refs[-shards:]
    offset = 0
    for group in range(len(parts) // 4):
        four = parts[4 * group : 4 * group + 4]
        last = vectors and group == len(parts) // 4 - 1
        rows = (four[0].shape[0] - (VECTOR_ROWS if last else 0)) // shards

        def total(source):
            a, b, c, d = (ref[source, :].astype(FLOAT) for ref in four)
            return ((a + b) + (c + d)).astype(HALF)

        for step, out_ref in enumerate(outs):
            out_ref[offset : offset + rows, :] = total(aligned((shard ^ step) * rows, rows))
        offset += rows
        if last:
            value = total(slice(shards * rows, shards * rows + VECTOR_ROWS))
            for out_ref in outs:
                out_ref[offset : offset + VECTOR_ROWS, :] = value


def merge(where, groups, shards, vectors=False):
    extra = VECTOR_ROWS if vectors else 0
    rows = (sum(four[0].shape[0] for four in groups) - extra) // shards + extra
    kernel = partial(merge_kernel, shards=shards, vectors=vectors)
    inputs = [part for four in groups for part in four]
    return vmem_call(kernel, "merge", where, inputs, [struct((rows, WIDE))] * shards, 10 * shards * rows * WIDE)


def total_kernel(place_ref, *refs, shards):
    parts, outs = refs[:shards], refs[shards:]
    offset = 0
    for out_ref in outs:
        rows = slice(offset, offset + out_ref.shape[0])
        terms = [ref[rows, :].astype(FLOAT) for ref in parts]
        while len(terms) > 1:
            half = len(terms) // 2
            terms = [terms[i] + terms[i + half] for i in range(half)]
        out_ref[...] = terms[0].astype(HALF)
        offset += out_ref.shape[0]


def total(where, parts, vectors=False):
    rows = parts[0].shape[0] - (VECTOR_ROWS if vectors else 0)
    outs = [struct((rows, WIDE))] + ([struct((VECTOR_ROWS, WIDE))] if vectors else [])
    outs = vmem_call(partial(total_kernel, shards=len(parts)), "total", where, parts, outs, 10 * rows * WIDE)
    bits = 8
    while bits < lax.axis_size("replica"):
        outs = [(v.astype(FLOAT) + swap(v, "replica", bits).astype(FLOAT)).astype(HALF) for v in outs]
        bits *= 2
    return outs


def finish_kernel(place_ref, *refs, mats, rows):
    chip, core = place_ref[1], place_ref[2]
    pieces, outs = refs[:8], list(refs[8:])
    if SMALL in mats:
        block_ref = outs.pop()
        smalls, outs = outs[len(mats) - 1 :], outs[: len(mats) - 1] + [block_ref]
    offset = 0
    for mat, out_ref in zip(mats, outs):
        for number, ref in enumerate(pieces):
            put_piece(out_ref, ref, 0, offset, 0, mat, chip ^ (number // 2), core ^ (number % 2))
        offset += rows_of(mat)
    if SMALL in mats:
        unfold_small(block_ref, 0, *smalls, rows)


def finish(where, pieces, mats, outs, rows=0):
    pieces = [piece[None] for piece in pieces]
    scratch = [pltpu.VMEM(SMALL[1:] + (WIDE,), FLOAT)] if SMALL in mats else []
    moved = 6 * sum(out.size for out in outs)
    return vmem_call(partial(finish_kernel, mats=mats, rows=rows), "finish", where, pieces, outs, moved, scratch)


def vector_out_kernel(place_ref, total_ref, *refs):
    tables, up_ref, shorts, class_ref = refs[:8], refs[8], refs[9:11], refs[11]
    shard = place_ref[0]
    wide = 2 * WIDE
    each = tables[0].shape[0]
    shards = wide // each
    values = total_ref[...].astype(FLOAT)
    table = jnp.concatenate([values[0:8], values[8:16]], axis=1)
    table = pltpu.roll(table, (shards - shard) * each, 1)[:, :each]
    for line, ref in enumerate(tables):
        ref[...] = table[line : line + 1].reshape(each)
    lines = up_ref.shape[0] // WIDE
    for line in range(lines):
        row = jnp.zeros((1, WIDE), FLOAT)
        for which in range(shards):
            row = row + jnp.where(shard == which, values[16 + which * lines + line : 17 + which * lines + line], 0.0)
        up_ref[line * WIDE : (line + 1) * WIDE] = row.reshape(WIDE)
    each = shorts[0].shape[0]
    for part, ref in enumerate(shorts):
        row = pltpu.roll(values[24:32, part * LANES : (part + 1) * LANES], (shards - shard) * each, 1)
        ref[...] = row[0:1, :each].reshape(each)
    class_ref[...] = values[24:25, 2 * LANES : 2 * LANES + class_ref.shape[0]].reshape(class_ref.shape[0])


def vector_out(where, value, shards, inner, classes):
    outs = [struct((2 * WIDE // shards,), FLOAT)] * 8 + [struct((inner // shards,), FLOAT)]
    outs += [struct((LANES // shards,), FLOAT)] * 2 + [struct((classes,), FLOAT)]
    return vmem_call(vector_out_kernel, "vector_out", where, [value], outs, 4 * value.size)


def body(
    tokens, cotangent, piece_starts, labels, qkv_weight, query_bias, value_bias, out_weight, out_bias, attention_gain,
    attention_shift, up_weight, up_bias, down_weight, down_bias, feed_gain, feed_shift, student_weight, student_bias,
    pool_weight, dense_weight, dense_bias, class_weight, class_bias,
):
    count, length, wide = tokens.shape
    inner = up_weight.shape[1]
    classes = class_weight.shape[1]
    student_rows = student_weight.shape[0]
    shards = lax.axis_size("shard")
    replica = lax.axis_index("replica")
    where = jnp.stack([lax.axis_index("shard"), (replica >> 1) & 3, replica & 1]).astype(jnp.int32)
    tokens, cotangent = tokens.reshape(length, wide), cotangent.reshape(length, wide)
    qkv_mats = ((3, qkv_weight.shape[0]),)
    up_mats = ((1, out_weight.shape[0]), (4, up_weight.shape[0]))
    down_mats = ((1, down_weight.shape[0]), SMALL)

    (piece,) = pack(where, [qkv_weight], qkv_mats)
    near = from_shards(piece)
    lines = vector_lines(
        where,
        [after(query_bias, piece), value_bias, out_bias, attention_gain, attention_shift, down_bias, feed_gain, feed_shift],
        up_bias, [student_bias, dense_bias], class_bias,
    )
    (up_piece,) = pack(where, [out_weight, up_weight], up_mats, lines)
    small, down_piece = pack(
        where, [after(down_weight, piece), student_weight, pool_weight, dense_weight, class_weight], down_mats
    )
    tokens_t = flip(after(tokens, piece))
    near[0], up_piece, small, down_piece, tokens_t = lax.optimization_barrier((near[0], up_piece, small, down_piece, tokens_t))
    near_stack = jnp.stack(near)
    qkv_around = around(near_stack)
    up_near = [swap(up_piece, "shard", bits) for bits in range(1, shards - 1)]
    qkv_around[1], *up_near = lax.optimization_barrier((qkv_around[1], *up_near))
    up_near.append(swap(after(up_piece, qkv_around[1]), "shard", shards - 1))
    qkv_pieces = both_cores(qkv_around)
    (qkv,) = place(where, qkv_pieces, [qkv_weight], [struct((shards * qkv_weight.shape[0], 3 * wide))], qkv_mats)
    up_near[0] = after(up_near[0], qkv)
    table, up_b, small_b, up_stack = vmem_call(
        partial(table_kernel, classes=classes, base=all_rows(up_mats)), "table", where, [lines] + up_near,
        [
            struct((8, wide), FLOAT), struct((8, inner), FLOAT), struct((8, LANES), FLOAT),
            struct((shards - 1,) + up_piece.shape),
        ],
        8 * 8 * inner,
    )
    down_piece = after(down_piece, up_stack)
    up_around = around(up_stack)
    down_near = [swap(down_piece, "shard", bits) for bits in range(1, shards - 1)]
    qkv = after(qkv, up_stack)
    joined = project(tokens, qkv, table)
    joined, down_piece, down_near[0] = lax.optimization_barrier((joined, down_piece, down_near[0]))
    down_near.append(swap(down_piece, "shard", shards - 1))
    mixed, mixed_t, lse = attend_forward(joined, piece_starts)
    whole_of = lambda shard: struct((shards * shard.shape[0], shard.shape[1]))
    mixed, *arrived = lax.optimization_barrier((mixed, *down_near, *up_around))
    down_near, up_around = arrived[: shards - 1], arrived[shards - 1 :]
    down_stack = jnp.stack(down_near)
    down_around = around(after(down_stack, mixed))
    out_w, up = place(
        where, both_cores(up_around), [out_weight, up_weight], [whole_of(out_weight), whole_of(up_weight)], up_mats
    )

    first, first_t, active, active_t, slope, unit1, rate1 = feed_up(
        mixed, tokens, after(out_w, down_stack), up, table, up_b
    )
    rest = [whole_of(s) for s in (down_weight, student_weight, pool_weight, dense_weight)]
    rest.append(struct((shards * class_weight.shape[0], LANES)))
    active, *down_around = lax.optimization_barrier((active, *down_around))
    down, student_w, pool_w, dense_w, class_w = place(
        where, both_cores(down_around), [down_weight, small], rest, down_mats, student_rows
    )
    hidden, hidden_t, unit2, rate2, student_t, pool = feed_down(
        first, active, down, student_w, pool_w, table, small_b
    )
    logits, grad_pool, grad_student, residual2, half2, grad_dense, grad_class, small_sums, sums2 = student_pass(
        labels, cotangent, pool, unit2, rate2, student_w, pool_w, dense_w, class_w, small_b, table, classes
    )
    core_swap = lambda value: swap(value, "replica", 1)
    exchange = lambda parts: [parts[0]] + [swap(part, "replica", 2 * far) for far, part in enumerate(parts) if far > 0]
    spread = lambda parts: [parts[0]] + [swap(part, "shard", far) for far, part in enumerate(parts) if far > 0]
    send_down, keep_down = weight_grad(where, active_t, half2, "grad_down")
    send_small, keep_small = small_grad(
        where, after(hidden_t, send_down), grad_student, student_t, grad_pool, grad_dense, grad_class, shards
    )
    parts_a = split(where, [after(keep_down, keep_small)], [core_swap(send_down)], shards)
    exchanged_a = exchange(parts_a)
    grad_inner, residual1, half1, grad_mixed, sums1, up_sums = back(
        after(half2, parts_a[0], keep_small), residual2, slope, unit1, rate1, down, up, out_w, table
    )
    send_up, keep_up = weight_grad(where, first_t, grad_inner, "grad_up")
    swapped_small = core_swap(send_small)
    send_up, mixed_t, swapped_small, *exchanged_a = lax.optimization_barrier((send_up, mixed_t, swapped_small, *exchanged_a))
    send_out, keep_out = weight_grad(where, mixed_t, half1, "grad_out")
    parts_b = split(where, [keep_out, keep_up], [core_swap(send_out), core_swap(send_up)], shards)
    exchanged_b = exchange(parts_b)
    heads, head_sums = attend_backward(joined, piece_starts, mixed, after(grad_mixed, parts_b[0]), lse)
    send_qkv, keep_qkv = weight_grad(where, tokens_t, heads, "grad_qkv")
    send_qkv, *exchanged_b = lax.optimization_barrier((send_qkv, *exchanged_b))
    ready = merge(where, [exchanged_b, exchanged_a], shards)
    near_ab = spread(ready)
    keep_qkv = after(keep_qkv, ready[0])
    (vectors,) = vmem_call(
        vector_kernel, "vectors", where,
        [head_sums, sums1, sums2, up_sums, small_sums], [struct((VECTOR_ROWS, WIDE))], 4 * VECTOR_ROWS * WIDE,
        [pltpu.VMEM((VECTOR_ROWS, WIDE), FLOAT)],
    )
    parts_c = split(
        where, [keep_qkv, keep_small], [core_swap(send_qkv), swapped_small], shards, (vectors, core_swap(vectors))
    )
    exchanged_c = exchange(parts_c)
    input_grad = input_pass(after(heads, parts_c[0]), residual1, qkv)
    near_ab[0] = after(near_ab[0], input_grad)
    (piece_ab,) = total(where, near_ab)
    piece_ab, *exchanged_c = lax.optimization_barrier((piece_ab, *exchanged_c))
    ready = merge(where, [exchanged_c], shards, True)
    near_c = spread(ready)
    around_ab = around(after(piece_ab, near_c[1]))
    near_c[0], *around_ab = lax.optimization_barrier((near_c[0], *around_ab))
    pieces_ab = both_cores(around_ab)
    piece_c, vectors = total(where, near_c, True)
    around_c = around(piece_c)
    full = lambda shard: struct(shard.shape, FLOAT)
    ab_mats = up_mats + down_mats[:1]
    grad_out, grad_up, grad_down = finish(
        where, pieces_ab, ab_mats, [full(s) for s in (out_weight, up_weight, down_weight)]
    )
    around_c[-1] = after(around_c[-1], grad_out)
    pieces_c = both_cores(around_c)
    *g_table, g_up_b, g_student_b, g_dense_b, g_class_b = vector_out(where, vectors, shards, inner, classes)
    grad_qkv, g_student, g_pool, g_dense, g_class = finish(
        where, pieces_c, qkv_mats + (SMALL,),
        [full(s) for s in (qkv_weight, student_weight, pool_weight, dense_weight, class_weight)], student_rows,
    )
    return (
        hidden.reshape(count, length, wide), logits, input_grad.reshape(count, length, wide),
        grad_qkv, g_table[0], g_table[1], grad_out, g_table[2], g_table[3], g_table[4], grad_up, g_up_b, grad_down,
        g_table[5], g_table[6], g_table[7], g_student, g_student_b, g_pool, g_dense, g_dense_b, g_class, g_class_b,
    )


def solution(mesh):
    placed = (
        P(("shard", "replica"), None, None),
        P(("shard", "replica"), None, None),
        P(("shard", "replica"), None),
        P(("shard", "replica")),
        P("shard", None),
        P("shard"),
        P("shard"),
        P("shard", None),
        P("shard"),
        P("shard"),
        P("shard"),
        P("shard", None),
        P("shard"),
        P("shard", None),
        P("shard"),
        P("shard"),
        P("shard"),
        P("shard", None),
        P("shard"),
        P("shard", None),
        P("shard", None),
        P("shard"),
        P("shard", None),
        P(),
    )
    return jax.shard_map(
        body,
        mesh=mesh,
        in_specs=placed,
        out_specs=(
            P(("shard", "replica"), None, None),
            P(("shard", "replica"), None),
            P(("shard", "replica"), None, None),
            P("shard", None),
            P("shard"),
            P("shard"),
            P("shard", None),
            P("shard"),
            P("shard"),
            P("shard"),
            P("shard", None),
            P("shard"),
            P("shard", None),
            P("shard"),
            P("shard"),
            P("shard"),
            P("shard", None),
            P("shard"),
            P("shard", None),
            P("shard", None),
            P("shard"),
            P("shard", None),
            P(),
        ),
        check_vma=False,
    )
```

```python
from functools import partial

import jax
import jax.numpy as jnp
from jax import lax
from jax.experimental import pallas as pl
from jax.experimental.pallas import tpu as pltpu
from jax.sharding import PartitionSpec as P

HEADS = 12
POOL_HEADS = 2
PIECE = 256
NORM_EPS = 1e-06
MASKED_SCORE = -1e30
FLOAT = jnp.float32
HALF = jnp.bfloat16
PRECISE = lax.Precision.HIGHEST
LANES = 128
BLOCK = 256

ERF_SLOPE = 0.42
ERF_TERMS = (
    0.23691840576326206,
    0.2382680869907842,
    0.20182398814655725,
    0.2493386597508521,
    -0.10108083678814953,
    0.4156989047782712,
    -0.3092846516362072,
    0.06831743518928779,
)


LIGHT = pl.CostEstimate(flops=100000, transcendentals=0, bytes_accessed=100000)


def params_of(kinds, limit=44 << 20):
    return pltpu.CompilerParams(dimension_semantics=kinds, vmem_limit_bytes=limit)


def whole(shape, space=None):
    return pl.BlockSpec(shape, lambda *_: (0,) * len(shape))


def memory(kinds):
    return [pl.BlockSpec(memory_space=kind) for kind in kinds]


def mult(left, right):
    return jnp.dot(left, right, preferred_element_type=FLOAT)


def mult_rt(left, right):
    return lax.dot_general(left, right, (((1,), (1,)), ((), ())), preferred_element_type=FLOAT)


def mult_lt(left, right):
    return lax.dot_general(left, right, (((0,), (0,)), ((), ())), preferred_element_type=FLOAT)


def precise(left, right, dims):
    return lax.dot_general(
        left, right, ((dims[:1], dims[1:]), ((), ())), precision=PRECISE, preferred_element_type=FLOAT
    )


def key_extent(block, length):
    return min(length, (block + 2) * BLOCK)


def allowed_block(starts_ref, first_row, first_col, shape, row_axis):
    rows = first_row + lax.broadcasted_iota(jnp.int32, shape, row_axis)
    cols = first_col + lax.broadcasted_iota(jnp.int32, shape, 1 - row_axis)
    allowed = cols <= rows
    for piece in range(starts_ref.shape[1]):
        start = starts_ref[0, piece]
        inside = (rows >= start) & (rows < start + PIECE) & (cols >= start) & (cols < start + PIECE)
        allowed = allowed | inside
    return allowed


def fill_bias(starts_ref, bias_ref, length, row_axis):
    for block in range(length // BLOCK):
        wide = key_extent(block, length) - block * BLOCK
        shape = (BLOCK, wide) if row_axis == 0 else (wide, BLOCK)
        allowed = allowed_block(starts_ref, block * BLOCK, block * BLOCK, shape, row_axis)
        bias = jnp.where(allowed, 0.0, MASKED_SCORE).astype(FLOAT)
        if row_axis == 0:
            bias_ref[block, :, 0:wide] = bias
        else:
            bias_ref[block, 0:wide, :] = bias


def half_lanes(value, half):
    lane = lax.broadcasted_iota(jnp.int32, value.shape, 1)
    keep = (lane < LANES // 2) if half == 0 else (lane >= LANES // 2)
    return jnp.where(keep, value, jnp.zeros_like(value))


def attend_forward_kernel(starts_ref, q_ref, k_ref, v_ref, mixed_ref, flipped_ref, lse_ref, bias_ref):
    length = q_ref.shape[0]
    scale = (LANES // 2) ** (-0.5)

    @pl.when(pl.program_id(0) == 0)
    def _():
        fill_bias(starts_ref, bias_ref, length, 0)

    values = [half_lanes(v_ref[...], half) for half in range(2)]
    lane = lax.broadcasted_iota(jnp.int32, (BLOCK, LANES), 1)
    for block in range(length // BLOCK):
        begin = block * BLOCK
        extent = key_extent(block, length)
        query = q_ref[begin : begin + BLOCK, :] * jnp.asarray(scale, HALF)
        outs = []
        logs = []
        for half in range(2):
            scores = mult_rt(half_lanes(query, half), k_ref[0:extent, :])
            edge = scores[:, begin:extent] + bias_ref[block, :, 0 : extent - begin]
            parts = [edge] if begin == 0 else [scores[:, 0:begin], edge]
            ceiling = parts[0].max(axis=1, keepdims=True)
            for part in parts[1:]:
                ceiling = jnp.maximum(ceiling, part.max(axis=1, keepdims=True))
            total = 0.0
            mixed = 0.0
            place = 0
            for part in parts:
                raised = jnp.exp(part - ceiling)
                total = total + raised.sum(axis=1, keepdims=True)
                mixed = mixed + mult(
                    raised.astype(HALF), values[half][place : place + part.shape[1], :]
                )
                place += part.shape[1]
            outs.append(mixed / total)
            logs.append(ceiling + jnp.log(total))
        rounded = (outs[0] + outs[1]).astype(HALF)
        mixed_ref[begin : begin + BLOCK, :] = rounded
        flipped_ref[:, begin : begin + BLOCK] = rounded.T
        both = jnp.where(lane == 0, logs[0], logs[1])
        lse_ref[:, begin : begin + BLOCK] = both.T[0:8, :]


def attend_forward(joined, starts):
    length, wide = joined.shape
    pairs = wide // 3 // LANES
    return pl.pallas_call(
        attend_forward_kernel,
        grid=(pairs,),
        in_specs=[
            pl.BlockSpec(memory_space=pltpu.SMEM),
            pl.BlockSpec((length, LANES), lambda h: (0, h)),
            pl.BlockSpec((length, LANES), lambda h: (0, pairs + h)),
            pl.BlockSpec((length, LANES), lambda h: (0, 2 * pairs + h)),
        ],
        out_specs=[
            pl.BlockSpec((length, LANES), lambda h: (0, h)),
            pl.BlockSpec((LANES, length), lambda h: (h, 0)),
            pl.BlockSpec((8, length), lambda h: (h, 0)),
        ],
        out_shape=[
            jax.ShapeDtypeStruct((length, wide // 3), HALF),
            jax.ShapeDtypeStruct((wide // 3, length), HALF),
            jax.ShapeDtypeStruct((pairs * 8, length), FLOAT),
        ],
        scratch_shapes=[pltpu.VMEM((length // BLOCK, BLOCK, 2 * BLOCK), FLOAT)],
        compiler_params=params_of(("arbitrary",)),
        cost_estimate=LIGHT,
        name="attend_forward",
    )(starts, joined, joined, joined)


def attend_backward_kernel(
    starts_ref, q_ref, k_ref, v_ref, mixed_ref, grad_ref, lse_ref, out_ref, sums_ref, bias_ref, dk_ref, dv_ref
):
    length = q_ref.shape[0]
    scale = (LANES // 2) ** (-0.5)

    @pl.when(pl.program_id(0) == 0)
    def _():
        fill_bias(starts_ref, bias_ref, length, 1)

    product = grad_ref[...].astype(FLOAT) * mixed_ref[...].astype(FLOAT)
    row = lax.broadcasted_iota(jnp.int32, (8, LANES), 0)
    col = lax.broadcasted_iota(jnp.int32, (8, LANES), 1)
    picks = jnp.where((col < LANES // 2) == (row == 0), 1.0, 0.0).astype(FLOAT)
    inner = precise(picks, product, (1, 1))
    keys = [half_lanes(k_ref[...] * jnp.asarray(scale, HALF), half) for half in range(2)]
    values = [half_lanes(v_ref[...], half) for half in range(2)]
    dk_ref[...] = jnp.zeros_like(dk_ref)
    dv_ref[...] = jnp.zeros_like(dv_ref)
    query_sum = jnp.zeros((1, LANES), FLOAT)
    for block in range(length // BLOCK):
        begin = block * BLOCK
        extent = key_extent(block, length)
        query = q_ref[begin : begin + BLOCK, :]
        grad = grad_ref[begin : begin + BLOCK, :]
        grad_query = 0.0
        for half in range(2):
            scores = mult_rt(keys[half][0:extent, :], query)
            grad_probs = mult_rt(values[half][0:extent, :], grad)
            lse = lse_ref[half : half + 1, begin : begin + BLOCK]
            base = inner[half : half + 1, begin : begin + BLOCK]
            edge = scores[begin:extent, :] + bias_ref[block, 0 : extent - begin, :]
            shifted = edge if begin == 0 else jnp.concatenate([scores[0:begin, :], edge], axis=0)
            probs = jnp.exp(shifted - lse)
            grad_scores = (probs * (grad_probs - base)).astype(HALF)
            grad_half = half_lanes(grad, half)
            query_half = half_lanes(query * jnp.asarray(scale, HALF), half)
            dv_ref[0:extent, :] += mult(probs.astype(HALF), grad_half)
            dk_ref[0:extent, :] += mult(grad_scores, query_half)
            grad_query = grad_query + mult_lt(grad_scores, keys[half][0:extent, :])
        rounded = grad_query.astype(HALF)
        out_ref[0, begin : begin + BLOCK, :] = rounded
        query_sum = query_sum + rounded.astype(FLOAT).sum(axis=0, keepdims=True)
    out_ref[1, :, :] = dk_ref[...].astype(HALF)
    value = dv_ref[...].astype(HALF)
    out_ref[2, :, :] = value
    value_sum = value.astype(FLOAT).sum(axis=0, keepdims=True)
    sums_ref[...] = jnp.where(row == 0, query_sum, value_sum)


def attend_backward(joined, starts, mixed, grad_mixed, lse):
    length, wide = joined.shape
    pairs = wide // 3 // LANES
    return pl.pallas_call(
        attend_backward_kernel,
        grid=(pairs,),
        in_specs=[
            pl.BlockSpec(memory_space=pltpu.SMEM),
            pl.BlockSpec((length, LANES), lambda h: (0, h)),
            pl.BlockSpec((length, LANES), lambda h: (0, pairs + h)),
            pl.BlockSpec((length, LANES), lambda h: (0, 2 * pairs + h)),
            pl.BlockSpec((length, LANES), lambda h: (0, h)),
            pl.BlockSpec((length, LANES), lambda h: (0, h)),
            pl.BlockSpec((8, length), lambda h: (h, 0)),
        ],
        out_specs=[
            pl.BlockSpec((3, length, LANES), lambda h: (0, 0, h)),
            pl.BlockSpec((8, LANES), lambda h: (0, h)),
        ],
        out_shape=[
            jax.ShapeDtypeStruct((3, length, wide // 3), HALF),
            jax.ShapeDtypeStruct((8, wide // 3), FLOAT),
        ],
        scratch_shapes=[
            pltpu.VMEM((length // BLOCK, 2 * BLOCK, BLOCK), FLOAT),
            pltpu.VMEM((length, LANES), FLOAT),
            pltpu.VMEM((length, LANES), FLOAT),
        ],
        compiler_params=params_of(("arbitrary",)),
        cost_estimate=LIGHT,
        name="attend_backward",
    )(starts, joined, joined, joined, mixed, grad_mixed, lse)


def normalise(values):
    middle = values.mean(axis=1, keepdims=True)
    centered = values - middle
    spread = (centered * centered).mean(axis=1, keepdims=True)
    rate = lax.rsqrt(spread + NORM_EPS)
    return centered * rate, rate


def normalise_backward(grad_unit, unit, rate):
    along = grad_unit.mean(axis=1, keepdims=True)
    across = (grad_unit * unit).mean(axis=1, keepdims=True)
    return rate * (grad_unit - along - unit * across)


def gelu_pair(inner):
    size = jnp.abs(inner)
    ratio = 1.0 / (1.0 + (ERF_SLOPE * 2.0**-0.5) * size)
    tail = jnp.full_like(ratio, 0.5 * ERF_TERMS[-1])
    for term in ERF_TERMS[-2::-1]:
        tail = tail * ratio + 0.5 * term
    bell = jnp.exp(-0.5 * inner * inner)
    tail = tail * ratio * bell
    below = jnp.where(inner < 0.0, tail, 1.0 - tail)
    return inner * below, below + inner * (bell * (2.0 * jnp.pi) ** -0.5)


QUERY_B, VALUE_B, OUT_B, GAIN1, SHIFT1, DOWN_B, GAIN2, SHIFT2 = range(8)


def flip_kernel(value_ref, out_ref):
    out_ref[...] = value_ref[...].T


def flip(value):
    return pl.pallas_call(
        flip_kernel,
        in_specs=memory([pltpu.VMEM]),
        out_specs=pl.BlockSpec(memory_space=pltpu.VMEM),
        out_shape=jax.ShapeDtypeStruct(value.shape[::-1], value.dtype),
        compiler_params=params_of(None, FULL),
        cost_estimate=LIGHT,
        name="flip",
    )(value)


def project_kernel(tokens_ref, weight_ref, table_ref, out_ref):
    wide = tokens_ref.shape[1]
    for part in range(3):
        value = mult(tokens_ref[...], weight_ref[:, part * wide : (part + 1) * wide])
        if part == 0:
            value = value + table_ref[QUERY_B : QUERY_B + 1, :]
        elif part == 2:
            value = value + table_ref[VALUE_B : VALUE_B + 1, :]
        out_ref[:, part * wide : (part + 1) * wide] = value.astype(HALF)


def project(tokens, weight, table):
    length, wide = tokens.shape
    return pl.pallas_call(
        project_kernel,
        grid=(length // BLOCK,),
        in_specs=[pl.BlockSpec((BLOCK, wide), lambda i: (i, 0))] + memory([pltpu.VMEM] * 2),
        out_specs=pl.BlockSpec((BLOCK, 3 * wide), lambda i: (i, 0)),
        out_shape=jax.ShapeDtypeStruct((length, 3 * wide), HALF),
        compiler_params=params_of(("arbitrary",)),
        cost_estimate=LIGHT,
        name="project",
    )(tokens, weight, table)


def feed_up_kernel(
    mixed_ref, tokens_ref, out_w_ref, up_ref, table_ref, up_b_ref,
    first_ref, first_t_ref, active_ref, active_t_ref, slope_ref, unit1_ref, rate1_ref,
):
    wide = tokens_ref.shape[1]
    line = lambda which: table_ref[which : which + 1, :]
    residual = tokens_ref[...].astype(FLOAT) + (mult(mixed_ref[...], out_w_ref[...]) + line(OUT_B))
    unit, rate = normalise(residual)
    unit1_ref[...] = unit.astype(HALF)
    rate1_ref[...] = jnp.broadcast_to(rate, rate1_ref.shape)
    first = unit * line(GAIN1) + line(SHIFT1)
    first_ref[...] = first
    first_half = first.astype(HALF)
    first_t_ref[...] = first_half.T
    for part in range(up_ref.shape[1] // wide):
        cols = slice(part * wide, (part + 1) * wide)
        inner = mult(first_half, up_ref[:, cols]) + up_b_ref[0:1, cols]
        active, slope = gelu_pair(inner)
        active = active.astype(HALF)
        active_ref[:, cols] = active
        active_t_ref[cols, :] = active.T
        slope_ref[:, cols] = slope.astype(HALF)


def block_specs():
    rows = lambda cols: pl.BlockSpec((BLOCK, cols), lambda i: (i, 0))
    flipped = lambda cols: pl.BlockSpec((cols, BLOCK), lambda i: (0, i))
    return rows, flipped


def feed_up(mixed, tokens, out_w, up, table, up_b):
    length, wide = tokens.shape
    inner = up.shape[1]
    rows, flipped = block_specs()
    weights = (out_w, up, table, up_b)
    return pl.pallas_call(
        feed_up_kernel,
        grid=(length // BLOCK,),
        in_specs=[rows(wide), rows(wide)] + memory([pltpu.VMEM] * len(weights)),
        out_specs=[rows(wide), flipped(wide), rows(inner), flipped(inner), rows(inner), rows(wide), rows(LANES)],
        out_shape=[
            struct((length, wide), FLOAT), struct((wide, length)), struct((length, inner)), struct((inner, length)),
            struct((length, inner)), struct((length, wide)), struct((length, LANES), FLOAT),
        ],
        compiler_params=params_of(("arbitrary",)),
        cost_estimate=LIGHT,
        name="feed_up",
    )(mixed, tokens, *weights)


def feed_down_kernel(
    first_ref, active_ref, down_ref, student_w_ref, pool_w_ref, table_ref, student_b_ref,
    hidden_ref, hidden_t_ref, unit2_ref, rate2_ref, student_t_ref, pool_ref,
):
    line = lambda which: table_ref[which : which + 1, :]
    total = first_ref[...] + line(DOWN_B) + mult(active_ref[...], down_ref[...])
    unit, rate = normalise(total)
    unit2_ref[...] = unit.astype(HALF)
    rate2_ref[...] = jnp.broadcast_to(rate, rate2_ref.shape)
    hidden = (unit * line(GAIN2) + line(SHIFT2)).astype(HALF)
    hidden_ref[...] = hidden
    hidden_t_ref[...] = hidden.T
    student = (mult(hidden, student_w_ref[...]) + student_b_ref[0:1, :]).astype(HALF)
    student_t_ref[...] = student.T
    pool_ref[...] = mult(student, pool_w_ref[...]).astype(HALF)


def feed_down(first, active, down, student_w, pool_w, table, student_b):
    length, wide = first.shape
    small = student_w.shape[1]
    rows, flipped = block_specs()
    weights = (down, student_w, pool_w, table, student_b)
    return pl.pallas_call(
        feed_down_kernel,
        grid=(length // BLOCK,),
        in_specs=[rows(wide), rows(active.shape[1])] + memory([pltpu.VMEM] * len(weights)),
        out_specs=[rows(wide), flipped(wide), rows(wide), rows(LANES), flipped(small), rows(3 * small)],
        out_shape=[
            struct((length, wide)), struct((wide, length)), struct((length, wide)), struct((length, LANES), FLOAT),
            struct((small, length)), struct((length, 3 * small)),
        ],
        compiler_params=params_of(("arbitrary",)),
        cost_estimate=LIGHT,
        name="feed_down",
    )(first, active, *weights)


def student_kernel(
    label_ref, cotangent_ref, pool_ref, unit2_ref, rate2_ref, student_w_ref, pool_w_ref, dense_ref, class_ref,
    small_b_ref, table_ref,
    logits_ref, grad_pool_ref, grad_student_ref, residual_ref, residual_half_ref, dense_grad_ref, class_grad_ref,
    small_sums_ref, sums_ref,
):
    length, three = pool_ref.shape
    small = three // 3
    scale = (small // POOL_HEADS) ** (-0.5)
    head_of = lambda axis: lax.broadcasted_iota(jnp.int32, (small, small), axis) // (small // POOL_HEADS)
    same = jnp.where(head_of(0) == head_of(1), 1.0, 0.0).astype(FLOAT)
    top = lax.broadcasted_iota(jnp.int32, (8, small), 0) == 0
    query = pool_ref[0:8, 0:small].astype(FLOAT)[0:1, :]
    key = pool_ref[:, small : 2 * small].astype(FLOAT)
    value = pool_ref[:, 2 * small : 3 * small].astype(FLOAT)
    scores = precise(key * query, same, (1, 0)) * scale
    raised = jnp.exp(scores - scores.max(axis=0, keepdims=True))
    weights = raised / raised.sum(axis=0, keepdims=True)
    pooled = (weights * value).sum(axis=0, keepdims=True)
    spread = lambda vector: jnp.where(top, vector, 0.0)
    dense = dense_ref[...].astype(FLOAT)
    classes = class_ref[...].astype(FLOAT)
    before = precise(spread(pooled), dense, (1, 0)) + small_b_ref[1:2, :]
    summary = jnp.tanh(before[0:1, :])
    logits = (precise(spread(summary), classes, (1, 0)) + small_b_ref[2:3, :])[0:1, :]
    lane = lax.broadcasted_iota(jnp.int32, (1, small), 1)
    real = small_b_ref[3:4, :] > 0.5
    masked = jnp.where(real, logits, MASKED_SCORE)
    lifted = jnp.where(real, jnp.exp(masked - masked.max(axis=1, keepdims=True)), 0.0)
    grad_logits = lifted / lifted.sum(axis=1, keepdims=True) - jnp.where(lane == label_ref[0], 1.0, 0.0)
    logits_ref[...] = logits[:, 0 : logits_ref.shape[1]]
    class_grad_ref[...] = precise(spread(summary), spread(grad_logits), (0, 0))
    grad_summary = precise(spread(grad_logits), classes, (1, 1))[0:1, :]
    grad_before = grad_summary * (1.0 - summary * summary)
    dense_grad_ref[...] = precise(spread(pooled), spread(grad_before), (0, 0))
    grad_pooled = precise(spread(grad_before), dense, (1, 1))[0:1, :]
    grad_weights = precise(value * grad_pooled, same, (1, 0))
    inner = (weights * grad_weights).sum(axis=0, keepdims=True)
    grad_scores = weights * (grad_weights - inner)
    grad_query = (grad_scores * key).sum(axis=0, keepdims=True) * scale
    first = lax.broadcasted_iota(jnp.int32, (length, small), 0) == 0
    grad_pool_ref[:, 0:small] = jnp.where(first, grad_query, 0.0).astype(HALF)
    grad_pool_ref[:, small : 2 * small] = (grad_scores * query * scale).astype(HALF)
    grad_pool_ref[:, 2 * small : 3 * small] = (weights * grad_pooled).astype(HALF)
    grad_student = mult_rt(grad_pool_ref[...], pool_w_ref[...])
    which = lax.broadcasted_iota(jnp.int32, (8, small), 0)
    student_sum = grad_student.sum(axis=0, keepdims=True)
    small_sums_ref[...] = jnp.where(
        which == 0, student_sum, jnp.where(which == 1, grad_before, jnp.where(which == 2, grad_logits, 0.0))
    )
    grad_student_ref[...] = grad_student.astype(HALF)

    sums_ref[...] = jnp.zeros_like(sums_ref)

    def one_block(block, _):
        rows = pl.ds(pl.multiple_of(block * BLOCK, BLOCK), BLOCK)
        grad = cotangent_ref[rows, :].astype(FLOAT) + mult_rt(grad_student_ref[rows, :], student_w_ref[...])
        unit = unit2_ref[rows, :].astype(FLOAT)
        residual = normalise_backward(grad * table_ref[GAIN2 : GAIN2 + 1, :], unit, rate2_ref[rows, 0:1])
        residual_ref[rows, :] = residual
        residual_half_ref[rows, :] = residual.astype(HALF)
        sums_ref[0:1, :] += (grad * unit).sum(axis=0, keepdims=True)
        sums_ref[1:2, :] += grad.sum(axis=0, keepdims=True)
        sums_ref[2:3, :] += residual.sum(axis=0, keepdims=True)
        return 0

    lax.fori_loop(0, length // BLOCK, one_block, 0)


def student_pass(label, cotangent, pool, unit2, rate2, student_w, pool_w, dense, classes, small_b, table, count):
    length, wide = cotangent.shape
    small = student_w.shape[1]
    struct = jax.ShapeDtypeStruct
    args = (cotangent, pool, unit2, rate2, student_w, pool_w, dense, classes, small_b, table)
    return pl.pallas_call(
        student_kernel,
        in_specs=memory([pltpu.SMEM] + [pltpu.VMEM] * len(args)),
        out_specs=memory([pltpu.VMEM] * 9),
        out_shape=[
            struct((1, count), FLOAT), struct((length, 3 * small), HALF), struct((length, small), HALF),
            struct((length, wide), FLOAT), struct((length, wide), HALF), struct((small, small), FLOAT),
            struct((small, small), FLOAT), struct((8, small), FLOAT), struct((8, wide), FLOAT),
        ],
        compiler_params=params_of(None),
        cost_estimate=LIGHT,
        name="student",
    )(label, *args)


def back_kernel(
    half_ref, residual_ref, slope_ref, unit1_ref, rate1_ref, down_ref, up_ref, out_w_ref, table_ref,
    inner_ref, residual1_ref, one_ref, mixed_ref, sums_ref, up_sums_ref,
):
    wide = residual_ref.shape[1]

    @pl.when(pl.program_id(0) == 0)
    def _():
        sums_ref[...] = jnp.zeros_like(sums_ref)
        up_sums_ref[...] = jnp.zeros_like(up_sums_ref)

    total = residual_ref[...]
    for part in range(up_ref.shape[1] // wide):
        cols = slice(part * wide, (part + 1) * wide)
        grad = mult_rt(half_ref[...], down_ref[cols, :]) * slope_ref[:, cols].astype(FLOAT)
        up_sums_ref[0:1, cols] += grad.sum(axis=0, keepdims=True)
        grad = grad.astype(HALF)
        inner_ref[:, cols] = grad
        total = total + mult_rt(grad, up_ref[:, cols])
    unit = unit1_ref[...].astype(FLOAT)
    residual = normalise_backward(total * table_ref[GAIN1 : GAIN1 + 1, :], unit, rate1_ref[:, 0:1])
    residual1_ref[...] = residual
    one = residual.astype(HALF)
    one_ref[...] = one
    mixed_ref[...] = mult_rt(one, out_w_ref[...]).astype(HALF)
    sums_ref[0:1, :] += (total * unit).sum(axis=0, keepdims=True)
    sums_ref[1:2, :] += total.sum(axis=0, keepdims=True)
    sums_ref[2:3, :] += residual.sum(axis=0, keepdims=True)


def back(half, residual, slope, unit1, rate1, down, up, out_w, table):
    length, wide = residual.shape
    inner = up.shape[1]
    rows = lambda cols: pl.BlockSpec((BLOCK, cols), lambda i: (i, 0))
    struct = jax.ShapeDtypeStruct
    weights = (down, up, out_w, table)
    return pl.pallas_call(
        back_kernel,
        grid=(length // BLOCK,),
        in_specs=[rows(wide), rows(wide), rows(inner), rows(wide), rows(LANES)] + memory([pltpu.VMEM] * len(weights)),
        out_specs=[rows(inner), rows(wide), rows(wide), rows(wide), whole((8, wide)), whole((8, inner))],
        out_shape=[
            struct((length, inner), HALF), struct((length, wide), FLOAT), struct((length, wide), HALF),
            struct((length, wide), HALF), struct((8, wide), FLOAT), struct((8, inner), FLOAT),
        ],
        compiler_params=params_of(("arbitrary",)),
        cost_estimate=LIGHT,
        name="back",
    )(half, residual, slope, unit1, rate1, *weights)


def input_kernel(grad_ref, residual_ref, weight_ref, out_ref):
    wide = residual_ref.shape[1]
    total = residual_ref[...]
    for part in range(3):
        total = total + mult_rt(grad_ref[part], weight_ref[:, part * wide : (part + 1) * wide])
    out_ref[...] = total


def input_pass(grad, residual, weight):
    length, wide = residual.shape
    return pl.pallas_call(
        input_kernel,
        grid=(length // BLOCK,),
        in_specs=[
            pl.BlockSpec((3, BLOCK, wide), lambda i: (0, i, 0)), pl.BlockSpec((BLOCK, wide), lambda i: (i, 0)),
            pl.BlockSpec(memory_space=pltpu.VMEM),
        ],
        out_specs=pl.BlockSpec((BLOCK, wide), lambda i: (i, 0)),
        out_shape=jax.ShapeDtypeStruct((length, wide), FLOAT),
        compiler_params=params_of(("arbitrary",)),
        cost_estimate=LIGHT,
        name="input_pass",
    )(grad, residual, weight)


def swap(value, axis, bits):
    size = lax.axis_size(axis)
    return lax.ppermute(value, axis, [(i, i ^ bits) for i in range(size)])


def around(value):
    return [value] + [swap(value, "replica", bits) for bits in (2, 4, 6)]


WIDE = 384
SMALL = (0, 128)
SMALL_ROWS = 16
VECTOR_ROWS = 32


def rows_of(mat):
    return SMALL_ROWS if mat == SMALL else mat[0] * mat[1] // 4


def all_rows(mats):
    return sum(rows_of(mat) for mat in mats)


def after(value, *others):
    return lax.optimization_barrier((value,) + others)[0]


FULL = 60 << 20


def vmem_call(kernel, name, where, inputs, outs, moved, scratch=(), limit=32 << 20):
    return pl.pallas_call(
        kernel,
        in_specs=memory([pltpu.SMEM] + [pltpu.VMEM] * len(inputs)),
        out_specs=memory([pltpu.VMEM] * len(outs)),
        out_shape=outs,
        scratch_shapes=list(scratch),
        compiler_params=params_of(None, limit),
        cost_estimate=LIGHT,
        name=name,
    )(where, *inputs)


def struct(shape, kind=HALF):
    return jax.ShapeDtypeStruct(shape, kind)


def aligned(begin, rows):
    return pl.ds(pl.multiple_of(begin, rows), rows)


def small_places(student_rows):
    third = student_rows // 3
    return third, third + 32


def fold_small(block_ref, base, student_ref, pool_ref, dense_ref, class_ref):
    third, last = small_places(student_ref.shape[0])
    for part in range(3):
        block_ref[base : base + third, part * LANES : (part + 1) * LANES] = student_ref[part * third : (part + 1) * third, :]
    block_ref[base + third : base + last, :] = pool_ref[...]
    rest = slice(base + last, base + 128)
    block_ref[rest, :] = jnp.zeros((128 - last, WIDE), block_ref.dtype)
    block_ref[rest, 0:LANES] = dense_ref[...]
    block_ref[rest, LANES : LANES + class_ref.shape[1]] = class_ref[...]


def unfold_small(block_ref, shard, student_ref, pool_ref, dense_ref, class_ref, rows):
    third, last = small_places(rows)
    base, short = shard * 128, 128 - last
    for part in range(3):
        begin = shard * rows + part * third
        student_ref[begin : begin + third, :] = block_ref[base : base + third, part * LANES : (part + 1) * LANES].astype(student_ref.dtype)
    target = slice(shard * short, (shard + 1) * short)
    pool_ref[target, :] = block_ref[base + third : base + last, :].astype(pool_ref.dtype)
    dense_ref[target, :] = block_ref[base + last : base + 128, 0:LANES].astype(dense_ref.dtype)
    classes = class_ref.shape[1]
    class_ref[target, :] = block_ref[base + last : base + 128, LANES : LANES + classes].astype(class_ref.dtype)


def pack_kernel(place_ref, *refs, mats, lines):
    chip, core = place_ref[1], place_ref[2]
    piece_ref = refs[-1]
    offset = 0
    if lines:
        base = all_rows(mats)
        for half in range(2):
            piece_ref[base : base + 16, half * LANES : (half + 1) * LANES] = refs[-2][half * 16 : half * 16 + 16, :]
        piece_ref[base : base + 16, 2 * LANES :] = jnp.zeros((16, WIDE - 2 * LANES), HALF)
    for mat, ref in zip(mats, refs):
        if mat == SMALL:
            small_ref = refs[-2]
            fold_small(small_ref, 0, *refs[len(mats) - 1 : len(mats) + 3])
            piece_ref[offset : offset + SMALL_ROWS, :] = small_ref[aligned((chip * 2 + core) * SMALL_ROWS, SMALL_ROWS), :]
            continue
        rows = mat[1] // 4
        for chunk in range(mat[0]):
            lanes = aligned(chunk * 2 * WIDE + core * WIDE, WIDE)
            piece_ref[offset : offset + rows, :] = ref[aligned(chip * rows, rows), lanes]
            offset += rows


def pack(where, shards, mats, lines=None):
    outs = [struct((all_rows(mats) + (0 if lines is None else 16), WIDE))]
    shards = list(shards) + ([] if lines is None else [lines])
    if SMALL in mats:
        outs = [struct(SMALL[1:] + (WIDE,))] + outs
    return vmem_call(partial(pack_kernel, mats=mats, lines=lines is not None), "pack", where, shards, outs, 2 * sum(s.size for s in shards), limit=FULL)


def put_piece(out_ref, ref, step, offset, base, mat, chip, core):
    if mat == SMALL:
        target = aligned(base + (chip * 2 + core) * SMALL_ROWS, SMALL_ROWS)
        out_ref[target, :] = ref[step, offset : offset + SMALL_ROWS, :].astype(out_ref.dtype)
        return
    rows = mat[1] // 4
    for chunk in range(mat[0]):
        lanes = aligned(chunk * 2 * WIDE + core * WIDE, WIDE)
        first = offset + chunk * rows
        out_ref[aligned(base + chip * rows, rows), lanes] = ref[step, first : first + rows, :].astype(out_ref.dtype)


def place_kernel(place_ref, *refs, mats, rows):
    shard, chip, core = place_ref[0], place_ref[1], place_ref[2]
    count = len(mats)
    pieces, owns, outs = refs[:8], refs[8 : 8 + count], list(refs[8 + count :])
    if SMALL in mats:
        block_ref = outs.pop()
        smalls, outs = outs[count - 1 :], outs[: count - 1] + [block_ref]
    offset = 0
    for mat, own_ref, out_ref in zip(mats, owns, outs):
        height = mat[1]
        out_ref[aligned(shard * height, height), :] = own_ref[...]
        for number, ref in enumerate(pieces):
            far, other = number // 2, number % 2
            for step in range(ref.shape[0]):
                base = (shard ^ (step + 1)) * height
                put_piece(out_ref, ref, step, offset, base, mat, chip ^ far, core ^ other)
        offset += rows_of(mat)
    if SMALL in mats:
        for step in range(pieces[0].shape[0] + 1):
            unfold_small(block_ref, step, *smalls, rows)


def place(where, pieces, owns, outs, mats, rows=0):
    shards = pieces[0].shape[0] + 1
    scratch = [pltpu.VMEM((shards * SMALL[1], WIDE), HALF)] if SMALL in mats else []
    moved = 4 * shards * sum(own.size for own in owns)
    return vmem_call(partial(place_kernel, mats=mats, rows=rows), "place", where, pieces + list(owns), outs, moved, scratch)


def table_kernel(place_ref, *refs, classes, base):
    *lines, table_ref, up_ref, short_ref, stack_ref = refs
    shard = place_ref[0]
    wide, inner = table_ref.shape[1], up_ref.shape[1]
    shards = len(lines)
    ups = inner // shards // LANES
    table = jnp.zeros(table_ref.shape, FLOAT)
    shorts = jnp.zeros((8, LANES), FLOAT)
    for step, ref in enumerate(lines):
        target = shard ^ step
        if step == 0:
            block = ref[...].astype(FLOAT)
        else:
            stack_ref[step - 1] = ref[...]
            block = jnp.concatenate([ref[base : base + 16, half * LANES : half * LANES + LANES] for half in range(2)], axis=0)
            block = block.astype(FLOAT)
        both = jnp.concatenate([block[0:8], block[8:16], jnp.zeros((8, wide - 2 * LANES), FLOAT)], axis=1)
        table = table + pltpu.roll(both, target * (wide // shards), 1)
        for line in range(ups):
            row = block[16 + line : 17 + line]
            up_ref[:, aligned(target * (inner // shards) + line * LANES, LANES)] = jnp.broadcast_to(row, (8, LANES))
        shorts = shorts + pltpu.roll(block[16 : 24], target * (LANES // shards), 1)
    table_ref[...] = table
    lane = lax.broadcasted_iota(jnp.int32, (1, LANES), 1)
    short_ref[0:2, :] = shorts[6:8]
    short_ref[2:3, :] = lines[0][...].astype(FLOAT)[24:25]
    short_ref[3:4, :] = jnp.where(lane < classes, 1.0, 0.0)
    short_ref[4:8, :] = jnp.zeros((4, LANES), FLOAT)


def lines_kernel(place_ref, *refs):
    *vectors, up_ref, student_ref, dense_ref, class_ref, out_ref, full_ref = refs
    full_ref[...] = jnp.zeros_like(full_ref)

    def put(row, value):
        full_ref[row : row + 1, 0 : value.shape[0]] = value.astype(FLOAT).reshape(1, value.shape[0])

    for line, ref in enumerate(vectors):
        put(line, ref[0:LANES])
        put(8 + line, ref[LANES:])
    for line in range(up_ref.shape[0] // LANES):
        put(16 + line, up_ref[line * LANES : (line + 1) * LANES])
    put(22, student_ref[...])
    put(23, dense_ref[...])
    put(24, class_ref[...])
    out_ref[...] = full_ref[...].astype(HALF)


def vector_lines(where, vectors, up_bias, shorts, class_bias):
    inputs = [*vectors, up_bias, *shorts, class_bias]
    (lines,) = vmem_call(lines_kernel, "lines", where, inputs, [struct((32, LANES))], 0, [pltpu.VMEM((32, LANES), FLOAT)], FULL)
    return lines


def from_shards(value):
    return [swap(value, "shard", bits) for bits in range(1, lax.axis_size("shard"))]


def both_cores(values):
    return [piece for value in values for piece in (value, swap(value, "replica", 1))]


def weight_grad_kernel(place_ref, left_ref, right_ref, send_ref, keep_ref):
    core = place_ref[2]
    left = left_ref[...]
    for chunk in range(send_ref.shape[0]):
        for ref, which in ((send_ref, 1 - core), (keep_ref, core)):
            if len(right_ref.shape) == 3:
                right = right_ref[chunk, :, aligned(which * WIDE, WIDE)]
            else:
                right = right_ref[:, aligned(chunk * 2 * WIDE + which * WIDE, WIDE)]
            ref[chunk] = mult(left, right).astype(HALF)


def weight_grad(where, left, right, name, block=256):
    height, length = left.shape
    chunks = right.shape[0] if right.ndim == 3 else right.shape[1] // (2 * WIDE)
    out = struct((chunks, height, WIDE))
    return pl.pallas_call(
        weight_grad_kernel,
        grid=(height // block,),
        in_specs=[pl.BlockSpec(memory_space=pltpu.SMEM), pl.BlockSpec((block, length), lambda i: (i, 0))]
        + memory([pltpu.VMEM]),
        out_specs=[pl.BlockSpec((chunks, block, WIDE), lambda i: (0, i, 0))] * 2,
        out_shape=[out, out],
        compiler_params=params_of(("arbitrary",)),
        cost_estimate=LIGHT,
        name=name,
    )(where, left, right)


def small_grad_kernel(place_ref, hidden_ref, grad_student_ref, student_ref, grad_pool_ref, dense_ref, class_ref, send_ref, keep_ref, block_ref, first_ref, pool_ref):
    core = place_ref[2]
    shards = send_ref.shape[1] // (4 * SMALL_ROWS)
    first_ref[...] = mult(hidden_ref[...], grad_student_ref[...])
    pool_ref[...] = mult(student_ref[...], grad_pool_ref[...])
    part = lambda ref, shard: ref.at[pl.ds(shard * (ref.shape[0] // shards), ref.shape[0] // shards)]
    for shard in range(shards):
        fold_small(block_ref, shard * 128, *(part(ref, shard) for ref in (first_ref, pool_ref, dense_ref, class_ref)))
    for shard in range(shards):
        for chip in range(4):
            target = pl.ds((shard * 4 + chip) * SMALL_ROWS, SMALL_ROWS)
            for ref, which in ((send_ref, 1 - core), (keep_ref, core)):
                ref[0, target, :] = block_ref[aligned(shard * 128 + (chip * 2 + which) * SMALL_ROWS, SMALL_ROWS), :].astype(HALF)


def small_grad(where, hidden, grad_student, student, grad_pool, dense, classes, shards):
    outs = [struct((1, shards * 4 * SMALL_ROWS, WIDE))] * 2
    scratch = [
        pltpu.VMEM((shards * 128, WIDE), FLOAT), pltpu.VMEM((hidden.shape[0], LANES), FLOAT), pltpu.VMEM((LANES, WIDE), FLOAT)
    ]
    inputs = [hidden, grad_student, student, grad_pool, dense, classes]
    return vmem_call(small_grad_kernel, "small_grad", where, inputs, outs, 4 * hidden.size, scratch)


def vector_kernel(place_ref, heads_ref, one_ref, two_ref, up_ref, short_ref, half_ref, out_ref):
    half = heads_ref.shape[1] // 2
    for side in range(2):
        lanes = slice(side * half, (side + 1) * half)
        lines = [heads_ref[0:1, lanes], heads_ref[1:2, lanes], one_ref[2:3, lanes], one_ref[0:1, lanes], one_ref[1:2, lanes]]
        lines += [two_ref[2:3, lanes], two_ref[0:1, lanes], two_ref[1:2, lanes]]
        for row, line in enumerate(lines):
            out_ref[side * 8 + row : side * 8 + row + 1, :] = line
    for row in range(up_ref.shape[1] // WIDE):
        out_ref[16 + row : 17 + row, :] = up_ref[0:1, row * WIDE : (row + 1) * WIDE]
    out_ref[24:32, :] = jnp.zeros((8, WIDE), FLOAT)
    for part in range(3):
        out_ref[24:25, part * LANES : (part + 1) * LANES] = short_ref[part : part + 1, :]
    half_ref[...] = out_ref[...].astype(HALF)


def split_kernel(place_ref, *refs, count, shards, vectors):
    chip = place_ref[1]
    keeps, recvs, outs = refs[:count], refs[count : 2 * count], refs[-4:]
    total = sum(keep.shape[0] * keep.shape[1] for keep in keeps) // (4 * shards)
    offset = 0
    for keep_ref, recv_ref in zip(keeps, recvs):
        height = keep_ref.shape[1] // shards
        rows = height // 4
        for chunk in range(keep_ref.shape[0]):
            for shard in range(shards):
                for far, out_ref in enumerate(outs):
                    source = aligned(shard * height + (chip ^ far) * rows, rows)
                    value = keep_ref[chunk, source, :].astype(FLOAT) + recv_ref[chunk, source, :].astype(FLOAT)
                    first = shard * total + offset
                    out_ref[first : first + rows, :] = value.astype(HALF)
            offset += rows
    if vectors:
        value = (refs[2 * count][...].astype(FLOAT) + refs[2 * count + 1][...].astype(FLOAT)).astype(HALF)
        for out_ref in outs:
            out_ref[shards * total : shards * total + VECTOR_ROWS, :] = value


def split(where, keeps, recvs, shards, vectors=()):
    total = sum(keep.shape[0] * keep.shape[1] for keep in keeps) // 4 + (VECTOR_ROWS if vectors else 0)
    kernel = partial(split_kernel, count=len(keeps), shards=shards, vectors=bool(vectors))
    inputs = list(keeps) + list(recvs) + list(vectors)
    return vmem_call(kernel, "split", where, inputs, [struct((total, WIDE))] * 4, 20 * total * WIDE)


def merge_kernel(place_ref, *refs, shards, vectors):
    shard = place_ref[0]
    parts, outs = refs[: -shards], refs[-shards:]
    offset = 0
    for group in range(len(parts) // 4):
        four = parts[4 * group : 4 * group + 4]
        last = vectors and group == len(parts) // 4 - 1
        rows = (four[0].shape[0] - (VECTOR_ROWS if last else 0)) // shards

        def total(source):
            a, b, c, d = (ref[source, :].astype(FLOAT) for ref in four)
            return ((a + b) + (c + d)).astype(HALF)

        for step, out_ref in enumerate(outs):
            out_ref[offset : offset + rows, :] = total(aligned((shard ^ step) * rows, rows))
        offset += rows
        if last:
            value = total(slice(shards * rows, shards * rows + VECTOR_ROWS))
            for out_ref in outs:
                out_ref[offset : offset + VECTOR_ROWS, :] = value


def merge(where, groups, shards, vectors=False):
    extra = VECTOR_ROWS if vectors else 0
    rows = (sum(four[0].shape[0] for four in groups) - extra) // shards + extra
    kernel = partial(merge_kernel, shards=shards, vectors=vectors)
    inputs = [part for four in groups for part in four]
    return vmem_call(kernel, "merge", where, inputs, [struct((rows, WIDE))] * shards, 10 * shards * rows * WIDE)


def total_kernel(place_ref, *refs, shards):
    parts, outs = refs[:shards], refs[shards:]
    offset = 0
    for out_ref in outs:
        rows = slice(offset, offset + out_ref.shape[0])
        terms = [ref[rows, :].astype(FLOAT) for ref in parts]
        while len(terms) > 1:
            half = len(terms) // 2
            terms = [terms[i] + terms[i + half] for i in range(half)]
        out_ref[...] = terms[0].astype(HALF)
        offset += out_ref.shape[0]


def total(where, parts, vectors=False):
    rows = parts[0].shape[0] - (VECTOR_ROWS if vectors else 0)
    outs = [struct((rows, WIDE))] + ([struct((VECTOR_ROWS, WIDE))] if vectors else [])
    outs = vmem_call(partial(total_kernel, shards=len(parts)), "total", where, parts, outs, 10 * rows * WIDE)
    bits = 8
    while bits < lax.axis_size("replica"):
        outs = [(v.astype(FLOAT) + swap(v, "replica", bits).astype(FLOAT)).astype(HALF) for v in outs]
        bits *= 2
    return outs


def finish_kernel(place_ref, *refs, mats, rows):
    chip, core = place_ref[1], place_ref[2]
    pieces, outs = refs[:8], list(refs[8:])
    if SMALL in mats:
        block_ref = outs.pop()
        smalls, outs = outs[len(mats) - 1 :], outs[: len(mats) - 1] + [block_ref]
    offset = 0
    for mat, out_ref in zip(mats, outs):
        for number, ref in enumerate(pieces):
            put_piece(out_ref, ref, 0, offset, 0, mat, chip ^ (number // 2), core ^ (number % 2))
        offset += rows_of(mat)
    if SMALL in mats:
        unfold_small(block_ref, 0, *smalls, rows)


def finish(where, pieces, mats, outs, rows=0):
    pieces = [piece[None] for piece in pieces]
    scratch = [pltpu.VMEM(SMALL[1:] + (WIDE,), FLOAT)] if SMALL in mats else []
    moved = 6 * sum(out.size for out in outs)
    return vmem_call(partial(finish_kernel, mats=mats, rows=rows), "finish", where, pieces, outs, moved, scratch)


def vector_out_kernel(place_ref, total_ref, *refs):
    tables, up_ref, shorts, class_ref = refs[:8], refs[8], refs[9:11], refs[11]
    shard = place_ref[0]
    wide = 2 * WIDE
    each = tables[0].shape[0]
    shards = wide // each
    values = total_ref[...].astype(FLOAT)
    table = jnp.concatenate([values[0:8], values[8:16]], axis=1)
    table = pltpu.roll(table, (shards - shard) * each, 1)[:, :each]
    for line, ref in enumerate(tables):
        ref[...] = table[line : line + 1].reshape(each)
    lines = up_ref.shape[0] // WIDE
    for line in range(lines):
        row = jnp.zeros((1, WIDE), FLOAT)
        for which in range(shards):
            row = row + jnp.where(shard == which, values[16 + which * lines + line : 17 + which * lines + line], 0.0)
        up_ref[line * WIDE : (line + 1) * WIDE] = row.reshape(WIDE)
    each = shorts[0].shape[0]
    for part, ref in enumerate(shorts):
        row = pltpu.roll(values[24:32, part * LANES : (part + 1) * LANES], (shards - shard) * each, 1)
        ref[...] = row[0:1, :each].reshape(each)
    class_ref[...] = values[24:25, 2 * LANES : 2 * LANES + class_ref.shape[0]].reshape(class_ref.shape[0])


def vector_out(where, value, shards, inner, classes):
    outs = [struct((2 * WIDE // shards,), FLOAT)] * 8 + [struct((inner // shards,), FLOAT)]
    outs += [struct((LANES // shards,), FLOAT)] * 2 + [struct((classes,), FLOAT)]
    return vmem_call(vector_out_kernel, "vector_out", where, [value], outs, 4 * value.size)


def body(
    tokens, cotangent, piece_starts, labels, qkv_weight, query_bias, value_bias, out_weight, out_bias, attention_gain,
    attention_shift, up_weight, up_bias, down_weight, down_bias, feed_gain, feed_shift, student_weight, student_bias,
    pool_weight, dense_weight, dense_bias, class_weight, class_bias,
):
    count, length, wide = tokens.shape
    inner = up_weight.shape[1]
    classes = class_weight.shape[1]
    student_rows = student_weight.shape[0]
    shards = lax.axis_size("shard")
    replica = lax.axis_index("replica")
    where = jnp.stack([lax.axis_index("shard"), (replica >> 1) & 3, replica & 1]).astype(jnp.int32)
    tokens, cotangent = tokens.reshape(length, wide), cotangent.reshape(length, wide)
    qkv_mats = ((3, qkv_weight.shape[0]),)
    up_mats = ((1, out_weight.shape[0]), (4, up_weight.shape[0]))
    down_mats = ((1, down_weight.shape[0]), SMALL)

    (piece,) = pack(where, [qkv_weight], qkv_mats)
    near = from_shards(piece)
    lines = vector_lines(
        where,
        [after(query_bias, piece), value_bias, out_bias, attention_gain, attention_shift, down_bias, feed_gain, feed_shift],
        up_bias, [student_bias, dense_bias], class_bias,
    )
    (up_piece,) = pack(where, [out_weight, up_weight], up_mats, lines)
    small, down_piece = pack(
        where, [after(down_weight, piece), student_weight, pool_weight, dense_weight, class_weight], down_mats
    )
    tokens_t = flip(after(tokens, piece))
    near[0], up_piece, small, down_piece, tokens_t = lax.optimization_barrier((near[0], up_piece, small, down_piece, tokens_t))
    near_stack = jnp.stack(near)
    qkv_around = around(near_stack)
    up_near = [swap(up_piece, "shard", bits) for bits in range(1, shards - 1)]
    up_near.append(swap(after(up_piece, up_near[0]), "shard", shards - 1))
    qkv_around[1], *up_near[:-1] = lax.optimization_barrier((qkv_around[1], *up_near[:-1]))
    qkv_pieces = both_cores(qkv_around)
    qkv_pieces[0], up_near[-1] = lax.optimization_barrier((qkv_pieces[0], up_near[-1]))
    (qkv,) = place(where, qkv_pieces, [qkv_weight], [struct((shards * qkv_weight.shape[0], 3 * wide))], qkv_mats)
    up_near[0] = after(up_near[0], qkv)
    table, up_b, small_b, up_stack = vmem_call(
        partial(table_kernel, classes=classes, base=all_rows(up_mats)), "table", where, [lines] + up_near,
        [
            struct((8, wide), FLOAT), struct((8, inner), FLOAT), struct((8, LANES), FLOAT),
            struct((shards - 1,) + up_piece.shape),
        ],
        8 * 8 * inner,
    )
    down_piece = after(down_piece, up_stack)
    up_around = around(up_stack)
    down_near = [swap(down_piece, "shard", bits) for bits in range(1, shards - 1)]
    qkv = after(qkv, up_stack)
    joined = project(tokens, qkv, table)
    joined, down_piece, down_near[0] = lax.optimization_barrier((joined, down_piece, down_near[0]))
    down_near.append(swap(down_piece, "shard", shards - 1))
    mixed, mixed_t, lse = attend_forward(joined, piece_starts)
    whole_of = lambda shard: struct((shards * shard.shape[0], shard.shape[1]))
    mixed, *arrived = lax.optimization_barrier((mixed, *down_near, *up_around))
    down_near, up_around = arrived[: shards - 1], arrived[shards - 1 :]
    down_stack = jnp.stack(down_near)
    down_around = around(after(down_stack, mixed))
    out_w, up = place(
        where, both_cores(up_around), [out_weight, up_weight], [whole_of(out_weight), whole_of(up_weight)], up_mats
    )

    first, first_t, active, active_t, slope, unit1, rate1 = feed_up(
        mixed, tokens, after(out_w, down_stack), up, table, up_b
    )
    rest = [whole_of(s) for s in (down_weight, student_weight, pool_weight, dense_weight)]
    rest.append(struct((shards * class_weight.shape[0], LANES)))
    active, *down_around = lax.optimization_barrier((active, *down_around))
    down, student_w, pool_w, dense_w, class_w = place(
        where, both_cores(down_around), [down_weight, small], rest, down_mats, student_rows
    )
    hidden, hidden_t, unit2, rate2, student_t, pool = feed_down(
        first, active, down, student_w, pool_w, table, small_b
    )
    logits, grad_pool, grad_student, residual2, half2, grad_dense, grad_class, small_sums, sums2 = student_pass(
        labels, cotangent, pool, unit2, rate2, student_w, pool_w, dense_w, class_w, small_b, table, classes
    )
    core_swap = lambda value: swap(value, "replica", 1)
    exchange = lambda parts: [parts[0]] + [swap(part, "replica", 2 * far) for far, part in enumerate(parts) if far > 0]
    spread = lambda parts: [parts[0]] + [swap(part, "shard", far) for far, part in enumerate(parts) if far > 0]
    send_down, keep_down = weight_grad(where, active_t, half2, "grad_down")
    send_small, keep_small = small_grad(
        where, after(hidden_t, send_down), grad_student, student_t, grad_pool, grad_dense, grad_class, shards
    )
    parts_a = split(where, [after(keep_down, keep_small)], [core_swap(send_down)], shards)
    exchanged_a = exchange(parts_a)
    grad_inner, residual1, half1, grad_mixed, sums1, up_sums = back(
        after(half2, parts_a[0], keep_small), residual2, slope, unit1, rate1, down, up, out_w, table
    )
    send_up, keep_up = weight_grad(where, first_t, grad_inner, "grad_up")
    swapped_small = core_swap(send_small)
    send_up, mixed_t, swapped_small, *exchanged_a = lax.optimization_barrier((send_up, mixed_t, swapped_small, *exchanged_a))
    send_out, keep_out = weight_grad(where, mixed_t, half1, "grad_out")
    parts_b = split(where, [keep_out, keep_up], [core_swap(send_out), core_swap(send_up)], shards)
    exchanged_b = exchange(parts_b)
    heads, head_sums = attend_backward(joined, piece_starts, mixed, after(grad_mixed, parts_b[0]), lse)
    send_qkv, keep_qkv = weight_grad(where, tokens_t, heads, "grad_qkv")
    send_qkv, *exchanged_b = lax.optimization_barrier((send_qkv, *exchanged_b))
    ready = merge(where, [exchanged_b, exchanged_a], shards)
    near_ab = spread(ready)
    keep_qkv = after(keep_qkv, ready[0])
    (vectors,) = vmem_call(
        vector_kernel, "vectors", where,
        [head_sums, sums1, sums2, up_sums, small_sums], [struct((VECTOR_ROWS, WIDE))], 4 * VECTOR_ROWS * WIDE,
        [pltpu.VMEM((VECTOR_ROWS, WIDE), FLOAT)],
    )
    parts_c = split(
        where, [keep_qkv, keep_small], [core_swap(send_qkv), swapped_small], shards, (vectors, core_swap(vectors))
    )
    exchanged_c = exchange(parts_c)
    input_grad = input_pass(after(heads, parts_c[0]), residual1, qkv)
    near_ab[0] = after(near_ab[0], input_grad)
    (piece_ab,) = total(where, near_ab)
    piece_ab, *exchanged_c = lax.optimization_barrier((piece_ab, *exchanged_c))
    ready = merge(where, [exchanged_c], shards, True)
    near_c = spread(ready)
    around_ab = around(after(piece_ab, ready[0]))
    arrived = lax.optimization_barrier((*near_c, *around_ab))
    near_c, around_ab = arrived[: len(near_c)], arrived[len(near_c) :]
    pieces_ab = []
    for place_in_plane, value in enumerate(around_ab):
        if place_in_plane > 1:
            value = after(value, pieces_ab[2 * place_in_plane - 3])
        pieces_ab += [value, core_swap(value)]
    piece_c, vectors = total(where, near_c, True)
    around_c = around(piece_c)
    full = lambda shard: struct(shard.shape, FLOAT)
    ab_mats = up_mats + down_mats[:1]
    grad_out, grad_up, grad_down = finish(
        where, pieces_ab, ab_mats, [full(s) for s in (out_weight, up_weight, down_weight)]
    )
    around_c[-1] = after(around_c[-1], grad_out)
    pieces_c = both_cores(around_c)
    *g_table, g_up_b, g_student_b, g_dense_b, g_class_b = vector_out(where, vectors, shards, inner, classes)
    grad_qkv, g_student, g_pool, g_dense, g_class = finish(
        where, pieces_c, qkv_mats + (SMALL,),
        [full(s) for s in (qkv_weight, student_weight, pool_weight, dense_weight, class_weight)], student_rows,
    )
    return (
        hidden.reshape(count, length, wide), logits, input_grad.reshape(count, length, wide),
        grad_qkv, g_table[0], g_table[1], grad_out, g_table[2], g_table[3], g_table[4], grad_up, g_up_b, grad_down,
        g_table[5], g_table[6], g_table[7], g_student, g_student_b, g_pool, g_dense, g_dense_b, g_class, g_class_b,
    )


def solution(mesh):
    placed = (
        P(("shard", "replica"), None, None),
        P(("shard", "replica"), None, None),
        P(("shard", "replica"), None),
        P(("shard", "replica")),
        P("shard", None),
        P("shard"),
        P("shard"),
        P("shard", None),
        P("shard"),
        P("shard"),
        P("shard"),
        P("shard", None),
        P("shard"),
        P("shard", None),
        P("shard"),
        P("shard"),
        P("shard"),
        P("shard", None),
        P("shard"),
        P("shard", None),
        P("shard", None),
        P("shard"),
        P("shard", None),
        P(),
    )
    return jax.shard_map(
        body,
        mesh=mesh,
        in_specs=placed,
        out_specs=(
            P(("shard", "replica"), None, None),
            P(("shard", "replica"), None),
            P(("shard", "replica"), None, None),
            P("shard", None),
            P("shard"),
            P("shard"),
            P("shard", None),
            P("shard"),
            P("shard"),
            P("shard"),
            P("shard", None),
            P("shard"),
            P("shard", None),
            P("shard"),
            P("shard"),
            P("shard"),
            P("shard", None),
            P("shard"),
            P("shard", None),
            P("shard", None),
            P("shard"),
            P("shard", None),
            P(),
        ),
        check_vma=False,
    )
```

```python
from functools import partial

import jax
import jax.numpy as jnp
from jax import lax
from jax.experimental import pallas as pl
from jax.experimental.pallas import tpu as pltpu
from jax.sharding import PartitionSpec as P

HEADS = 12
POOL_HEADS = 2
PIECE = 256
NORM_EPS = 1e-06
MASKED_SCORE = -1e30
FLOAT = jnp.float32
HALF = jnp.bfloat16
PRECISE = lax.Precision.HIGHEST
LANES = 128
BLOCK = 256

ERF_SLOPE = 0.42
ERF_TERMS = (
    0.23691840576326206,
    0.2382680869907842,
    0.20182398814655725,
    0.2493386597508521,
    -0.10108083678814953,
    0.4156989047782712,
    -0.3092846516362072,
    0.06831743518928779,
)


LIGHT = pl.CostEstimate(flops=100000, transcendentals=0, bytes_accessed=100000)


def params_of(kinds, limit=44 << 20):
    return pltpu.CompilerParams(dimension_semantics=kinds, vmem_limit_bytes=limit)


def whole(shape, space=None):
    return pl.BlockSpec(shape, lambda *_: (0,) * len(shape))


def memory(kinds):
    return [pl.BlockSpec(memory_space=kind) for kind in kinds]


def mult(left, right):
    return jnp.dot(left, right, preferred_element_type=FLOAT)


def mult_rt(left, right):
    return lax.dot_general(left, right, (((1,), (1,)), ((), ())), preferred_element_type=FLOAT)


def mult_lt(left, right):
    return lax.dot_general(left, right, (((0,), (0,)), ((), ())), preferred_element_type=FLOAT)


def precise(left, right, dims):
    return lax.dot_general(
        left, right, ((dims[:1], dims[1:]), ((), ())), precision=PRECISE, preferred_element_type=FLOAT
    )


def key_extent(block, length):
    return min(length, (block + 2) * BLOCK)


def allowed_block(starts_ref, first_row, first_col, shape, row_axis):
    rows = first_row + lax.broadcasted_iota(jnp.int32, shape, row_axis)
    cols = first_col + lax.broadcasted_iota(jnp.int32, shape, 1 - row_axis)
    allowed = cols <= rows
    for piece in range(starts_ref.shape[1]):
        start = starts_ref[0, piece]
        inside = (rows >= start) & (rows < start + PIECE) & (cols >= start) & (cols < start + PIECE)
        allowed = allowed | inside
    return allowed


def fill_bias(starts_ref, bias_ref, length, row_axis):
    for block in range(length // BLOCK):
        wide = key_extent(block, length) - block * BLOCK
        shape = (BLOCK, wide) if row_axis == 0 else (wide, BLOCK)
        allowed = allowed_block(starts_ref, block * BLOCK, block * BLOCK, shape, row_axis)
        bias = jnp.where(allowed, 0.0, MASKED_SCORE).astype(FLOAT)
        if row_axis == 0:
            bias_ref[block, :, 0:wide] = bias
        else:
            bias_ref[block, 0:wide, :] = bias


def half_lanes(value, half):
    lane = lax.broadcasted_iota(jnp.int32, value.shape, 1)
    keep = (lane < LANES // 2) if half == 0 else (lane >= LANES // 2)
    return jnp.where(keep, value, jnp.zeros_like(value))


def attend_forward_kernel(starts_ref, q_ref, k_ref, v_ref, mixed_ref, flipped_ref, lse_ref, bias_ref):
    length = q_ref.shape[0]
    scale = (LANES // 2) ** (-0.5)

    @pl.when(pl.program_id(0) == 0)
    def _():
        fill_bias(starts_ref, bias_ref, length, 0)

    values = [half_lanes(v_ref[...], half) for half in range(2)]
    lane = lax.broadcasted_iota(jnp.int32, (BLOCK, LANES), 1)
    for block in range(length // BLOCK):
        begin = block * BLOCK
        extent = key_extent(block, length)
        query = q_ref[begin : begin + BLOCK, :] * jnp.asarray(scale, HALF)
        outs = []
        logs = []
        for half in range(2):
            scores = mult_rt(half_lanes(query, half), k_ref[0:extent, :])
            edge = scores[:, begin:extent] + bias_ref[block, :, 0 : extent - begin]
            parts = [edge] if begin == 0 else [scores[:, 0:begin], edge]
            ceiling = parts[0].max(axis=1, keepdims=True)
            for part in parts[1:]:
                ceiling = jnp.maximum(ceiling, part.max(axis=1, keepdims=True))
            total = 0.0
            mixed = 0.0
            place = 0
            for part in parts:
                raised = jnp.exp(part - ceiling)
                total = total + raised.sum(axis=1, keepdims=True)
                mixed = mixed + mult(
                    raised.astype(HALF), values[half][place : place + part.shape[1], :]
                )
                place += part.shape[1]
            outs.append(mixed / total)
            logs.append(ceiling + jnp.log(total))
        rounded = (outs[0] + outs[1]).astype(HALF)
        mixed_ref[begin : begin + BLOCK, :] = rounded
        flipped_ref[:, begin : begin + BLOCK] = rounded.T
        both = jnp.where(lane == 0, logs[0], logs[1])
        lse_ref[:, begin : begin + BLOCK] = both.T[0:8, :]


def attend_forward(joined, starts):
    length, wide = joined.shape
    pairs = wide // 3 // LANES
    return pl.pallas_call(
        attend_forward_kernel,
        grid=(pairs,),
        in_specs=[
            pl.BlockSpec(memory_space=pltpu.SMEM),
            pl.BlockSpec((length, LANES), lambda h: (0, h)),
            pl.BlockSpec((length, LANES), lambda h: (0, pairs + h)),
            pl.BlockSpec((length, LANES), lambda h: (0, 2 * pairs + h)),
        ],
        out_specs=[
            pl.BlockSpec((length, LANES), lambda h: (0, h)),
            pl.BlockSpec((LANES, length), lambda h: (h, 0)),
            pl.BlockSpec((8, length), lambda h: (h, 0)),
        ],
        out_shape=[
            jax.ShapeDtypeStruct((length, wide // 3), HALF),
            jax.ShapeDtypeStruct((wide // 3, length), HALF),
            jax.ShapeDtypeStruct((pairs * 8, length), FLOAT),
        ],
        scratch_shapes=[pltpu.VMEM((length // BLOCK, BLOCK, 2 * BLOCK), FLOAT)],
        compiler_params=params_of(("arbitrary",)),
        cost_estimate=LIGHT,
        name="attend_forward",
    )(starts, joined, joined, joined)


def attend_backward_kernel(
    starts_ref, q_ref, k_ref, v_ref, mixed_ref, grad_ref, lse_ref, out_ref, sums_ref, bias_ref, dk_ref, dv_ref
):
    length = q_ref.shape[0]
    scale = (LANES // 2) ** (-0.5)

    @pl.when(pl.program_id(0) == 0)
    def _():
        fill_bias(starts_ref, bias_ref, length, 1)

    product = grad_ref[...].astype(FLOAT) * mixed_ref[...].astype(FLOAT)
    row = lax.broadcasted_iota(jnp.int32, (8, LANES), 0)
    col = lax.broadcasted_iota(jnp.int32, (8, LANES), 1)
    picks = jnp.where((col < LANES // 2) == (row == 0), 1.0, 0.0).astype(FLOAT)
    inner = precise(picks, product, (1, 1))
    keys = [half_lanes(k_ref[...] * jnp.asarray(scale, HALF), half) for half in range(2)]
    values = [half_lanes(v_ref[...], half) for half in range(2)]
    dk_ref[...] = jnp.zeros_like(dk_ref)
    dv_ref[...] = jnp.zeros_like(dv_ref)
    query_sum = jnp.zeros((1, LANES), FLOAT)
    for block in range(length // BLOCK):
        begin = block * BLOCK
        extent = key_extent(block, length)
        query = q_ref[begin : begin + BLOCK, :]
        grad = grad_ref[begin : begin + BLOCK, :]
        grad_query = 0.0
        for half in range(2):
            scores = mult_rt(keys[half][0:extent, :], query)
            grad_probs = mult_rt(values[half][0:extent, :], grad)
            lse = lse_ref[half : half + 1, begin : begin + BLOCK]
            base = inner[half : half + 1, begin : begin + BLOCK]
            edge = scores[begin:extent, :] + bias_ref[block, 0 : extent - begin, :]
            shifted = edge if begin == 0 else jnp.concatenate([scores[0:begin, :], edge], axis=0)
            probs = jnp.exp(shifted - lse)
            grad_scores = (probs * (grad_probs - base)).astype(HALF)
            grad_half = half_lanes(grad, half)
            query_half = half_lanes(query * jnp.asarray(scale, HALF), half)
            dv_ref[0:extent, :] += mult(probs.astype(HALF), grad_half)
            dk_ref[0:extent, :] += mult(grad_scores, query_half)
            grad_query = grad_query + mult_lt(grad_scores, keys[half][0:extent, :])
        rounded = grad_query.astype(HALF)
        out_ref[0, begin : begin + BLOCK, :] = rounded
        query_sum = query_sum + rounded.astype(FLOAT).sum(axis=0, keepdims=True)
    out_ref[1, :, :] = dk_ref[...].astype(HALF)
    value = dv_ref[...].astype(HALF)
    out_ref[2, :, :] = value
    value_sum = value.astype(FLOAT).sum(axis=0, keepdims=True)
    sums_ref[...] = jnp.where(row == 0, query_sum, value_sum)


def attend_backward(joined, starts, mixed, grad_mixed, lse):
    length, wide = joined.shape
    pairs = wide // 3 // LANES
    return pl.pallas_call(
        attend_backward_kernel,
        grid=(pairs,),
        in_specs=[
            pl.BlockSpec(memory_space=pltpu.SMEM),
            pl.BlockSpec((length, LANES), lambda h: (0, h)),
            pl.BlockSpec((length, LANES), lambda h: (0, pairs + h)),
            pl.BlockSpec((length, LANES), lambda h: (0, 2 * pairs + h)),
            pl.BlockSpec((length, LANES), lambda h: (0, h)),
            pl.BlockSpec((length, LANES), lambda h: (0, h)),
            pl.BlockSpec((8, length), lambda h: (h, 0)),
        ],
        out_specs=[
            pl.BlockSpec((3, length, LANES), lambda h: (0, 0, h)),
            pl.BlockSpec((8, LANES), lambda h: (0, h)),
        ],
        out_shape=[
            jax.ShapeDtypeStruct((3, length, wide // 3), HALF),
            jax.ShapeDtypeStruct((8, wide // 3), FLOAT),
        ],
        scratch_shapes=[
            pltpu.VMEM((length // BLOCK, 2 * BLOCK, BLOCK), FLOAT),
            pltpu.VMEM((length, LANES), FLOAT),
            pltpu.VMEM((length, LANES), FLOAT),
        ],
        compiler_params=params_of(("arbitrary",)),
        cost_estimate=LIGHT,
        name="attend_backward",
    )(starts, joined, joined, joined, mixed, grad_mixed, lse)


def normalise(values):
    middle = values.mean(axis=1, keepdims=True)
    centered = values - middle
    spread = (centered * centered).mean(axis=1, keepdims=True)
    rate = lax.rsqrt(spread + NORM_EPS)
    return centered * rate, rate


def normalise_backward(grad_unit, unit, rate):
    along = grad_unit.mean(axis=1, keepdims=True)
    across = (grad_unit * unit).mean(axis=1, keepdims=True)
    return rate * (grad_unit - along - unit * across)


def gelu_pair(inner):
    size = jnp.abs(inner)
    ratio = 1.0 / (1.0 + (ERF_SLOPE * 2.0**-0.5) * size)
    tail = jnp.full_like(ratio, 0.5 * ERF_TERMS[-1])
    for term in ERF_TERMS[-2::-1]:
        tail = tail * ratio + 0.5 * term
    bell = jnp.exp(-0.5 * inner * inner)
    tail = tail * ratio * bell
    below = jnp.where(inner < 0.0, tail, 1.0 - tail)
    return inner * below, below + inner * (bell * (2.0 * jnp.pi) ** -0.5)


QUERY_B, VALUE_B, OUT_B, GAIN1, SHIFT1, DOWN_B, GAIN2, SHIFT2 = range(8)


def flip_kernel(value_ref, out_ref):
    out_ref[...] = value_ref[...].T


def flip(value):
    return pl.pallas_call(
        flip_kernel,
        in_specs=memory([pltpu.VMEM]),
        out_specs=pl.BlockSpec(memory_space=pltpu.VMEM),
        out_shape=jax.ShapeDtypeStruct(value.shape[::-1], value.dtype),
        compiler_params=params_of(None, FULL),
        cost_estimate=LIGHT,
        name="flip",
    )(value)


def project_kernel(tokens_ref, weight_ref, table_ref, out_ref):
    wide = tokens_ref.shape[1]
    for part in range(3):
        value = mult(tokens_ref[...], weight_ref[:, part * wide : (part + 1) * wide])
        if part == 0:
            value = value + table_ref[QUERY_B : QUERY_B + 1, :]
        elif part == 2:
            value = value + table_ref[VALUE_B : VALUE_B + 1, :]
        out_ref[:, part * wide : (part + 1) * wide] = value.astype(HALF)


def project(tokens, weight, table):
    length, wide = tokens.shape
    return pl.pallas_call(
        project_kernel,
        grid=(length // BLOCK,),
        in_specs=[pl.BlockSpec((BLOCK, wide), lambda i: (i, 0))] + memory([pltpu.VMEM] * 2),
        out_specs=pl.BlockSpec((BLOCK, 3 * wide), lambda i: (i, 0)),
        out_shape=jax.ShapeDtypeStruct((length, 3 * wide), HALF),
        compiler_params=params_of(("arbitrary",)),
        cost_estimate=LIGHT,
        name="project",
    )(tokens, weight, table)


def feed_up_kernel(
    mixed_ref, tokens_ref, out_w_ref, up_ref, table_ref, up_b_ref,
    first_ref, first_t_ref, active_ref, active_t_ref, slope_ref, unit1_ref, rate1_ref,
):
    wide = tokens_ref.shape[1]
    line = lambda which: table_ref[which : which + 1, :]
    residual = tokens_ref[...].astype(FLOAT) + (mult(mixed_ref[...], out_w_ref[...]) + line(OUT_B))
    unit, rate = normalise(residual)
    unit1_ref[...] = unit.astype(HALF)
    rate1_ref[...] = jnp.broadcast_to(rate, rate1_ref.shape)
    first = unit * line(GAIN1) + line(SHIFT1)
    first_ref[...] = first
    first_half = first.astype(HALF)
    first_t_ref[...] = first_half.T
    for part in range(up_ref.shape[1] // wide):
        cols = slice(part * wide, (part + 1) * wide)
        inner = mult(first_half, up_ref[:, cols]) + up_b_ref[0:1, cols]
        active, slope = gelu_pair(inner)
        active = active.astype(HALF)
        active_ref[:, cols] = active
        active_t_ref[cols, :] = active.T
        slope_ref[:, cols] = slope.astype(HALF)


def block_specs():
    rows = lambda cols: pl.BlockSpec((BLOCK, cols), lambda i: (i, 0))
    flipped = lambda cols: pl.BlockSpec((cols, BLOCK), lambda i: (0, i))
    return rows, flipped


def feed_up(mixed, tokens, out_w, up, table, up_b):
    length, wide = tokens.shape
    inner = up.shape[1]
    rows, flipped = block_specs()
    weights = (out_w, up, table, up_b)
    return pl.pallas_call(
        feed_up_kernel,
        grid=(length // BLOCK,),
        in_specs=[rows(wide), rows(wide)] + memory([pltpu.VMEM] * len(weights)),
        out_specs=[rows(wide), flipped(wide), rows(inner), flipped(inner), rows(inner), rows(wide), rows(LANES)],
        out_shape=[
            struct((length, wide), FLOAT), struct((wide, length)), struct((length, inner)), struct((inner, length)),
            struct((length, inner)), struct((length, wide)), struct((length, LANES), FLOAT),
        ],
        compiler_params=params_of(("arbitrary",), 36 << 20),
        cost_estimate=LIGHT,
        name="feed_up",
    )(mixed, tokens, *weights)


def feed_down_kernel(
    first_ref, active_ref, down_ref, student_w_ref, pool_w_ref, table_ref, student_b_ref,
    hidden_ref, hidden_t_ref, unit2_ref, rate2_ref, student_t_ref, pool_ref,
):
    line = lambda which: table_ref[which : which + 1, :]
    total = first_ref[...] + line(DOWN_B) + mult(active_ref[...], down_ref[...])
    unit, rate = normalise(total)
    unit2_ref[...] = unit.astype(HALF)
    rate2_ref[...] = jnp.broadcast_to(rate, rate2_ref.shape)
    hidden = (unit * line(GAIN2) + line(SHIFT2)).astype(HALF)
    hidden_ref[...] = hidden
    hidden_t_ref[...] = hidden.T
    student = (mult(hidden, student_w_ref[...]) + student_b_ref[0:1, :]).astype(HALF)
    student_t_ref[...] = student.T
    pool_ref[...] = mult(student, pool_w_ref[...]).astype(HALF)


def feed_down(first, active, down, student_w, pool_w, table, student_b):
    length, wide = first.shape
    small = student_w.shape[1]
    rows, flipped = block_specs()
    weights = (down, student_w, pool_w, table, student_b)
    return pl.pallas_call(
        feed_down_kernel,
        grid=(length // BLOCK,),
        in_specs=[rows(wide), rows(active.shape[1])] + memory([pltpu.VMEM] * len(weights)),
        out_specs=[rows(wide), flipped(wide), rows(wide), rows(LANES), flipped(small), rows(3 * small)],
        out_shape=[
            struct((length, wide)), struct((wide, length)), struct((length, wide)), struct((length, LANES), FLOAT),
            struct((small, length)), struct((length, 3 * small)),
        ],
        compiler_params=params_of(("arbitrary",)),
        cost_estimate=LIGHT,
        name="feed_down",
    )(first, active, *weights)


def student_kernel(
    label_ref, cotangent_ref, pool_ref, unit2_ref, rate2_ref, student_w_ref, pool_w_ref, dense_ref, class_ref,
    small_b_ref, table_ref,
    logits_ref, grad_pool_ref, grad_student_ref, residual_ref, residual_half_ref, dense_grad_ref, class_grad_ref,
    small_sums_ref, sums_ref,
):
    length, three = pool_ref.shape
    small = three // 3
    scale = (small // POOL_HEADS) ** (-0.5)
    head_of = lambda axis: lax.broadcasted_iota(jnp.int32, (small, small), axis) // (small // POOL_HEADS)
    same = jnp.where(head_of(0) == head_of(1), 1.0, 0.0).astype(FLOAT)
    top = lax.broadcasted_iota(jnp.int32, (8, small), 0) == 0
    query = pool_ref[0:8, 0:small].astype(FLOAT)[0:1, :]
    key = pool_ref[:, small : 2 * small].astype(FLOAT)
    value = pool_ref[:, 2 * small : 3 * small].astype(FLOAT)
    scores = precise(key * query, same, (1, 0)) * scale
    raised = jnp.exp(scores - scores.max(axis=0, keepdims=True))
    weights = raised / raised.sum(axis=0, keepdims=True)
    pooled = (weights * value).sum(axis=0, keepdims=True)
    spread = lambda vector: jnp.where(top, vector, 0.0)
    dense = dense_ref[...].astype(FLOAT)
    classes = class_ref[...].astype(FLOAT)
    before = precise(spread(pooled), dense, (1, 0)) + small_b_ref[1:2, :]
    summary = jnp.tanh(before[0:1, :])
    logits = (precise(spread(summary), classes, (1, 0)) + small_b_ref[2:3, :])[0:1, :]
    lane = lax.broadcasted_iota(jnp.int32, (1, small), 1)
    real = small_b_ref[3:4, :] > 0.5
    masked = jnp.where(real, logits, MASKED_SCORE)
    lifted = jnp.where(real, jnp.exp(masked - masked.max(axis=1, keepdims=True)), 0.0)
    grad_logits = lifted / lifted.sum(axis=1, keepdims=True) - jnp.where(lane == label_ref[0], 1.0, 0.0)
    logits_ref[...] = logits[:, 0 : logits_ref.shape[1]]
    class_grad_ref[...] = precise(spread(summary), spread(grad_logits), (0, 0))
    grad_summary = precise(spread(grad_logits), classes, (1, 1))[0:1, :]
    grad_before = grad_summary * (1.0 - summary * summary)
    dense_grad_ref[...] = precise(spread(pooled), spread(grad_before), (0, 0))
    grad_pooled = precise(spread(grad_before), dense, (1, 1))[0:1, :]
    grad_weights = precise(value * grad_pooled, same, (1, 0))
    inner = (weights * grad_weights).sum(axis=0, keepdims=True)
    grad_scores = weights * (grad_weights - inner)
    grad_query = (grad_scores * key).sum(axis=0, keepdims=True) * scale
    first = lax.broadcasted_iota(jnp.int32, (length, small), 0) == 0
    grad_pool_ref[:, 0:small] = jnp.where(first, grad_query, 0.0).astype(HALF)
    grad_pool_ref[:, small : 2 * small] = (grad_scores * query * scale).astype(HALF)
    grad_pool_ref[:, 2 * small : 3 * small] = (weights * grad_pooled).astype(HALF)
    grad_student = mult_rt(grad_pool_ref[...], pool_w_ref[...])
    which = lax.broadcasted_iota(jnp.int32, (8, small), 0)
    student_sum = grad_student.sum(axis=0, keepdims=True)
    small_sums_ref[...] = jnp.where(
        which == 0, student_sum, jnp.where(which == 1, grad_before, jnp.where(which == 2, grad_logits, 0.0))
    )
    grad_student_ref[...] = grad_student.astype(HALF)

    sums_ref[...] = jnp.zeros_like(sums_ref)

    def one_block(block, _):
        rows = pl.ds(pl.multiple_of(block * BLOCK, BLOCK), BLOCK)
        grad = cotangent_ref[rows, :].astype(FLOAT) + mult_rt(grad_student_ref[rows, :], student_w_ref[...])
        unit = unit2_ref[rows, :].astype(FLOAT)
        residual = normalise_backward(grad * table_ref[GAIN2 : GAIN2 + 1, :], unit, rate2_ref[rows, 0:1])
        residual_ref[rows, :] = residual
        residual_half_ref[rows, :] = residual.astype(HALF)
        sums_ref[0:1, :] += (grad * unit).sum(axis=0, keepdims=True)
        sums_ref[1:2, :] += grad.sum(axis=0, keepdims=True)
        sums_ref[2:3, :] += residual.sum(axis=0, keepdims=True)
        return 0

    lax.fori_loop(0, length // BLOCK, one_block, 0)


def student_pass(label, cotangent, pool, unit2, rate2, student_w, pool_w, dense, classes, small_b, table, count):
    length, wide = cotangent.shape
    small = student_w.shape[1]
    struct = jax.ShapeDtypeStruct
    args = (cotangent, pool, unit2, rate2, student_w, pool_w, dense, classes, small_b, table)
    return pl.pallas_call(
        student_kernel,
        in_specs=memory([pltpu.SMEM] + [pltpu.VMEM] * len(args)),
        out_specs=memory([pltpu.VMEM] * 9),
        out_shape=[
            struct((1, count), FLOAT), struct((length, 3 * small), HALF), struct((length, small), HALF),
            struct((length, wide), FLOAT), struct((length, wide), HALF), struct((small, small), FLOAT),
            struct((small, small), FLOAT), struct((8, small), FLOAT), struct((8, wide), FLOAT),
        ],
        compiler_params=params_of(None),
        cost_estimate=LIGHT,
        name="student",
    )(label, *args)


def back_kernel(
    half_ref, residual_ref, slope_ref, unit1_ref, rate1_ref, down_ref, up_ref, out_w_ref, table_ref,
    inner_ref, residual1_ref, one_ref, mixed_ref, sums_ref, up_sums_ref,
):
    wide = residual_ref.shape[1]

    @pl.when(pl.program_id(0) == 0)
    def _():
        sums_ref[...] = jnp.zeros_like(sums_ref)
        up_sums_ref[...] = jnp.zeros_like(up_sums_ref)

    total = residual_ref[...]
    for part in range(up_ref.shape[1] // wide):
        cols = slice(part * wide, (part + 1) * wide)
        grad = mult_rt(half_ref[...], down_ref[cols, :]) * slope_ref[:, cols].astype(FLOAT)
        up_sums_ref[0:1, cols] += grad.sum(axis=0, keepdims=True)
        grad = grad.astype(HALF)
        inner_ref[:, cols] = grad
        total = total + mult_rt(grad, up_ref[:, cols])
    unit = unit1_ref[...].astype(FLOAT)
    residual = normalise_backward(total * table_ref[GAIN1 : GAIN1 + 1, :], unit, rate1_ref[:, 0:1])
    residual1_ref[...] = residual
    one = residual.astype(HALF)
    one_ref[...] = one
    mixed_ref[...] = mult_rt(one, out_w_ref[...]).astype(HALF)
    sums_ref[0:1, :] += (total * unit).sum(axis=0, keepdims=True)
    sums_ref[1:2, :] += total.sum(axis=0, keepdims=True)
    sums_ref[2:3, :] += residual.sum(axis=0, keepdims=True)


def back(half, residual, slope, unit1, rate1, down, up, out_w, table):
    length, wide = residual.shape
    inner = up.shape[1]
    rows = lambda cols: pl.BlockSpec((BLOCK, cols), lambda i: (i, 0))
    struct = jax.ShapeDtypeStruct
    weights = (down, up, out_w, table)
    return pl.pallas_call(
        back_kernel,
        grid=(length // BLOCK,),
        in_specs=[rows(wide), rows(wide), rows(inner), rows(wide), rows(LANES)] + memory([pltpu.VMEM] * len(weights)),
        out_specs=[rows(inner), rows(wide), rows(wide), rows(wide), whole((8, wide)), whole((8, inner))],
        out_shape=[
            struct((length, inner), HALF), struct((length, wide), FLOAT), struct((length, wide), HALF),
            struct((length, wide), HALF), struct((8, wide), FLOAT), struct((8, inner), FLOAT),
        ],
        compiler_params=params_of(("arbitrary",)),
        cost_estimate=LIGHT,
        name="back",
    )(half, residual, slope, unit1, rate1, *weights)


def input_kernel(grad_ref, residual_ref, weight_ref, out_ref):
    wide = residual_ref.shape[1]
    total = residual_ref[...]
    for part in range(3):
        total = total + mult_rt(grad_ref[part], weight_ref[:, part * wide : (part + 1) * wide])
    out_ref[...] = total


def input_pass(grad, residual, weight):
    length, wide = residual.shape
    return pl.pallas_call(
        input_kernel,
        grid=(length // BLOCK,),
        in_specs=[
            pl.BlockSpec((3, BLOCK, wide), lambda i: (0, i, 0)), pl.BlockSpec((BLOCK, wide), lambda i: (i, 0)),
            pl.BlockSpec(memory_space=pltpu.VMEM),
        ],
        out_specs=pl.BlockSpec((BLOCK, wide), lambda i: (i, 0)),
        out_shape=jax.ShapeDtypeStruct((length, wide), FLOAT),
        compiler_params=params_of(("arbitrary",)),
        cost_estimate=LIGHT,
        name="input_pass",
    )(grad, residual, weight)


def swap(value, axis, bits):
    size = lax.axis_size(axis)
    return lax.ppermute(value, axis, [(i, i ^ bits) for i in range(size)])


def around(value):
    return [value] + [swap(value, "replica", bits) for bits in (2, 4, 6)]


WIDE = 384
SMALL = (0, 128)
SMALL_ROWS = 16
VECTOR_ROWS = 32


def rows_of(mat):
    return SMALL_ROWS if mat == SMALL else mat[0] * mat[1] // 4


def all_rows(mats):
    return sum(rows_of(mat) for mat in mats)


def after(value, *others):
    return lax.optimization_barrier((value,) + others)[0]


FULL = 60 << 20


def vmem_call(kernel, name, where, inputs, outs, moved, scratch=(), limit=32 << 20):
    return pl.pallas_call(
        kernel,
        in_specs=memory([pltpu.SMEM] + [pltpu.VMEM] * len(inputs)),
        out_specs=memory([pltpu.VMEM] * len(outs)),
        out_shape=outs,
        scratch_shapes=list(scratch),
        compiler_params=params_of(None, limit),
        cost_estimate=LIGHT,
        name=name,
    )(where, *inputs)


def struct(shape, kind=HALF):
    return jax.ShapeDtypeStruct(shape, kind)


def aligned(begin, rows):
    return pl.ds(pl.multiple_of(begin, rows), rows)


def small_places(student_rows):
    third = student_rows // 3
    return third, third + 32


def fold_small(block_ref, base, student_ref, pool_ref, dense_ref, class_ref):
    third, last = small_places(student_ref.shape[0])
    for part in range(3):
        block_ref[base : base + third, part * LANES : (part + 1) * LANES] = student_ref[part * third : (part + 1) * third, :]
    block_ref[base + third : base + last, :] = pool_ref[...]
    rest = slice(base + last, base + 128)
    block_ref[rest, :] = jnp.zeros((128 - last, WIDE), block_ref.dtype)
    block_ref[rest, 0:LANES] = dense_ref[...]
    block_ref[rest, LANES : LANES + class_ref.shape[1]] = class_ref[...]


def unfold_small(block_ref, shard, student_ref, pool_ref, dense_ref, class_ref, rows):
    third, last = small_places(rows)
    base, short = shard * 128, 128 - last
    for part in range(3):
        begin = shard * rows + part * third
        student_ref[begin : begin + third, :] = block_ref[base : base + third, part * LANES : (part + 1) * LANES].astype(student_ref.dtype)
    target = slice(shard * short, (shard + 1) * short)
    pool_ref[target, :] = block_ref[base + third : base + last, :].astype(pool_ref.dtype)
    dense_ref[target, :] = block_ref[base + last : base + 128, 0:LANES].astype(dense_ref.dtype)
    classes = class_ref.shape[1]
    class_ref[target, :] = block_ref[base + last : base + 128, LANES : LANES + classes].astype(class_ref.dtype)


def pack_kernel(place_ref, *refs, mats, lines):
    chip, core = place_ref[1], place_ref[2]
    piece_ref = refs[-1]
    offset = 0
    if lines:
        base = all_rows(mats)
        for half in range(2):
            piece_ref[base : base + 16, half * LANES : (half + 1) * LANES] = refs[-2][half * 16 : half * 16 + 16, :]
        piece_ref[base : base + 16, 2 * LANES :] = jnp.zeros((16, WIDE - 2 * LANES), HALF)
    for mat, ref in zip(mats, refs):
        if mat == SMALL:
            small_ref = refs[-2]
            fold_small(small_ref, 0, *refs[len(mats) - 1 : len(mats) + 3])
            piece_ref[offset : offset + SMALL_ROWS, :] = small_ref[aligned((chip * 2 + core) * SMALL_ROWS, SMALL_ROWS), :]
            continue
        rows = mat[1] // 4
        for chunk in range(mat[0]):
            lanes = aligned(chunk * 2 * WIDE + core * WIDE, WIDE)
            piece_ref[offset : offset + rows, :] = ref[aligned(chip * rows, rows), lanes]
            offset += rows


def pack(where, shards, mats, lines=None):
    outs = [struct((all_rows(mats) + (0 if lines is None else 16), WIDE))]
    shards = list(shards) + ([] if lines is None else [lines])
    if SMALL in mats:
        outs = [struct(SMALL[1:] + (WIDE,))] + outs
    return vmem_call(partial(pack_kernel, mats=mats, lines=lines is not None), "pack", where, shards, outs, 2 * sum(s.size for s in shards), limit=FULL)


def put_piece(out_ref, ref, step, offset, base, mat, chip, core):
    if mat == SMALL:
        target = aligned(base + (chip * 2 + core) * SMALL_ROWS, SMALL_ROWS)
        out_ref[target, :] = ref[step, offset : offset + SMALL_ROWS, :].astype(out_ref.dtype)
        return
    rows = mat[1] // 4
    for chunk in range(mat[0]):
        lanes = aligned(chunk * 2 * WIDE + core * WIDE, WIDE)
        first = offset + chunk * rows
        out_ref[aligned(base + chip * rows, rows), lanes] = ref[step, first : first + rows, :].astype(out_ref.dtype)


def place_kernel(place_ref, *refs, mats, rows):
    shard, chip, core = place_ref[0], place_ref[1], place_ref[2]
    count = len(mats)
    pieces, owns, outs = refs[:8], refs[8 : 8 + count], list(refs[8 + count :])
    if SMALL in mats:
        block_ref = outs.pop()
        smalls, outs = outs[count - 1 :], outs[: count - 1] + [block_ref]
    offset = 0
    for mat, own_ref, out_ref in zip(mats, owns, outs):
        height = mat[1]
        out_ref[aligned(shard * height, height), :] = own_ref[...]
        for number, ref in enumerate(pieces):
            far, other = number // 2, number % 2
            for step in range(ref.shape[0]):
                base = (shard ^ (step + 1)) * height
                put_piece(out_ref, ref, step, offset, base, mat, chip ^ far, core ^ other)
        offset += rows_of(mat)
    if SMALL in mats:
        for step in range(pieces[0].shape[0] + 1):
            unfold_small(block_ref, step, *smalls, rows)


def place(where, pieces, owns, outs, mats, rows=0):
    shards = pieces[0].shape[0] + 1
    scratch = [pltpu.VMEM((shards * SMALL[1], WIDE), HALF)] if SMALL in mats else []
    moved = 4 * shards * sum(own.size for own in owns)
    return vmem_call(partial(place_kernel, mats=mats, rows=rows), "place", where, pieces + list(owns), outs, moved, scratch)


def table_kernel(place_ref, *refs, classes, base):
    *lines, table_ref, up_ref, short_ref, stack_ref = refs
    shard = place_ref[0]
    wide, inner = table_ref.shape[1], up_ref.shape[1]
    shards = len(lines)
    ups = inner // shards // LANES
    table = jnp.zeros(table_ref.shape, FLOAT)
    shorts = jnp.zeros((8, LANES), FLOAT)
    for step, ref in enumerate(lines):
        target = shard ^ step
        if step == 0:
            block = ref[...].astype(FLOAT)
        else:
            stack_ref[step - 1] = ref[...]
            block = jnp.concatenate([ref[base : base + 16, half * LANES : half * LANES + LANES] for half in range(2)], axis=0)
            block = block.astype(FLOAT)
        both = jnp.concatenate([block[0:8], block[8:16], jnp.zeros((8, wide - 2 * LANES), FLOAT)], axis=1)
        table = table + pltpu.roll(both, target * (wide // shards), 1)
        for line in range(ups):
            row = block[16 + line : 17 + line]
            up_ref[:, aligned(target * (inner // shards) + line * LANES, LANES)] = jnp.broadcast_to(row, (8, LANES))
        shorts = shorts + pltpu.roll(block[16 : 24], target * (LANES // shards), 1)
    table_ref[...] = table
    lane = lax.broadcasted_iota(jnp.int32, (1, LANES), 1)
    short_ref[0:2, :] = shorts[6:8]
    short_ref[2:3, :] = lines[0][...].astype(FLOAT)[24:25]
    short_ref[3:4, :] = jnp.where(lane < classes, 1.0, 0.0)
    short_ref[4:8, :] = jnp.zeros((4, LANES), FLOAT)


def lines_kernel(place_ref, *refs):
    *vectors, up_ref, student_ref, dense_ref, class_ref, out_ref, full_ref = refs
    full_ref[...] = jnp.zeros_like(full_ref)

    def put(row, value):
        full_ref[row : row + 1, 0 : value.shape[0]] = value.astype(FLOAT).reshape(1, value.shape[0])

    for line, ref in enumerate(vectors):
        put(line, ref[0:LANES])
        put(8 + line, ref[LANES:])
    for line in range(up_ref.shape[0] // LANES):
        put(16 + line, up_ref[line * LANES : (line + 1) * LANES])
    put(22, student_ref[...])
    put(23, dense_ref[...])
    put(24, class_ref[...])
    out_ref[...] = full_ref[...].astype(HALF)


def vector_lines(where, vectors, up_bias, shorts, class_bias):
    inputs = [*vectors, up_bias, *shorts, class_bias]
    (lines,) = vmem_call(lines_kernel, "lines", where, inputs, [struct((32, LANES))], 0, [pltpu.VMEM((32, LANES), FLOAT)], FULL)
    return lines


def from_shards(value):
    return [swap(value, "shard", bits) for bits in range(1, lax.axis_size("shard"))]


def both_cores(values):
    return [piece for value in values for piece in (value, swap(value, "replica", 1))]


def weight_grad_kernel(place_ref, left_ref, right_ref, send_ref, keep_ref):
    core = place_ref[2]
    left = left_ref[...]
    for chunk in range(send_ref.shape[0]):
        for ref, which in ((send_ref, 1 - core), (keep_ref, core)):
            if len(right_ref.shape) == 3:
                right = right_ref[chunk, :, aligned(which * WIDE, WIDE)]
            else:
                right = right_ref[:, aligned(chunk * 2 * WIDE + which * WIDE, WIDE)]
            ref[chunk] = mult(left, right).astype(HALF)


def weight_grad(where, left, right, name, block=256):
    height, length = left.shape
    chunks = right.shape[0] if right.ndim == 3 else right.shape[1] // (2 * WIDE)
    out = struct((chunks, height, WIDE))
    return pl.pallas_call(
        weight_grad_kernel,
        grid=(height // block,),
        in_specs=[pl.BlockSpec(memory_space=pltpu.SMEM), pl.BlockSpec((block, length), lambda i: (i, 0))]
        + memory([pltpu.VMEM]),
        out_specs=[pl.BlockSpec((chunks, block, WIDE), lambda i: (0, i, 0))] * 2,
        out_shape=[out, out],
        compiler_params=params_of(("arbitrary",)),
        cost_estimate=LIGHT,
        name=name,
    )(where, left, right)


def small_grad_kernel(place_ref, hidden_ref, grad_student_ref, student_ref, grad_pool_ref, dense_ref, class_ref, send_ref, keep_ref, block_ref, first_ref, pool_ref):
    core = place_ref[2]
    shards = send_ref.shape[1] // (4 * SMALL_ROWS)
    first_ref[...] = mult(hidden_ref[...], grad_student_ref[...])
    pool_ref[...] = mult(student_ref[...], grad_pool_ref[...])
    part = lambda ref, shard: ref.at[pl.ds(shard * (ref.shape[0] // shards), ref.shape[0] // shards)]
    for shard in range(shards):
        fold_small(block_ref, shard * 128, *(part(ref, shard) for ref in (first_ref, pool_ref, dense_ref, class_ref)))
    for shard in range(shards):
        for chip in range(4):
            target = pl.ds((shard * 4 + chip) * SMALL_ROWS, SMALL_ROWS)
            for ref, which in ((send_ref, 1 - core), (keep_ref, core)):
                ref[0, target, :] = block_ref[aligned(shard * 128 + (chip * 2 + which) * SMALL_ROWS, SMALL_ROWS), :].astype(HALF)


def small_grad(where, hidden, grad_student, student, grad_pool, dense, classes, shards):
    outs = [struct((1, shards * 4 * SMALL_ROWS, WIDE))] * 2
    scratch = [
        pltpu.VMEM((shards * 128, WIDE), FLOAT), pltpu.VMEM((hidden.shape[0], LANES), FLOAT), pltpu.VMEM((LANES, WIDE), FLOAT)
    ]
    inputs = [hidden, grad_student, student, grad_pool, dense, classes]
    return vmem_call(small_grad_kernel, "small_grad", where, inputs, outs, 4 * hidden.size, scratch)


def vector_kernel(place_ref, heads_ref, one_ref, two_ref, up_ref, short_ref, half_ref, out_ref):
    half = heads_ref.shape[1] // 2
    for side in range(2):
        lanes = slice(side * half, (side + 1) * half)
        lines = [heads_ref[0:1, lanes], heads_ref[1:2, lanes], one_ref[2:3, lanes], one_ref[0:1, lanes], one_ref[1:2, lanes]]
        lines += [two_ref[2:3, lanes], two_ref[0:1, lanes], two_ref[1:2, lanes]]
        for row, line in enumerate(lines):
            out_ref[side * 8 + row : side * 8 + row + 1, :] = line
    for row in range(up_ref.shape[1] // WIDE):
        out_ref[16 + row : 17 + row, :] = up_ref[0:1, row * WIDE : (row + 1) * WIDE]
    out_ref[24:32, :] = jnp.zeros((8, WIDE), FLOAT)
    for part in range(3):
        out_ref[24:25, part * LANES : (part + 1) * LANES] = short_ref[part : part + 1, :]
    half_ref[...] = out_ref[...].astype(HALF)


def split_kernel(place_ref, *refs, count, shards, vectors):
    chip = place_ref[1]
    keeps, recvs, outs = refs[:count], refs[count : 2 * count], refs[-4:]
    total = sum(keep.shape[0] * keep.shape[1] for keep in keeps) // (4 * shards)
    offset = 0
    for keep_ref, recv_ref in zip(keeps, recvs):
        height = keep_ref.shape[1] // shards
        rows = height // 4
        for chunk in range(keep_ref.shape[0]):
            for shard in range(shards):
                for far, out_ref in enumerate(outs):
                    source = aligned(shard * height + (chip ^ far) * rows, rows)
                    value = keep_ref[chunk, source, :].astype(FLOAT) + recv_ref[chunk, source, :].astype(FLOAT)
                    first = shard * total + offset
                    out_ref[first : first + rows, :] = value.astype(HALF)
            offset += rows
    if vectors:
        value = (refs[2 * count][...].astype(FLOAT) + refs[2 * count + 1][...].astype(FLOAT)).astype(HALF)
        for out_ref in outs:
            out_ref[shards * total : shards * total + VECTOR_ROWS, :] = value


def split(where, keeps, recvs, shards, vectors=()):
    total = sum(keep.shape[0] * keep.shape[1] for keep in keeps) // 4 + (VECTOR_ROWS if vectors else 0)
    kernel = partial(split_kernel, count=len(keeps), shards=shards, vectors=bool(vectors))
    inputs = list(keeps) + list(recvs) + list(vectors)
    return vmem_call(kernel, "split", where, inputs, [struct((total, WIDE))] * 4, 20 * total * WIDE)


def merge_kernel(place_ref, *refs, shards, vectors):
    shard = place_ref[0]
    parts, outs = refs[: -shards], refs[-shards:]
    offset = 0
    for group in range(len(parts) // 4):
        four = parts[4 * group : 4 * group + 4]
        last = vectors and group == len(parts) // 4 - 1
        rows = (four[0].shape[0] - (VECTOR_ROWS if last else 0)) // shards

        def total(source):
            a, b, c, d = (ref[source, :].astype(FLOAT) for ref in four)
            return ((a + b) + (c + d)).astype(HALF)

        for step, out_ref in enumerate(outs):
            out_ref[offset : offset + rows, :] = total(aligned((shard ^ step) * rows, rows))
        offset += rows
        if last:
            value = total(slice(shards * rows, shards * rows + VECTOR_ROWS))
            for out_ref in outs:
                out_ref[offset : offset + VECTOR_ROWS, :] = value


def merge(where, groups, shards, vectors=False):
    extra = VECTOR_ROWS if vectors else 0
    rows = (sum(four[0].shape[0] for four in groups) - extra) // shards + extra
    kernel = partial(merge_kernel, shards=shards, vectors=vectors)
    inputs = [part for four in groups for part in four]
    return vmem_call(kernel, "merge", where, inputs, [struct((rows, WIDE))] * shards, 10 * shards * rows * WIDE)


def total_kernel(place_ref, *refs, shards):
    parts, outs = refs[:shards], refs[shards:]
    offset = 0
    for out_ref in outs:
        rows = slice(offset, offset + out_ref.shape[0])
        terms = [ref[rows, :].astype(FLOAT) for ref in parts]
        while len(terms) > 1:
            half = len(terms) // 2
            terms = [terms[i] + terms[i + half] for i in range(half)]
        out_ref[...] = terms[0].astype(HALF)
        offset += out_ref.shape[0]


def total(where, parts, vectors=False):
    rows = parts[0].shape[0] - (VECTOR_ROWS if vectors else 0)
    outs = [struct((rows, WIDE))] + ([struct((VECTOR_ROWS, WIDE))] if vectors else [])
    outs = vmem_call(partial(total_kernel, shards=len(parts)), "total", where, parts, outs, 10 * rows * WIDE)
    bits = 8
    while bits < lax.axis_size("replica"):
        outs = [(v.astype(FLOAT) + swap(v, "replica", bits).astype(FLOAT)).astype(HALF) for v in outs]
        bits *= 2
    return outs


def finish_kernel(place_ref, *refs, mats, rows):
    chip, core = place_ref[1], place_ref[2]
    pieces, outs = refs[:8], list(refs[8:])
    if SMALL in mats:
        block_ref = outs.pop()
        smalls, outs = outs[len(mats) - 1 :], outs[: len(mats) - 1] + [block_ref]
    offset = 0
    for mat, out_ref in zip(mats, outs):
        for number, ref in enumerate(pieces):
            put_piece(out_ref, ref, 0, offset, 0, mat, chip ^ (number // 2), core ^ (number % 2))
        offset += rows_of(mat)
    if SMALL in mats:
        unfold_small(block_ref, 0, *smalls, rows)


def finish(where, pieces, mats, outs, rows=0):
    pieces = [piece[None] for piece in pieces]
    scratch = [pltpu.VMEM(SMALL[1:] + (WIDE,), FLOAT)] if SMALL in mats else []
    moved = 6 * sum(out.size for out in outs)
    return vmem_call(partial(finish_kernel, mats=mats, rows=rows), "finish", where, pieces, outs, moved, scratch)


def vector_out_kernel(place_ref, total_ref, *refs):
    tables, up_ref, shorts, class_ref = refs[:8], refs[8], refs[9:11], refs[11]
    shard = place_ref[0]
    wide = 2 * WIDE
    each = tables[0].shape[0]
    shards = wide // each
    values = total_ref[...].astype(FLOAT)
    table = jnp.concatenate([values[0:8], values[8:16]], axis=1)
    table = pltpu.roll(table, (shards - shard) * each, 1)[:, :each]
    for line, ref in enumerate(tables):
        ref[...] = table[line : line + 1].reshape(each)
    lines = up_ref.shape[0] // WIDE
    for line in range(lines):
        row = jnp.zeros((1, WIDE), FLOAT)
        for which in range(shards):
            row = row + jnp.where(shard == which, values[16 + which * lines + line : 17 + which * lines + line], 0.0)
        up_ref[line * WIDE : (line + 1) * WIDE] = row.reshape(WIDE)
    each = shorts[0].shape[0]
    for part, ref in enumerate(shorts):
        row = pltpu.roll(values[24:32, part * LANES : (part + 1) * LANES], (shards - shard) * each, 1)
        ref[...] = row[0:1, :each].reshape(each)
    class_ref[...] = values[24:25, 2 * LANES : 2 * LANES + class_ref.shape[0]].reshape(class_ref.shape[0])


def vector_out(where, value, shards, inner, classes):
    outs = [struct((2 * WIDE // shards,), FLOAT)] * 8 + [struct((inner // shards,), FLOAT)]
    outs += [struct((LANES // shards,), FLOAT)] * 2 + [struct((classes,), FLOAT)]
    return vmem_call(vector_out_kernel, "vector_out", where, [value], outs, 4 * value.size)


def body(
    tokens, cotangent, piece_starts, labels, qkv_weight, query_bias, value_bias, out_weight, out_bias, attention_gain,
    attention_shift, up_weight, up_bias, down_weight, down_bias, feed_gain, feed_shift, student_weight, student_bias,
    pool_weight, dense_weight, dense_bias, class_weight, class_bias,
):
    count, length, wide = tokens.shape
    inner = up_weight.shape[1]
    classes = class_weight.shape[1]
    student_rows = student_weight.shape[0]
    shards = lax.axis_size("shard")
    replica = lax.axis_index("replica")
    where = jnp.stack([lax.axis_index("shard"), (replica >> 1) & 3, replica & 1]).astype(jnp.int32)
    tokens, cotangent = tokens.reshape(length, wide), cotangent.reshape(length, wide)
    qkv_mats = ((3, qkv_weight.shape[0]),)
    up_mats = ((1, out_weight.shape[0]), (4, up_weight.shape[0]))
    down_mats = ((1, down_weight.shape[0]), SMALL)

    (piece,) = pack(where, [qkv_weight], qkv_mats)
    near = from_shards(piece)
    lines = vector_lines(
        where,
        [after(query_bias, piece), value_bias, out_bias, attention_gain, attention_shift, down_bias, feed_gain, feed_shift],
        up_bias, [student_bias, dense_bias], class_bias,
    )
    (up_piece,) = pack(where, [out_weight, up_weight], up_mats, lines)
    small, down_piece = pack(
        where, [after(down_weight, piece), student_weight, pool_weight, dense_weight, class_weight], down_mats
    )
    tokens_t = flip(after(tokens, piece))
    near[0], up_piece, small, down_piece, tokens_t = lax.optimization_barrier((near[0], up_piece, small, down_piece, tokens_t))
    near_stack = jnp.stack(near)
    qkv_around = around(near_stack)
    up_near = [swap(up_piece, "shard", bits) for bits in range(1, shards - 1)]
    up_near.append(swap(after(up_piece, up_near[0]), "shard", shards - 1))
    qkv_around[1], *up_near[:-1] = lax.optimization_barrier((qkv_around[1], *up_near[:-1]))
    qkv_pieces = both_cores(qkv_around)
    qkv_pieces[0], up_near[-1] = lax.optimization_barrier((qkv_pieces[0], up_near[-1]))
    (qkv,) = place(where, qkv_pieces, [qkv_weight], [struct((shards * qkv_weight.shape[0], 3 * wide))], qkv_mats)
    up_near[0] = after(up_near[0], qkv)
    table, up_b, small_b, up_stack = vmem_call(
        partial(table_kernel, classes=classes, base=all_rows(up_mats)), "table", where, [lines] + up_near,
        [
            struct((8, wide), FLOAT), struct((8, inner), FLOAT), struct((8, LANES), FLOAT),
            struct((shards - 1,) + up_piece.shape),
        ],
        8 * 8 * inner,
    )
    down_piece = after(down_piece, up_stack)
    up_around = around(up_stack)
    down_near = [swap(down_piece, "shard", bits) for bits in range(1, shards - 1)]
    qkv = after(qkv, up_stack)
    joined = project(tokens, qkv, table)
    joined, down_piece, down_near[0] = lax.optimization_barrier((joined, down_piece, down_near[0]))
    down_near.append(swap(down_piece, "shard", shards - 1))
    mixed, mixed_t, lse = attend_forward(joined, piece_starts)
    whole_of = lambda shard: struct((shards * shard.shape[0], shard.shape[1]))
    mixed, *arrived = lax.optimization_barrier((mixed, *down_near, *up_around))
    down_near, up_around = arrived[: shards - 1], arrived[shards - 1 :]
    down_stack = jnp.stack(down_near)
    down_around = around(after(down_stack, mixed))
    out_w, up = place(
        where, both_cores(up_around), [out_weight, up_weight], [whole_of(out_weight), whole_of(up_weight)], up_mats
    )

    first, first_t, active, active_t, slope, unit1, rate1 = feed_up(
        mixed, tokens, after(out_w, down_stack), up, table, up_b
    )
    rest = [whole_of(s) for s in (down_weight, student_weight, pool_weight, dense_weight)]
    rest.append(struct((shards * class_weight.shape[0], LANES)))
    active, *down_around = lax.optimization_barrier((active, *down_around))
    down, student_w, pool_w, dense_w, class_w = place(
        where, both_cores(down_around), [down_weight, small], rest, down_mats, student_rows
    )
    hidden, hidden_t, unit2, rate2, student_t, pool = feed_down(
        first, active, down, student_w, pool_w, table, small_b
    )
    logits, grad_pool, grad_student, residual2, half2, grad_dense, grad_class, small_sums, sums2 = student_pass(
        labels, cotangent, pool, unit2, rate2, student_w, pool_w, dense_w, class_w, small_b, table, classes
    )
    core_swap = lambda value: swap(value, "replica", 1)
    exchange = lambda parts: [parts[0]] + [swap(part, "replica", 2 * far) for far, part in enumerate(parts) if far > 0]
    spread = lambda parts: [parts[0]] + [swap(part, "shard", far) for far, part in enumerate(parts) if far > 0]
    send_down, keep_down = weight_grad(where, active_t, half2, "grad_down")
    send_small, keep_small = small_grad(
        where, after(hidden_t, send_down), grad_student, student_t, grad_pool, grad_dense, grad_class, shards
    )
    parts_a = split(where, [after(keep_down, keep_small)], [core_swap(send_down)], shards)
    exchanged_a = exchange(parts_a)
    grad_inner, residual1, half1, grad_mixed, sums1, up_sums = back(
        after(half2, parts_a[0], keep_small), residual2, slope, unit1, rate1, down, up, out_w, table
    )
    send_up, keep_up = weight_grad(where, first_t, grad_inner, "grad_up")
    swapped_small = core_swap(send_small)
    send_up, mixed_t, swapped_small, *exchanged_a = lax.optimization_barrier((send_up, mixed_t, swapped_small, *exchanged_a))
    send_out, keep_out = weight_grad(where, mixed_t, half1, "grad_out")
    parts_b = split(where, [keep_out, keep_up], [core_swap(send_out), core_swap(send_up)], shards)
    exchanged_b = exchange(parts_b)
    heads, head_sums = attend_backward(joined, piece_starts, mixed, after(grad_mixed, parts_b[0]), lse)
    send_qkv, keep_qkv = weight_grad(where, tokens_t, heads, "grad_qkv")
    send_qkv, *exchanged_b = lax.optimization_barrier((send_qkv, *exchanged_b))
    ready = merge(where, [exchanged_b, exchanged_a], shards)
    near_ab = spread(ready)
    keep_qkv = after(keep_qkv, ready[0])
    (vectors,) = vmem_call(
        vector_kernel, "vectors", where,
        [head_sums, sums1, sums2, up_sums, small_sums], [struct((VECTOR_ROWS, WIDE))], 4 * VECTOR_ROWS * WIDE,
        [pltpu.VMEM((VECTOR_ROWS, WIDE), FLOAT)],
    )
    parts_c = split(
        where, [keep_qkv, keep_small], [core_swap(send_qkv), swapped_small], shards, (vectors, core_swap(vectors))
    )
    exchanged_c = exchange(parts_c)
    input_grad = input_pass(after(heads, parts_c[0]), residual1, qkv)
    near_ab[0] = after(near_ab[0], input_grad)
    (piece_ab,) = total(where, near_ab)
    piece_ab, *exchanged_c = lax.optimization_barrier((piece_ab, *exchanged_c))
    ready = merge(where, [exchanged_c], shards, True)
    near_c = spread(ready)
    around_ab = around(after(piece_ab, ready[0]))
    arrived = lax.optimization_barrier((*near_c, *around_ab))
    near_c, around_ab = arrived[: len(near_c)], arrived[len(near_c) :]
    pieces_ab = []
    for place_in_plane, value in enumerate(around_ab):
        if place_in_plane > 1:
            value = after(value, pieces_ab[2 * place_in_plane - 3])
        pieces_ab += [value, core_swap(value)]
    piece_c, vectors = total(where, near_c, True)
    around_c = around(piece_c)
    full = lambda shard: struct(shard.shape, FLOAT)
    ab_mats = up_mats + down_mats[:1]
    grad_out, grad_up, grad_down = finish(
        where, pieces_ab, ab_mats, [full(s) for s in (out_weight, up_weight, down_weight)]
    )
    around_c[-1] = after(around_c[-1], grad_out)
    pieces_c = both_cores(around_c)
    *g_table, g_up_b, g_student_b, g_dense_b, g_class_b = vector_out(where, vectors, shards, inner, classes)
    grad_qkv, g_student, g_pool, g_dense, g_class = finish(
        where, pieces_c, qkv_mats + (SMALL,),
        [full(s) for s in (qkv_weight, student_weight, pool_weight, dense_weight, class_weight)], student_rows,
    )
    return (
        hidden.reshape(count, length, wide), logits, input_grad.reshape(count, length, wide),
        grad_qkv, g_table[0], g_table[1], grad_out, g_table[2], g_table[3], g_table[4], grad_up, g_up_b, grad_down,
        g_table[5], g_table[6], g_table[7], g_student, g_student_b, g_pool, g_dense, g_dense_b, g_class, g_class_b,
    )


def solution(mesh):
    placed = (
        P(("shard", "replica"), None, None),
        P(("shard", "replica"), None, None),
        P(("shard", "replica"), None),
        P(("shard", "replica")),
        P("shard", None),
        P("shard"),
        P("shard"),
        P("shard", None),
        P("shard"),
        P("shard"),
        P("shard"),
        P("shard", None),
        P("shard"),
        P("shard", None),
        P("shard"),
        P("shard"),
        P("shard"),
        P("shard", None),
        P("shard"),
        P("shard", None),
        P("shard", None),
        P("shard"),
        P("shard", None),
        P(),
    )
    return jax.shard_map(
        body,
        mesh=mesh,
        in_specs=placed,
        out_specs=(
            P(("shard", "replica"), None, None),
            P(("shard", "replica"), None),
            P(("shard", "replica"), None, None),
            P("shard", None),
            P("shard"),
            P("shard"),
            P("shard", None),
            P("shard"),
            P("shard"),
            P("shard"),
            P("shard", None),
            P("shard"),
            P("shard", None),
            P("shard"),
            P("shard"),
            P("shard"),
            P("shard", None),
            P("shard"),
            P("shard", None),
            P("shard", None),
            P("shard"),
            P("shard", None),
            P(),
        ),
        check_vma=False,
    )
```
